32 devices in a mesh: tok: 16 (over z, y, x), row: 2 (over core).
Axes of the slice: x: 2, y: 2, z: 4, core: 2. Of those that a mesh axis runs over, the one named last changes fastest.
Arguments:
- tokens: bfloat16 [8, 4096, 768], P('row', 'tok'), may hold values from -6 to 6
- out_grad: bfloat16 [8, 4096, 768], P('row', 'tok'), may hold values from -6 to 6
- doc_lengths: int32 [8, 4, 8], P('row'), may hold values from 1 to 512, 1024 in all within a row
- first_gain: float32 [768], replicated, may hold values from 0.1 to 1.9
- first_bias: float32 [768], replicated, may hold values from -3 to 3
- qkv_weight: bfloat16 [768, 2304], P('tok', 'row'), may hold values from -0.21875 to 0.21875
- query_bias: float32 [768], replicated, may hold values from -3 to 3
- value_bias: float32 [768], replicated, may hold values from -3 to 3
- proj_weight: bfloat16 [768, 768], P('tok', 'row'), may hold values from -3.5 to 3.5
- proj_bias: float32 [768], replicated, may hold values from -4 to 4
- second_gain: float32 [768], replicated, may hold values from 0.1 to 1.9
- second_bias: float32 [768], replicated, may hold values from -3 to 3
- up_weight: bfloat16 [768, 3072], P('tok', 'row'), may hold values from -0.21875 to 0.21875
- up_bias: float32 [3072], replicated, may hold values from -3 to 3
- down_weight: bfloat16 [3072, 768], P('tok', 'row'), may hold values from -0.875 to 0.875
- down_bias: float32 [768], replicated, may hold values from -4 to 4
Outputs:
- output: bfloat16 [8, 4096, 768], P('row', 'tok')
- tokens_grad: bfloat16 [8, 4096, 768], P('row', 'tok')
- qkv_weight_grad: float32 [768, 2304], P('tok', 'row')
- proj_weight_grad: float32 [768, 768], P('tok', 'row')
- up_weight_grad: float32 [768, 3072], P('tok', 'row')
- down_weight_grad: float32 [3072, 768], P('tok', 'row')
- first_gain_grad: float32 [768], replicated
- first_bias_grad: float32 [768], replicated
- query_bias_grad: float32 [768], replicated
- value_bias_grad: float32 [768], replicated
- proj_bias_grad: float32 [768], replicated
- second_gain_grad: float32 [768], replicated
- second_bias_grad: float32 [768], replicated
- up_bias_grad: float32 [3072], replicated
- down_bias_grad: float32 [768], replicated
The draws below stay inside these ranges and needn't reach their ends.
Inputs may be any that keep to these rules, and one draw needn't show every extreme that they name: `doc_lengths`: each packed row holds 8 documents whose lengths, in order, sum to 1024; some document has exactly 512 tokens.
All inputs are finite; a program needn't handle non-finite values.
Results may differ from the reference program's by a relative error of at most 0.018.
Values may be sent and summed in bfloat16 or wider, within the bound.
No kernel may reach another device: no remote copies, remote signals or barrier semaphores. Data moves between devices by JAX's collectives and lax.ppermute only.
A program may use at most 192 MiB of HBM per device.

```python
import math
import jax
import jax.numpy as jnp
import numpy as np
from jax import lax

D = 768
H = 12
HD = 64
FF = 3072
SEQ = 1024
DOCS = 8
DEPTH = 48
GROUPS = 4
ROWSX = 8
LINE = 4096


def block_scale(stream_key, shape, cuts, smallest, top_value):
    gain = 1.0
    for position, parts in cuts:
        heights = jax.random.uniform(jax.random.fold_in(jax.random.fold_in(stream_key, 6), position), (parts,), jnp.float32, smallest / len(cuts), top_value / len(cuts))
        gain = gain * jnp.repeat(jnp.exp(heights), shape[position] // parts).reshape((-1,) + (1,) * (len(shape) - 1 - position))
    return gain


def length_profile(count, total, reach, slope):
    loads = [(1 << 20) // math.isqrt(grade ** slope) + 1 for grade in range(2, count + 1)]
    spare, holding = total - reach - (count - 1), [1] * (count - 1)
    while spare > 0:
        movable = [i for i in range(count - 1) if holding[i] < reach]
        whole, remaining = sum([loads[i] for i in movable]), spare
        for i in movable:
            extra = min(reach - holding[i], max(1, remaining * loads[i] // whole), spare)
            holding[i] = holding[i] + extra
            spare = spare - extra
    return np.array([reach] + holding)


def ragged_sizes(key, amount, total, most, slope):
    if amount == 2:
        one = jax.random.randint(key, (), max(1, total - most), min(most, total - 1) + 1)
        return jnp.stack([one, total - one])
    lengths = jnp.asarray(length_profile(amount, total, most, slope), jnp.int32)
    pairs = (amount - 1) // 2
    source_of, taker = lengths[1:1 + 2 * pairs:2], lengths[2:2 + 2 * pairs:2]
    room = jnp.minimum(source_of - 1, most - taker)
    moved = jax.random.randint(jax.random.fold_in(key, 1), (pairs,), 0, 1 << 20) % (room + 1)
    lengths = lengths.at[1:1 + 2 * pairs:2].set(source_of - moved).at[2:2 + 2 * pairs:2].set(taker + moved)
    return lengths[jax.random.permutation(jax.random.fold_in(key, 2), amount)]


def bell_draw(rng, shape, spread, bound, cuts=(), held_as=jnp.bfloat16):
    values = jax.random.normal(rng, shape, jnp.float32) * spread
    if len(cuts) > 0:
        values = block_scale(rng, shape, cuts, -0.22, 0.18) * values
    return jnp.clip(values, min=-bound, max=bound).astype(held_as)


def setup_inputs(seed: int = 0) -> dict:
    splits = jax.random.split(jax.random.key(seed), 17)
    tokens = bell_draw(splits[0], (ROWSX, LINE, D), 1.0, 6.0, ((0, 2), (1, 16)))
    out_grad = bell_draw(splits[1], (ROWSX, LINE, D), 1.0, 6.0, ((0, 2), (1, 16)))
    doc_lengths = jax.vmap(lambda own: ragged_sizes(own, DOCS, SEQ, SEQ // 2, 2))(jax.random.split(splits[2], ROWSX * GROUPS)).reshape((ROWSX, GROUPS, DOCS)).astype(jnp.int32)
    first_gain = jnp.clip(1.0 + 0.18 * jax.random.normal(splits[3], (D,), jnp.float32), 0.1, 1.9)
    first_bias = bell_draw(splits[4], (D,), 0.5, 3.0, (), jnp.float32)
    qkv_weight = bell_draw(splits[5], (D, 3 * D), D ** -0.5, 0.21875, ((0, 16), (1, 2)))
    query_bias = bell_draw(splits[6], (D,), 0.5, 3.0, (), jnp.float32)
    value_bias = bell_draw(splits[7], (D,), 0.5, 3.0, (), jnp.float32)
    proj_weight = bell_draw(splits[8], (D, D), (max(D // 256, 1)) ** -0.5, 3.5, ((0, 16), (1, 2)))
    proj_bias = bell_draw(splits[9], (D,), 1.0, 4.0, (), jnp.float32)
    second_gain = jnp.clip(1.0 + 0.18 * jax.random.normal(splits[10], (D,), jnp.float32), 0.1, 1.9)
    second_bias = bell_draw(splits[11], (D,), 0.5, 3.0, (), jnp.float32)
    up_weight = bell_draw(splits[12], (D, FF), D ** -0.5, 0.21875, ((0, 16), (1, 2)))
    up_bias = bell_draw(splits[13], (FF,), 0.5, 3.0, (), jnp.float32)
    down_weight = bell_draw(splits[14], (FF, D), (FF // 64) ** -0.5, 0.875, ((0, 16), (1, 2)))
    down_bias = bell_draw(splits[15], (D,), 1.0, 4.0, (), jnp.float32)
    return {"tokens": tokens, "out_grad": out_grad, "doc_lengths": doc_lengths, "first_gain": first_gain, "first_bias": first_bias, "qkv_weight": qkv_weight, "query_bias": query_bias, "value_bias": value_bias, "proj_weight": proj_weight, "proj_bias": proj_bias, "second_gain": second_gain, "second_bias": second_bias, "up_weight": up_weight, "up_bias": up_bias, "down_weight": down_weight, "down_bias": down_bias}


EPSILON = 1e-05
MASKED = -1000000000.0
TANH_ROOT = 0.7978845608028654
TANH_CUBIC = 0.044715
HIGHEST_PREC = lax.Precision.HIGHEST

@jax.custom_vjp
def low(v):
    return lax.optimization_barrier(v.astype(jnp.bfloat16)).astype(jnp.float32)

@jax.custom_vjp
def low_back(v):
    return v

def low_keep(v):
    return (low(v), None)

def low_pass(kept, grad):
    return (grad,)

def back_keep(v):
    return (v, None)

def back_low(kept, grad):
    return (low(grad),)
low.defvjp(low_keep, low_pass)
low_back.defvjp(back_keep, back_low)

def matmul_high(left, right):
    return jnp.dot(left, right, precision=HIGHEST_PREC, preferred_element_type=jnp.float32)

def layer_norm(values, gain_vec, bias_vec):
    centre = values - lax.optimization_barrier(jnp.mean(values, axis=-1, keepdims=True))
    return centre * lax.rsqrt(lax.optimization_barrier(jnp.mean(centre * centre, axis=-1, keepdims=True)) + EPSILON) * gain_vec + bias_vec

def gelu_tanh(pre_act):
    return 0.5 * pre_act * (1.0 + jnp.tanh(TANH_ROOT * (pre_act + TANH_CUBIC * pre_act * pre_act * pre_act)))

def attend_row(pieces):
    queries, keys_in, values_in, segment_row = pieces
    positions = jnp.arange(SEQ, dtype=jnp.int32)
    scores = low_back(jnp.einsum('qhd,khd->hqk', queries, keys_in, precision=HIGHEST_PREC) * (1.0 / math.sqrt(HD)))
    allowed = (segment_row[:, None] == segment_row[None, :]) & (positions[None, :] <= positions[:, None])
    scores = jnp.where(allowed[None], scores, MASKED)
    row_max = lax.optimization_barrier(jnp.max(scores, axis=-1, keepdims=True))
    shifted = jnp.exp(scores - row_max)
    weights = low(shifted / lax.optimization_barrier(jnp.sum(shifted, axis=-1, keepdims=True)))
    return low_back(low(jnp.einsum('hqk,khd->qhd', weights, values_in, precision=HIGHEST_PREC)))

def reference(tokens, out_grad, doc_lengths, first_gain, first_bias, qkv_weight, query_bias, value_bias, proj_weight, proj_bias, second_gain, second_bias, up_weight, up_bias, down_weight, down_bias):
    rows_all = ROWSX * GROUPS
    branch_scale = 1.0 / math.sqrt(DEPTH)
    inputs = tokens.astype(jnp.float32).reshape(rows_all, SEQ, D)
    cotangent = out_grad.astype(jnp.float32).reshape(rows_all, SEQ, D)
    lengths_flat = doc_lengths.reshape(rows_all, DOCS)
    doc_ends = jnp.cumsum(lengths_flat, axis=-1)
    positions = jnp.arange(SEQ, dtype=jnp.int32)
    segment = lax.optimization_barrier(jnp.sum((doc_ends[:, None, :] <= positions[None, :, None]).astype(jnp.int32), axis=-1))

    def forward(values, gain_one, bias_one, weight_qkv, bias_query, bias_value, weight_proj, bias_proj, gain_two, bias_two, weight_up, bias_up, weight_down, bias_down):
        act_one = low(layer_norm(values, gain_one, bias_one))
        qkv_bias = jnp.concatenate([bias_query, jnp.zeros_like(bias_query), bias_value])
        qkv = low_back(low(matmul_high(act_one, weight_qkv) + qkv_bias))
        shaped = qkv.reshape(rows_all, SEQ, 3, H, HD)
        attended = lax.map(jax.checkpoint(attend_row), (shaped[:, :, 0], shaped[:, :, 1], shaped[:, :, 2], segment))
        mixed = low_back(matmul_high(attended.reshape(rows_all, SEQ, D), weight_proj) + bias_proj)
        middle = values + branch_scale * mixed
        act_two = low(layer_norm(middle, gain_two, bias_two))
        pre_act = low_back(matmul_high(act_two, weight_up) + bias_up)
        hidden = low(gelu_tanh(pre_act))
        branch_out = low_back(matmul_high(hidden, weight_down) + bias_down)
        return middle + branch_scale * branch_out
    result, pullback = jax.vjp(forward, inputs, first_gain.astype(jnp.float32), first_bias.astype(jnp.float32), qkv_weight.astype(jnp.float32), query_bias.astype(jnp.float32), value_bias.astype(jnp.float32), proj_weight.astype(jnp.float32), proj_bias.astype(jnp.float32), second_gain.astype(jnp.float32), second_bias.astype(jnp.float32), up_weight.astype(jnp.float32), up_bias.astype(jnp.float32), down_weight.astype(jnp.float32), down_bias.astype(jnp.float32))
    grads = pullback(cotangent)
    return (result.reshape(ROWSX, LINE, D).astype(jnp.bfloat16), grads[0].reshape(ROWSX, LINE, D).astype(jnp.bfloat16), grads[3], grads[6], grads[10], grads[12], grads[1], grads[2], grads[4], grads[5], grads[7], grads[8], grads[9], grads[11], grads[13])
```

```python
import math

import jax
import jax.numpy as jnp
from jax import lax
from jax.experimental import pallas as pl
from jax.experimental.pallas import tpu as pltpu
from jax.sharding import PartitionSpec as P

D = 768
H = 12
HD = 64
FF = 3072
DEPTH = 48
DOCS = 8
BLK = 256
QUAD = 4

EPSILON = 1e-05
TANH_ROOT = 0.7978845608028654
TANH_CUBIC = 0.044715
BETA = 1.0 / math.sqrt(DEPTH)
SCALE = 1.0 / math.sqrt(HD)
F32 = jnp.float32
BF16 = jnp.bfloat16
VMEM_LIMIT = 56 * 2**20

NT = (((1,), (1,)), ((), ()))
NN = (((1,), (0,)), ((), ()))
TN = (((0,), (0,)), ((), ()))


def mm(a, b, dims=NN):
    return lax.dot_general(a, b, dims, preferred_element_type=F32)


def params():
    return pltpu.CompilerParams(vmem_limit_bytes=VMEM_LIMIT)


def cost(flops, nbytes, trans=0):
    return pl.CostEstimate(flops=int(flops), bytes_accessed=int(nbytes), transcendentals=int(trans))


def norm_parts(x):
    centre = x - jnp.mean(x, axis=-1, keepdims=True)
    inverse = lax.rsqrt(jnp.mean(centre * centre, axis=-1, keepdims=True) + EPSILON)
    return centre * inverse, inverse


def norm_back(grad, normed, inverse, gain):
    spread = grad * gain
    return inverse * (
        spread
        - jnp.mean(spread, axis=-1, keepdims=True)
        - normed * jnp.mean(spread * normed, axis=-1, keepdims=True)
    )


def halves_copies(w_hbm, w_vmem, sem):
    width = w_hbm.shape[2]
    return [
        pltpu.make_async_copy(w_hbm.at[h], w_vmem.at[:, pl.ds(h * width, width)], sem.at[h])
        for h in range(2)
    ]


def qkv_kernel(x_ref, g_ref, b_ref, qb_ref, w_hbm, act_ref, qkv_ref, w_vmem, sem):
    first = pl.program_id(0) == 0

    @pl.when(first)
    def _():
        for c in halves_copies(w_hbm, w_vmem, sem):
            c.start()

    normed, _ = norm_parts(x_ref[...].astype(F32))
    act = (normed * g_ref[...] + b_ref[...]).astype(BF16)
    act_ref[...] = act

    @pl.when(first)
    def _():
        for c in halves_copies(w_hbm, w_vmem, sem):
            c.wait()

    qkv_ref[...] = (mm(act, w_vmem[...]) + qb_ref[...]).astype(BF16)


def norm_qkv(x, gain, bias, qkv_bias, w):
    n = x.shape[0]
    tile = BLK
    const = lambda i: (0, 0)
    return pl.pallas_call(
        qkv_kernel,
        grid=(n // tile,),
        in_specs=[
            pl.BlockSpec((tile, D), lambda i: (i, 0)),
            pl.BlockSpec((1, D), const),
            pl.BlockSpec((1, D), const),
            pl.BlockSpec((1, 3 * D), const),
            pl.BlockSpec(memory_space=pl.ANY),
        ],
        out_specs=[
            pl.BlockSpec((tile, D), lambda i: (i, 0)),
            pl.BlockSpec((tile, 3 * D), lambda i: (i, 0)),
        ],
        out_shape=[
            jax.ShapeDtypeStruct((n, D), BF16),
            jax.ShapeDtypeStruct((n, 3 * D), BF16),
        ],
        scratch_shapes=[pltpu.VMEM((D, 3 * D), BF16), pltpu.SemaphoreType.DMA((2,))],
        compiler_params=params(),
        cost_estimate=cost(2 * n * D * 3 * D, 2 * (n * 5 * D + 3 * D * D)),
        name="norm_qkv",
    )(x, gain, bias, qkv_bias, w)


def first_of_doc(lens_ref, positions):
    start = jnp.zeros_like(positions)
    end = 0
    for d in range(DOCS):
        end = end + lens_ref[0, d]
        start = jnp.where(positions >= end, end, start)
    return start


def lane_half(h):
    lane = lax.broadcasted_iota(jnp.int32, (1, 128), 1)
    return (lane >= h * HD) & (lane < (h + 1) * HD)


def attn_kernel(lens_ref, q_ref, k_ref, v_ref, o_ref, l_ref, start_ref):
    pair = pl.program_id(0)
    n = q_ref.shape[0]
    nb = n // BLK

    @pl.when(pair == 0)
    def _():
        start_ref[...] = first_of_doc(lens_ref, lax.broadcasted_iota(jnp.int32, (n, 1), 0))
        l_ref[...] = jnp.zeros_like(l_ref)

    lane = lax.broadcasted_iota(jnp.int32, (1, 128), 1)
    for i in range(nb):
        lo = max(0, i - 2)
        rows = pl.ds(i * BLK, BLK)
        keys = pl.ds(lo * BLK, (i + 1 - lo) * BLK)
        width = (i + 1 - lo) * BLK
        q = q_ref[rows, :] * jnp.asarray(SCALE, BF16)
        k = k_ref[keys, :]
        v = v_ref[keys, :]
        kpos = lax.broadcasted_iota(jnp.int32, (1, width), 1) + lo * BLK
        qpos = lax.broadcasted_iota(jnp.int32, (BLK, 1), 0) + i * BLK
        allowed = (kpos >= start_ref[rows, :]) & (kpos <= qpos)
        outs = []
        stats = l_ref[rows, :]
        for h in range(2):
            qh = jnp.where(lane_half(h), q, jnp.zeros_like(q))
            s = jnp.where(allowed, mm(qh, k, NT), -1e9)
            m = jnp.max(s, axis=-1, keepdims=True)
            p = jnp.exp(s - m)
            total = jnp.sum(p, axis=-1, keepdims=True)
            outs.append(mm(p.astype(BF16), v) / total)
            stats = jnp.where(lane == 2 * pair + h, m + jnp.log(total), stats)
        l_ref[rows, :] = stats
        o_ref[rows, :] = jnp.where(lane_half(0), outs[0], outs[1]).astype(BF16)


def attention(lens, qkv):
    n = qkv.shape[0]
    pairs = H // 2
    spec = lambda w: pl.BlockSpec((n, 128), lambda p: (0, w * pairs + p))
    return pl.pallas_call(
        attn_kernel,
        grid=(pairs,),
        in_specs=[pl.BlockSpec(memory_space=pltpu.SMEM), spec(0), spec(1), spec(2)],
        out_specs=[
            pl.BlockSpec((n, 128), lambda p: (0, p)),
            pl.BlockSpec((n, 128), lambda p: (0, 0)),
        ],
        out_shape=[jax.ShapeDtypeStruct((n, D), BF16), jax.ShapeDtypeStruct((n, 128), F32)],
        scratch_shapes=[pltpu.VMEM((n, 1), jnp.int32)],
        compiler_params=params(),
        cost_estimate=cost(2 * 2 * H * n * n * HD * 0.6, 2 * n * 4 * D, H * n * n * 0.6),
        name="attention",
    )(lens, qkv, qkv, qkv)


def attn_back_kernel(
    lens_ref, q_ref, k_ref, v_ref, o_ref, do_ref, l_ref, dq_ref, dk_ref, dv_ref,
    start_ref, lt_ref, dk_acc, dv_acc,
):
    pair = pl.program_id(0)
    n = q_ref.shape[0]
    nb = n // BLK

    @pl.when(pair == 0)
    def _():
        start_ref[...] = first_of_doc(lens_ref, lax.broadcasted_iota(jnp.int32, (8, n), 1))
        lt_ref[...] = l_ref[...].T

    prod = (o_ref[...].astype(F32) * do_ref[...].astype(F32)).T
    for h in range(2):
        half = lane_half(h)
        delta = jnp.sum(prod[h * HD : (h + 1) * HD, :], axis=0, keepdims=True)
        logs = lt_ref[pl.ds(2 * pair + h, 1), :]
        for i in range(nb):
            rows = pl.ds(i * BLK, BLK)
            q = q_ref[rows, :] * jnp.asarray(SCALE, BF16)
            q = jnp.where(half, q, jnp.zeros_like(q))
            do = do_ref[rows, :]
            do = jnp.where(half, do, jnp.zeros_like(do))
            logs_i = logs[:, i * BLK : (i + 1) * BLK]
            delta_i = delta[:, i * BLK : (i + 1) * BLK]
            start_i = start_ref[0:1, i * BLK : (i + 1) * BLK]
            qpos = lax.broadcasted_iota(jnp.int32, (1, BLK), 1) + i * BLK
            dq = jnp.zeros((BLK, 128), F32)
            for j in range(max(0, i - 2), i + 1):
                keys = pl.ds(j * BLK, BLK)
                k = k_ref[keys, :]
                v = v_ref[keys, :]
                kpos = lax.broadcasted_iota(jnp.int32, (BLK, 1), 0) + j * BLK
                allowed = kpos >= start_i
                if i == j:
                    allowed = allowed & (kpos <= qpos)
                p = jnp.where(allowed, jnp.exp(mm(k, q, NT) - logs_i), 0.0)
                dp = mm(v, do, NT)
                ds = (p * (dp - delta_i)).astype(BF16)
                dv = mm(p.astype(BF16), do)
                dk = mm(ds, q)
                if h == 0 and i == j:
                    dv_acc[keys, :] = dv
                    dk_acc[keys, :] = dk
                else:
                    dv_acc[keys, :] += dv
                    dk_acc[keys, :] += dk
                kh = jnp.where(half, k, jnp.zeros_like(k))
                dq = dq + mm(ds, kh, TN)
            dq = (dq * SCALE).astype(BF16)
            if h == 0:
                dq_ref[rows, :] = dq
            else:
                dq_ref[rows, :] = jnp.where(half, dq, dq_ref[rows, :])
    dk_ref[...] = dk_acc[...].astype(BF16)
    dv_ref[...] = dv_acc[...].astype(BF16)


def attention_back(lens, qkv, attended, dout, stats):
    n = qkv.shape[0]
    pairs = H // 2
    spec = lambda w: pl.BlockSpec((n, 128), lambda p: (0, w * pairs + p))
    one = pl.BlockSpec((n, 128), lambda p: (0, p))
    return pl.pallas_call(
        attn_back_kernel,
        grid=(pairs,),
        in_specs=[
            pl.BlockSpec(memory_space=pltpu.SMEM), spec(0), spec(1), spec(2), one, one,
            pl.BlockSpec((n, 128), lambda p: (0, 0)),
        ],
        out_specs=[one, one, one],
        out_shape=[jax.ShapeDtypeStruct((n, D), BF16)] * 3,
        scratch_shapes=[
            pltpu.VMEM((8, n), jnp.int32),
            pltpu.VMEM((128, n), F32),
            pltpu.VMEM((n, 128), F32),
            pltpu.VMEM((n, 128), F32),
        ],
        compiler_params=params(),
        cost_estimate=cost(5 * 2 * H * n * n * HD * 0.6, 2 * n * 8 * D, H * n * n * 0.6),
        name="attention_back",
    )(lens, qkv, qkv, qkv, attended, dout, stats)


def mlp_kernel(
    x_ref, c_ref, att_ref, pb_ref, g_ref, b_ref, ub_ref, db_ref, wp_hbm, wu_hbm, wd_hbm,
    out_ref, hid_ref, du_ref, act_ref, dz_ref, dm_ref, dy_ref, do_ref, vec_ref, uvec_ref,
    wp, wu, wd, sem,
):
    step = pl.program_id(0)
    copies = [
        halves_copies(wp_hbm, wp, sem.at[0]),
        halves_copies(wu_hbm, wu, sem.at[1]),
        halves_copies(wd_hbm, wd, sem.at[2]),
    ]

    @pl.when(step == 0)
    def _():
        for pair in copies:
            for c in pair:
                c.start()
        vec_ref[...] = jnp.zeros_like(vec_ref)
        uvec_ref[...] = jnp.zeros_like(uvec_ref)
        for c in copies[0]:
            c.wait()

    middle = x_ref[...].astype(F32) + BETA * (mm(att_ref[...], wp[...]) + pb_ref[...])
    normed, inverse = norm_parts(middle)
    act = (normed * g_ref[...] + b_ref[...]).astype(BF16)
    act_ref[...] = act
    grad_out = c_ref[...].astype(F32)
    dz = (BETA * grad_out).astype(BF16)
    dz_ref[...] = dz

    @pl.when(step == 0)
    def _():
        for c in copies[1] + copies[2]:
            c.wait()

    chunk = 768
    branch = jnp.zeros(middle.shape, F32)
    da = jnp.zeros(middle.shape, F32)
    for f in range(FF // chunk):
        cols = pl.ds(f * chunk, chunk)
        u = mm(act, wu[:, cols]) + ub_ref[:, cols]
        u2 = u * u
        half_t = 0.5 * jnp.tanh(u * (TANH_ROOT + (TANH_ROOT * TANH_CUBIC) * u2))
        gate = 0.5 + half_t
        hidden = (u * gate).astype(BF16)
        hid_ref[:, cols] = hidden
        branch = branch + mm(hidden, wd[cols, :])
        slope = gate + u * (0.5 - 2.0 * half_t * half_t) * (
            TANH_ROOT + (3.0 * TANH_ROOT * TANH_CUBIC) * u2
        )
        du = (mm(dz, wd[cols, :], NT) * slope).astype(BF16)
        du_ref[:, cols] = du
        uvec_ref[0:1, cols] += jnp.sum(du.astype(F32), axis=0, keepdims=True)
        da = da + mm(du, wu[:, cols], NT)
    out_ref[...] = (middle + BETA * (branch + db_ref[...])).astype(BF16)
    dm = grad_out + norm_back(da, normed, inverse, g_ref[...])
    dm_ref[...] = dm
    dy = (BETA * dm).astype(BF16)
    dy_ref[...] = dy
    do_ref[...] = mm(dy, wp[...], NT).astype(BF16)
    vec_ref[0:1, :] += jnp.sum(da * normed, axis=0, keepdims=True)
    vec_ref[1:2, :] += jnp.sum(da, axis=0, keepdims=True)
    vec_ref[2:3, :] += jnp.sum(dy.astype(F32), axis=0, keepdims=True)
    vec_ref[3:4, :] += jnp.sum(dz.astype(F32), axis=0, keepdims=True)


def mlp(x, c, att, pb, gain, bias, ub, db, wp, wu, wd):
    n = x.shape[0]
    tile = BLK
    const = lambda i: (0, 0)
    row = lambda w: pl.BlockSpec((tile, w), lambda i: (i, 0))
    vec = lambda w: pl.BlockSpec((1, w), const)
    hbm = pl.BlockSpec(memory_space=pl.ANY)
    sds = jax.ShapeDtypeStruct
    return pl.pallas_call(
        mlp_kernel,
        grid=(n // tile,),
        in_specs=[row(D), row(D), row(D), vec(D), vec(D), vec(D), vec(FF), vec(D), hbm, hbm, hbm],
        out_specs=[
            row(D), row(FF), row(FF), row(D), row(D), row(D), row(D), row(D),
            pl.BlockSpec((8, D), const), pl.BlockSpec((8, FF), const),
        ],
        out_shape=[
            sds((n, D), BF16), sds((n, FF), BF16), sds((n, FF), BF16), sds((n, D), BF16),
            sds((n, D), BF16), sds((n, D), F32), sds((n, D), BF16), sds((n, D), BF16),
            sds((8, D), F32), sds((8, FF), F32),
        ],
        scratch_shapes=[
            pltpu.VMEM((D, D), BF16),
            pltpu.VMEM((D, FF), BF16),
            pltpu.VMEM((FF, D), BF16),
            pltpu.SemaphoreType.DMA((3, 2)),
        ],
        compiler_params=params(),
        cost_estimate=cost(2 * n * (4 * D * FF + 2 * D * D), 2 * n * (10 * D + 2 * FF), n * FF),
        name="mlp",
    )(x, c, att, pb, gain, bias, ub, db, wp, wu, wd)


def outer_kernel(a_ref, b_ref, o_ref):
    r = mm(a_ref[...], b_ref[...], TN)
    if o_ref.shape[0] == 1:
        o_ref[0] = r.astype(BF16)
    else:
        width = o_ref.shape[2]
        o_ref[0] = r[:, :width].astype(BF16)
        o_ref[1] = r[:, width:].astype(BF16)


def outer_rows(a, b):
    n, left = a.shape
    right = b.shape[1]
    tile = 768
    return pl.pallas_call(
        outer_kernel,
        grid=(left // tile,),
        in_specs=[
            pl.BlockSpec((n, tile), lambda i: (0, i)),
            pl.BlockSpec((n, right), lambda i: (0, 0)),
        ],
        out_specs=pl.BlockSpec((2, tile, right // 2), lambda i: (0, i, 0)),
        out_shape=jax.ShapeDtypeStruct((2, left, right // 2), BF16),
        compiler_params=params(),
        cost_estimate=cost(2 * n * left * right, 2 * (n * (left + right) + left * right)),
        name="outer_rows",
    )(a, b)


def outer_cols(a, b, tile):
    n, left = a.shape
    right = b.shape[1]
    per = right // 2 // tile
    return pl.pallas_call(
        outer_kernel,
        grid=(right // tile,),
        in_specs=[
            pl.BlockSpec((n, left), lambda i: (0, 0)),
            pl.BlockSpec((n, tile), lambda i: (0, i)),
        ],
        out_specs=pl.BlockSpec((1, left, tile), lambda i: (i // per, 0, i % per)),
        out_shape=jax.ShapeDtypeStruct((2, left, right // 2), BF16),
        compiler_params=params(),
        cost_estimate=cost(2 * n * left * right, 2 * (n * (left + right) + left * right)),
        name="outer_cols",
    )(a, b)


def qkv_outer_kernel(a_ref, q_ref, k_ref, v_ref, o_ref, s_ref):
    for w, ref in enumerate((q_ref, k_ref, v_ref)):
        g = ref[...]
        r = mm(a_ref[...], g, TN).astype(BF16)
        if w == 0:
            o_ref[0, :, 0:D] = r
        elif w == 1:
            o_ref[0, :, D:] = r[:, : D // 2]
            o_ref[1, :, 0 : D // 2] = r[:, D // 2 :]
        else:
            o_ref[1, :, D // 2 :] = r
        s_ref[w : w + 1, :] = jnp.sum(g.astype(F32), axis=0, keepdims=True)


def qkv_outer(act, dq, dk, dv):
    n = act.shape[0]
    return pl.pallas_call(
        qkv_outer_kernel,
        out_shape=[
            jax.ShapeDtypeStruct((2, D, 3 * D // 2), BF16),
            jax.ShapeDtypeStruct((8, D), F32),
        ],
        compiler_params=params(),
        cost_estimate=cost(2 * n * D * 3 * D, 2 * (n * 4 * D + 3 * D * D)),
        name="qkv_outer",
    )(act, dq, dk, dv)


def input_grad_kernel(x_ref, dm_ref, g_ref, dq_ref, dk_ref, dv_ref, w_hbm, o_ref, vec_ref, w, sem):
    first = pl.program_id(0) == 0

    @pl.when(first)
    def _():
        for c in halves_copies(w_hbm, w, sem):
            c.start()
        vec_ref[...] = jnp.zeros_like(vec_ref)
        for c in halves_copies(w_hbm, w, sem):
            c.wait()

    da = mm(dq_ref[...], w[:, 0:D], NT)
    da = da + mm(dk_ref[...], w[:, D : 2 * D], NT)
    da = da + mm(dv_ref[...], w[:, 2 * D : 3 * D], NT)
    normed, inverse = norm_parts(x_ref[...].astype(F32))
    o_ref[...] = (dm_ref[...] + norm_back(da, normed, inverse, g_ref[...])).astype(BF16)
    vec_ref[0:1, :] += jnp.sum(da * normed, axis=0, keepdims=True)
    vec_ref[1:2, :] += jnp.sum(da, axis=0, keepdims=True)


def input_grad(x, dm, gain, dq, dk, dv, w):
    n = x.shape[0]
    tile = BLK
    const = lambda i: (0, 0)
    row = pl.BlockSpec((tile, D), lambda i: (i, 0))
    return pl.pallas_call(
        input_grad_kernel,
        grid=(n // tile,),
        in_specs=[row, row, pl.BlockSpec((1, D), const), row, row, row, pl.BlockSpec(memory_space=pl.ANY)],
        out_specs=[row, pl.BlockSpec((8, D), const)],
        out_shape=[jax.ShapeDtypeStruct((n, D), BF16), jax.ShapeDtypeStruct((8, D), F32)],
        scratch_shapes=[pltpu.VMEM((D, 3 * D), BF16), pltpu.SemaphoreType.DMA((2,))],
        compiler_params=params(),
        cost_estimate=cost(2 * n * D * 3 * D, 2 * (n * 7 * D + 3 * D * D)),
        name="input_grad",
    )(x, dm, gain, dq, dk, dv, w)


def quad_swap(pieces):
    count = lax.axis_size("tok")
    groups = [list(range(g, g + QUAD)) for g in range(0, count, QUAD)]
    return lax.all_to_all(pieces, "tok", 0, 0, axis_index_groups=groups, tiled=True)


def gather(shard):
    rows, cols = shard.shape
    over_row = lax.axis_size("row")
    whole = lax.all_gather(shard, ("row", "tok"), axis=0, tiled=True)
    height = rows * lax.axis_size("tok")
    whole = whole.reshape(over_row, height, cols)
    if over_row == 2:
        return whole
    return (
        whole.reshape(2, over_row // 2, height, cols)
        .transpose(0, 2, 1, 3)
        .reshape(2, height, over_row // 2 * cols)
    )


def scatter(halves):
    over_row = lax.axis_size("row")
    _, height, width = halves.shape
    if over_row != 2:
        cols = 2 * width // over_row
        halves = halves.reshape(2, height, over_row // 2, cols).transpose(0, 2, 1, 3)
        width = cols
    flat = halves.reshape(over_row * height, width)
    return lax.psum_scatter(flat, ("row", "tok"), scatter_dimension=0, tiled=True).astype(F32)


def per_device(
    tokens,
    out_grad,
    doc_lengths,
    first_gain,
    first_bias,
    qkv_weight,
    query_bias,
    value_bias,
    proj_weight,
    proj_bias,
    second_gain,
    second_bias,
    up_weight,
    up_bias,
    down_weight,
    down_bias,
):
    row_count, piece_len, width = tokens.shape
    n = row_count * piece_len
    tok_index = lax.axis_index("tok")
    lens = lax.dynamic_slice(
        doc_lengths,
        (tok_index % QUAD, tok_index // QUAD, 0),
        (1, 1, doc_lengths.shape[2]),
    )[0]

    x = quad_swap(tokens).reshape(n, width)
    c = quad_swap(out_grad).reshape(n, width)
    qkv_full = gather(qkv_weight)
    proj_full = gather(proj_weight)
    up_full = gather(up_weight)
    down_full = gather(down_weight)

    qkv_bias = jnp.concatenate([query_bias, jnp.zeros_like(query_bias), value_bias])[None]
    act1, qkv = norm_qkv(x, first_gain[None], first_bias[None], qkv_bias, qkv_full)
    attended, stats = attention(lens, qkv)
    out, hidden, du, act2, dz, dm, dy, dout, vecs, uvec = mlp(
        x, c, attended, proj_bias[None], second_gain[None], second_bias[None],
        up_bias[None], down_bias[None], proj_full, up_full, down_full,
    )
    output = quad_swap(out.reshape(row_count, piece_len, width))
    down_grad = scatter(outer_rows(hidden, dz))
    up_grad = scatter(outer_cols(act2, du, 768))
    proj_grad = scatter(outer_rows(attended, dy))
    dq, dk, dv = attention_back(lens, qkv, attended, dout, stats)
    qkv_outer_grad, qkv_vec = qkv_outer(act1, dq, dk, dv)
    qkv_grad = scatter(qkv_outer_grad)
    dx, vecs1 = input_grad(x, dm, first_gain[None], dq, dk, dv, qkv_full)
    tokens_grad = quad_swap(dx.reshape(row_count, piece_len, width))

    packed = jnp.concatenate(
        [
            vecs1[0], vecs1[1], qkv_vec[0], qkv_vec[2], vecs[2], vecs[0], vecs[1],
            vecs[3], uvec[0],
        ]
    ).reshape(-1, 128)
    total = lax.psum(packed, ("tok", "row")).reshape(-1)
    v = [total[i * D : (i + 1) * D] for i in range(8)]
    return (
        output, tokens_grad, qkv_grad, proj_grad, up_grad, down_grad,
        v[0], v[1], v[2], v[3], v[4], v[5], v[6], total[8 * D :], v[7],
    )


def solution(mesh):
    rows = P("row", "tok", None)
    weight = P("tok", "row")
    in_specs = (
        rows, rows, P("row", None, None), P(), P(), weight, P(), P(), weight, P(), P(), P(),
        weight, P(), weight, P(),
    )
    out_specs = (rows, rows, weight, weight, weight, weight) + (P(),) * 9
    return jax.shard_map(
        per_device, mesh=mesh, in_specs=in_specs, out_specs=out_specs, check_vma=False
    )
```

```python
import functools
import math

import jax
import jax.numpy as jnp
from jax import lax
from jax.experimental import pallas as pl
from jax.experimental.pallas import tpu as pltpu
from jax.sharding import PartitionSpec as P

D = 768
H = 12
HD = 64
FF = 3072
DEPTH = 48
DOCS = 8
BLK = 256
QUAD = 4

EPSILON = 1e-05
TANH_ROOT = 0.7978845608028654
TANH_CUBIC = 0.044715
BETA = 1.0 / math.sqrt(DEPTH)
SCALE = 1.0 / math.sqrt(HD)
F32 = jnp.float32
BF16 = jnp.bfloat16
VMEM_LIMIT = 56 * 2**20
EASE = 8

NT = (((1,), (1,)), ((), ()))
NN = (((1,), (0,)), ((), ()))
TN = (((0,), (0,)), ((), ()))


def mm(a, b, dims=NN):
    return lax.dot_general(a, b, dims, preferred_element_type=F32)


def params():
    return pltpu.CompilerParams(vmem_limit_bytes=VMEM_LIMIT)


def cost(flops, nbytes, trans=0):
    return pl.CostEstimate(
        flops=int(flops // EASE), bytes_accessed=int(nbytes // EASE), transcendentals=int(trans // EASE)
    )


def norm_parts(x):
    centre = x - jnp.mean(x, axis=-1, keepdims=True)
    inverse = lax.rsqrt(jnp.mean(centre * centre, axis=-1, keepdims=True) + EPSILON)
    return centre * inverse, inverse


def norm_back(grad, normed, inverse, gain):
    spread = grad * gain
    return inverse * (
        spread
        - jnp.mean(spread, axis=-1, keepdims=True)
        - normed * jnp.mean(spread * normed, axis=-1, keepdims=True)
    )


def whole(ref, sem):
    return pltpu.make_async_copy(ref, ref, sem)


def place_pieces(ids, pieces, quad_first, targets):
    count = len(pieces) // 2
    for side in range(2):
        for block in range(count):
            ref = pieces[side * count + block]
            for slot in range(ref.shape[0]):
                d, e = (slot, block) if quad_first else (block, slot)
                shard = (ids[1] ^ e) * QUAD + (ids[0] ^ d)
                rows = ref.shape[1]
                here = pl.ds(pl.multiple_of(shard * rows, 16), rows)
                for at, lanes, w, sem in targets:
                    there = pl.ds(pl.multiple_of((ids[2] ^ side) * lanes, 128), lanes)
                    src = ref.at[slot, :, pl.ds(at, lanes)]
                    pltpu.make_async_copy(src, w.at[here, there], sem).start()


def place_halves(halves, w, sem):
    cols = halves.shape[2]
    for h in range(2):
        pltpu.make_async_copy(halves.at[h], w.at[:, pl.ds(h * cols, cols)], sem).start()


def place(ids, parts, w, sem):
    if len(parts) == 1:
        place_halves(parts[0], w, sem)
    else:
        place_pieces(ids, parts, False, [(0, parts[0].shape[2], w, sem)])


def qkv_kernel(parts, ids, x_ref, g_ref, b_ref, qb_ref, *rest):
    w_hbm, (act_ref, qkv_ref, w_vmem, sem) = rest[:parts], rest[parts:]
    first = pl.program_id(0) == 0

    @pl.when(first)
    def _():
        place(ids, w_hbm, w_vmem, sem)

    normed, _ = norm_parts(x_ref[...].astype(F32))
    act = (normed * g_ref[...] + b_ref[...]).astype(BF16)
    act_ref[...] = act

    @pl.when(first)
    def _():
        whole(w_vmem, sem).wait()

    qkv_ref[...] = (mm(act, w_vmem[...]) + qb_ref[...]).astype(BF16)


def norm_qkv(ids, x, gain, bias, qkv_bias, w):
    n = x.shape[0]
    tile = BLK
    const = lambda i: (0, 0)
    return pl.pallas_call(
        functools.partial(qkv_kernel, len(w)),
        grid=(n // tile,),
        in_specs=[
            pl.BlockSpec(memory_space=pltpu.SMEM),
            pl.BlockSpec((tile, D), lambda i: (i, 0)),
            pl.BlockSpec((1, D), const),
            pl.BlockSpec((1, D), const),
            pl.BlockSpec((1, 3 * D), const),
        ]
        + [pl.BlockSpec(memory_space=pl.ANY)] * len(w),
        out_specs=[
            pl.BlockSpec((tile, D), lambda i: (i, 0)),
            pl.BlockSpec((tile, 3 * D), lambda i: (i, 0)),
        ],
        out_shape=[
            jax.ShapeDtypeStruct((n, D), BF16),
            jax.ShapeDtypeStruct((n, 3 * D), BF16),
        ],
        scratch_shapes=[pltpu.VMEM((D, 3 * D), BF16), pltpu.SemaphoreType.DMA],
        compiler_params=params(),
        cost_estimate=cost(2 * n * D * 3 * D, 2 * (n * 5 * D + 3 * D * D)),
        name="norm_qkv",
    )(ids, x, gain, bias, qkv_bias, *w)


def first_of_doc(lens_ref, positions):
    start = jnp.zeros_like(positions)
    end = 0
    for d in range(DOCS):
        end = end + lens_ref[0, d]
        start = jnp.where(positions >= end, end, start)
    return start


def lane_half(h):
    lane = lax.broadcasted_iota(jnp.int32, (1, 128), 1)
    return (lane >= h * HD) & (lane < (h + 1) * HD)


def attn_kernel(lens_ref, q_ref, k_ref, v_ref, o_ref, l_ref, start_ref):
    pair = pl.program_id(0)
    n = q_ref.shape[0]
    nb = n // BLK

    @pl.when(pair == 0)
    def _():
        start_ref[...] = first_of_doc(lens_ref, lax.broadcasted_iota(jnp.int32, (n, 1), 0))
        l_ref[...] = jnp.zeros_like(l_ref)

    lane = lax.broadcasted_iota(jnp.int32, (1, 128), 1)
    for i in range(nb):
        lo = max(0, i - 2)
        rows = pl.ds(i * BLK, BLK)
        keys = pl.ds(lo * BLK, (i + 1 - lo) * BLK)
        width = (i + 1 - lo) * BLK
        q = q_ref[rows, :] * jnp.asarray(SCALE, BF16)
        k = k_ref[keys, :]
        v = v_ref[keys, :]
        kpos = lax.broadcasted_iota(jnp.int32, (1, width), 1) + lo * BLK
        qpos = lax.broadcasted_iota(jnp.int32, (BLK, 1), 0) + i * BLK
        allowed = (kpos >= start_ref[rows, :]) & (kpos <= qpos)
        outs = []
        stats = l_ref[rows, :]
        for h in range(2):
            qh = jnp.where(lane_half(h), q, jnp.zeros_like(q))
            s = jnp.where(allowed, mm(qh, k, NT), -1e9)
            m = jnp.max(s, axis=-1, keepdims=True)
            p = jnp.exp(s - m)
            total = jnp.sum(p, axis=-1, keepdims=True)
            outs.append(mm(p.astype(BF16), v) / total)
            stats = jnp.where(lane == 2 * pair + h, m + jnp.log(total), stats)
        l_ref[rows, :] = stats
        o_ref[rows, :] = jnp.where(lane_half(0), outs[0], outs[1]).astype(BF16)


def attention(lens, qkv):
    n = qkv.shape[0]
    pairs = H // 2
    spec = lambda w: pl.BlockSpec((n, 128), lambda p: (0, w * pairs + p))
    return pl.pallas_call(
        attn_kernel,
        grid=(pairs,),
        in_specs=[pl.BlockSpec(memory_space=pltpu.SMEM), spec(0), spec(1), spec(2)],
        out_specs=[
            pl.BlockSpec((n, 128), lambda p: (0, p)),
            pl.BlockSpec((n, 128), lambda p: (0, 0)),
        ],
        out_shape=[jax.ShapeDtypeStruct((n, D), BF16), jax.ShapeDtypeStruct((n, 128), F32)],
        scratch_shapes=[pltpu.VMEM((n, 1), jnp.int32)],
        compiler_params=params(),
        cost_estimate=cost(2 * 2 * H * n * n * HD * 0.6, 2 * n * 4 * D, H * n * n * 0.6),
        name="attention",
    )(lens, qkv, qkv, qkv)


def attn_back_kernel(
    lens_ref, q_ref, k_ref, v_ref, o_ref, do_ref, l_ref, out_hbm,
    start_ref, lt_ref, dk_acc, dv_acc, bufs, sems,
):
    pair = pl.program_id(0)
    pairs = pl.num_programs(0)
    n = q_ref.shape[0]
    nb = n // BLK
    slot = pair % 2

    def copies(p, at):
        return [
            pltpu.make_async_copy(
                bufs.at[at, w],
                out_hbm.at[:, pl.ds(pl.multiple_of(w * D + p * 128, 128), 128)],
                sems.at[at, w],
            )
            for w in range(3)
        ]

    @pl.when(pair == 0)
    def _():
        start_ref[...] = first_of_doc(lens_ref, lax.broadcasted_iota(jnp.int32, (8, n), 1))
        lt_ref[...] = l_ref[...].T

    @pl.when(pair >= 2)
    def _():
        for c in copies(pair - 2, slot):
            c.wait()

    prod = (o_ref[...].astype(F32) * do_ref[...].astype(F32)).T
    for h in range(2):
        half = lane_half(h)
        delta = jnp.sum(prod[h * HD : (h + 1) * HD, :], axis=0, keepdims=True)
        logs = lt_ref[pl.ds(2 * pair + h, 1), :]
        for i in range(nb):
            rows = pl.ds(i * BLK, BLK)
            q = q_ref[rows, :] * jnp.asarray(SCALE, BF16)
            q = jnp.where(half, q, jnp.zeros_like(q))
            do = do_ref[rows, :]
            do = jnp.where(half, do, jnp.zeros_like(do))
            logs_i = logs[:, i * BLK : (i + 1) * BLK]
            delta_i = delta[:, i * BLK : (i + 1) * BLK]
            start_i = start_ref[0:1, i * BLK : (i + 1) * BLK]
            qpos = lax.broadcasted_iota(jnp.int32, (1, BLK), 1) + i * BLK
            dq = jnp.zeros((BLK, 128), F32)
            for j in range(max(0, i - 2), i + 1):
                keys = pl.ds(j * BLK, BLK)
                k = k_ref[keys, :]
                v = v_ref[keys, :]
                kpos = lax.broadcasted_iota(jnp.int32, (BLK, 1), 0) + j * BLK
                allowed = kpos >= start_i
                if i == j:
                    allowed = allowed & (kpos <= qpos)
                p = jnp.where(allowed, jnp.exp(mm(k, q, NT) - logs_i), 0.0)
                dp = mm(v, do, NT)
                ds = (p * (dp - delta_i)).astype(BF16)
                dv = mm(p.astype(BF16), do)
                dk = mm(ds, q)
                if h == 0 and i == j:
                    dv_acc[keys, :] = dv
                    dk_acc[keys, :] = dk
                else:
                    dv_acc[keys, :] += dv
                    dk_acc[keys, :] += dk
                kh = jnp.where(half, k, jnp.zeros_like(k))
                dq = dq + mm(ds, kh, TN)
            dq = (dq * SCALE).astype(BF16)
            if h == 0:
                bufs[slot, 0, rows, :] = dq
            else:
                bufs[slot, 0, rows, :] = jnp.where(half, dq, bufs[slot, 0, rows, :])
    bufs[slot, 1] = dk_acc[...].astype(BF16)
    bufs[slot, 2] = dv_acc[...].astype(BF16)
    for c in copies(pair, slot):
        c.start()

    @pl.when(pair == pairs - 1)
    def _():
        for c in copies(pair - 1, 1 - slot) + copies(pair, slot):
            c.wait()


def attention_back(lens, qkv, attended, dout, stats):
    n = qkv.shape[0]
    pairs = H // 2
    spec = lambda w: pl.BlockSpec((n, 128), lambda p: (0, w * pairs + p))
    one = pl.BlockSpec((n, 128), lambda p: (0, p))
    return pl.pallas_call(
        attn_back_kernel,
        grid=(pairs,),
        in_specs=[
            pl.BlockSpec(memory_space=pltpu.SMEM), spec(0), spec(1), spec(2), one, one,
            pl.BlockSpec((n, 128), lambda p: (0, 0)),
        ],
        out_specs=pl.BlockSpec(memory_space=pl.ANY),
        out_shape=jax.ShapeDtypeStruct((n, 3 * D), BF16),
        scratch_shapes=[
            pltpu.VMEM((8, n), jnp.int32),
            pltpu.VMEM((128, n), F32),
            pltpu.VMEM((n, 128), F32),
            pltpu.VMEM((n, 128), F32),
            pltpu.VMEM((2, 3, n, 128), BF16),
            pltpu.SemaphoreType.DMA((2, 3)),
        ],
        compiler_params=params(),
        cost_estimate=cost(5 * 2 * H * n * n * HD * 0.6, 2 * n * 8 * D, H * n * n * 0.6),
        name="attention_back",
    )(lens, qkv, qkv, qkv, attended, dout, stats)


def start_mlp_weights(ids, w_hbm, wp, wu, wd, sem):
    if len(w_hbm) == 3:
        place_halves(w_hbm[0], wp, sem.at[0])
        place_halves(w_hbm[1], wu, sem.at[1])
    else:
        up = (0, FF // 2, wu, sem.at[1])
        place_pieces(ids, w_hbm[:-1], False, [(FF // 2, D // 2, wp, sem.at[0]), up])
    place_halves(w_hbm[-1], wd, sem.at[2])


def mlp_kernel(
    parts, ids, x_ref, att_ref, pb_ref, g_ref, b_ref, ub_ref, db_ref, *rest
):
    w_hbm = rest[:parts]
    mid_ref, out_ref, hid_ref, slope_ref, act_ref, wp, wu, wd, sem = rest[parts:]
    step = pl.program_id(0)

    @pl.when(step == 0)
    def _():
        start_mlp_weights(ids, w_hbm, wp, wu, wd, sem)
        whole(wp, sem.at[0]).wait()

    middle = x_ref[...].astype(F32) + BETA * (mm(att_ref[...], wp[...]) + pb_ref[...])
    mid_ref[...] = middle
    normed, _ = norm_parts(middle)
    act = (normed * g_ref[...] + b_ref[...]).astype(BF16)
    act_ref[...] = act

    @pl.when(step == 0)
    def _():
        whole(wu, sem.at[1]).wait()
        whole(wd, sem.at[2]).wait()

    chunk = 768
    branch = jnp.zeros(middle.shape, F32)
    for f in range(FF // chunk):
        cols = pl.ds(f * chunk, chunk)
        u = mm(act, wu[:, cols]) + ub_ref[:, cols]
        u2 = u * u
        half_t = 0.5 * jnp.tanh(u * (TANH_ROOT + (TANH_ROOT * TANH_CUBIC) * u2))
        gate = 0.5 + half_t
        hidden = (u * gate).astype(BF16)
        hid_ref[:, cols] = hidden
        branch = branch + mm(hidden, wd[cols, :])
        slope = gate + u * (0.5 - 2.0 * half_t * half_t) * (
            TANH_ROOT + (3.0 * TANH_ROOT * TANH_CUBIC) * u2
        )
        slope_ref[:, cols] = slope.astype(BF16)
    out_ref[...] = (middle + BETA * (branch + db_ref[...])).astype(BF16)


MLP_SCRATCH = [
    pltpu.VMEM((D, D), BF16),
    pltpu.VMEM((D, FF), BF16),
    pltpu.VMEM((FF, D), BF16),
    pltpu.SemaphoreType.DMA((3,)),
]


def mlp(ids, x, att, pb, gain, bias, ub, db, w):
    n = x.shape[0]
    tile = BLK
    row = lambda w: pl.BlockSpec((tile, w), lambda i: (i, 0))
    vec = lambda w: pl.BlockSpec((1, w), lambda i: (0, 0))
    sds = jax.ShapeDtypeStruct
    return pl.pallas_call(
        functools.partial(mlp_kernel, len(w)),
        grid=(n // tile,),
        in_specs=[pl.BlockSpec(memory_space=pltpu.SMEM)]
        + [row(D), row(D), vec(D), vec(D), vec(D), vec(FF), vec(D)]
        + [pl.BlockSpec(memory_space=pl.ANY)] * len(w),
        out_specs=[row(D), row(D), row(FF), row(FF), row(D)],
        out_shape=[
            sds((n, D), F32), sds((n, D), BF16), sds((n, FF), BF16), sds((n, FF), BF16),
            sds((n, D), BF16),
        ],
        scratch_shapes=MLP_SCRATCH,
        compiler_params=params(),
        cost_estimate=cost(2 * n * (2 * D * FF + D * D), 2 * n * (7 * D + 2 * FF), n * FF),
        name="mlp",
    )(ids, x, att, pb, gain, bias, ub, db, *w)


def mlp_back_kernel(parts, ids, c_ref, mid_ref, slope_ref, g_ref, *rest):
    w_hbm = rest[:parts]
    du_ref, dm_ref, dy_ref, do_ref, vec_ref, uvec_ref, wp, wu, wd, sem = rest[parts:]
    step = pl.program_id(0)

    @pl.when(step == 0)
    def _():
        start_mlp_weights(ids, w_hbm, wp, wu, wd, sem)
        vec_ref[...] = jnp.zeros_like(vec_ref)
        uvec_ref[...] = jnp.zeros_like(uvec_ref)

    grad_out = c_ref[...].astype(F32)
    dz = (BETA * grad_out).astype(BF16)
    normed, inverse = norm_parts(mid_ref[...])

    @pl.when(step == 0)
    def _():
        whole(wd, sem.at[2]).wait()
        whole(wu, sem.at[1]).wait()
        whole(wp, sem.at[0]).wait()

    chunk = 768
    da = jnp.zeros(normed.shape, F32)
    for f in range(FF // chunk):
        cols = pl.ds(f * chunk, chunk)
        du = (mm(dz, wd[cols, :], NT) * slope_ref[:, cols].astype(F32)).astype(BF16)
        du_ref[:, cols] = du
        uvec_ref[0:1, cols] += jnp.sum(du.astype(F32), axis=0, keepdims=True)
        da = da + mm(du, wu[:, cols], NT)
    dm = grad_out + norm_back(da, normed, inverse, g_ref[...])
    dm_ref[...] = dm
    dy = (BETA * dm).astype(BF16)
    dy_ref[...] = dy
    do_ref[...] = mm(dy, wp[...], NT).astype(BF16)
    vec_ref[0:1, :] += jnp.sum(da * normed, axis=0, keepdims=True)
    vec_ref[1:2, :] += jnp.sum(da, axis=0, keepdims=True)
    vec_ref[2:3, :] += jnp.sum(dy.astype(F32), axis=0, keepdims=True)
    vec_ref[3:4, :] += jnp.sum(dz.astype(F32), axis=0, keepdims=True)


def mlp_back(ids, c, middle, slope, gain, w):
    n = c.shape[0]
    tile = BLK
    const = lambda i: (0, 0)
    row = lambda w: pl.BlockSpec((tile, w), lambda i: (i, 0))
    sds = jax.ShapeDtypeStruct
    return pl.pallas_call(
        functools.partial(mlp_back_kernel, len(w)),
        grid=(n // tile,),
        in_specs=[pl.BlockSpec(memory_space=pltpu.SMEM)]
        + [row(D), row(D), row(FF), pl.BlockSpec((1, D), const)]
        + [pl.BlockSpec(memory_space=pl.ANY)] * len(w),
        out_specs=[
            row(FF), row(D), row(D), row(D), pl.BlockSpec((8, D), const), pl.BlockSpec((8, FF), const),
        ],
        out_shape=[
            sds((n, FF), BF16), sds((n, D), F32), sds((n, D), BF16), sds((n, D), BF16),
            sds((8, D), F32), sds((8, FF), F32),
        ],
        scratch_shapes=MLP_SCRATCH,
        compiler_params=params(),
        cost_estimate=cost(2 * n * (2 * D * FF + D * D), 2 * n * (7 * D + 2 * FF), n * FF),
        name="mlp_back",
    )(ids, c, middle, slope, gain, *w)


def store_sides(row, r, mine, theirs):
    width = r.shape[1] // 2

    @pl.when(row == 0)
    def _():
        mine[...] = r[:, :width].astype(BF16)
        theirs[...] = r[:, width:].astype(BF16)

    @pl.when(row == 1)
    def _():
        theirs[...] = r[:, :width].astype(BF16)
        mine[...] = r[:, width:].astype(BF16)


def down_outer_kernel(a_ref, c_ref, o_ref, dz):
    @pl.when(pl.program_id(0) == 0)
    def _():
        dz[...] = (BETA * c_ref[...].astype(F32)).astype(BF16)

    r = mm(a_ref[...], dz[...], TN).astype(BF16)
    width = o_ref.shape[2]
    o_ref[0] = r[:, :width]
    o_ref[1] = r[:, width:]


def down_outer(hidden, c):
    n = hidden.shape[0]
    return pl.pallas_call(
        down_outer_kernel,
        grid=(FF // D,),
        in_specs=[
            pl.BlockSpec((n, D), lambda i: (0, i)),
            pl.BlockSpec((n, D), lambda i: (0, 0)),
        ],
        out_specs=pl.BlockSpec((2, D, D // 2), lambda i: (0, i, 0)),
        out_shape=jax.ShapeDtypeStruct((2, FF, D // 2), BF16),
        scratch_shapes=[pltpu.VMEM((n, D), BF16)],
        compiler_params=params(),
        cost_estimate=cost(2 * n * FF * D, 2 * (n * (FF + D) + FF * D)),
        name="down_outer",
    )(hidden, c)


def up_outer_kernel(ids, act_ref, du_ref, att_ref, dy_ref, mine, theirs):
    step = pl.program_id(0)
    r = mm(act_ref[...], du_ref[...], TN).astype(BF16)

    @pl.when(step < 2)
    def _():
        theirs[:, pl.ds(pl.multiple_of(step * D, 128), D)] = r

    @pl.when(step >= 2)
    def _():
        mine[:, pl.ds(pl.multiple_of((step - 2) * D, 128), D)] = r

    @pl.when(step == 3)
    def _():
        tail = slice(FF // 2, (FF + D) // 2)
        store_sides(ids[2], mm(att_ref[...], dy_ref[...], TN), mine.at[:, tail], theirs.at[:, tail])


def up_outer(ids, act, du, attended, dy):
    n = act.shape[0]
    width = (FF + D) // 2
    once = pl.BlockSpec((n, D), lambda i, s: (0, 0))
    out = pl.BlockSpec((D, width), lambda i, s: (0, 0))
    return pl.pallas_call(
        up_outer_kernel,
        grid_spec=pltpu.PrefetchScalarGridSpec(
            num_scalar_prefetch=1,
            grid=(FF // D,),
            in_specs=[
                once,
                pl.BlockSpec((n, D), lambda i, s: (0, (i + 2 * (1 - s[2])) % 4)),
                once,
                once,
            ],
            out_specs=[out, out],
        ),
        out_shape=[jax.ShapeDtypeStruct((D, width), BF16)] * 2,
        compiler_params=params(),
        cost_estimate=cost(2 * n * D * 2 * width, 2 * (n * (FF + 3 * D) + 2 * D * width)),
        name="up_outer",
    )(ids, act, du, attended, dy)


def qkv_outer_kernel(ids, act_ref, dqkv_ref, mine, theirs):
    step = pl.program_id(0)
    r = mm(act_ref[...], dqkv_ref[...], TN).astype(BF16)

    @pl.when(step == 0)
    def _():
        theirs[...] = r

    @pl.when(step == 1)
    def _():
        mine[...] = r


def qkv_outer(ids, act, dqkv):
    n = act.shape[0]
    width = 3 * D // 2
    out = pl.BlockSpec((D, width), lambda i, s: (0, 0))
    return pl.pallas_call(
        qkv_outer_kernel,
        grid_spec=pltpu.PrefetchScalarGridSpec(
            num_scalar_prefetch=1,
            grid=(2,),
            in_specs=[
                pl.BlockSpec((n, D), lambda i, s: (0, 0)),
                pl.BlockSpec((n, width), lambda i, s: (0, (i + 1 - s[2]) % 2)),
            ],
            out_specs=[out, out],
        ),
        out_shape=[jax.ShapeDtypeStruct((D, width), BF16)] * 2,
        compiler_params=params(),
        cost_estimate=cost(2 * n * D * 2 * width, 2 * (n * (D + 2 * width) + 2 * D * width)),
        name="qkv_outer",
    )(ids, act, dqkv)


def merge_kernel(quad_first, rows, ids, mine, theirs, *outs):
    for block, o in enumerate(outs):
        for slot in range(o.shape[0]):
            e, d = (block, slot) if quad_first else (slot, block)
            shard = (ids[1] ^ e) * QUAD + (ids[0] ^ d)
            here = pl.ds(pl.multiple_of(shard * rows, 16), rows)
            o[slot] = (mine[here, :].astype(F32) + theirs[here, :].astype(F32)).astype(BF16)


def merge(ids, mine, theirs, quad_first, name):
    left, width = mine.shape
    rows = left // (4 * QUAD)
    spec = pl.BlockSpec(memory_space=pltpu.VMEM)
    return pl.pallas_call(
        functools.partial(merge_kernel, quad_first, rows),
        in_specs=[pl.BlockSpec(memory_space=pltpu.SMEM), spec, spec],
        out_shape=[jax.ShapeDtypeStruct((4, rows, width), BF16)] * 4,
        compiler_params=params(),
        cost_estimate=cost(2 * mine.size, 6 * mine.size),
        name=name,
    )(ids, mine, theirs)


def add_quad_kernel(ids, a, b, c, d, *outs):
    for e in range(a.shape[0]):
        total = (a[e].astype(F32) + b[e].astype(F32)) + (c[e].astype(F32) + d[e].astype(F32))
        if len(outs) == 1:
            outs[0][ids[1] ^ e] = total.astype(BF16)
        else:
            outs[e][...] = total.astype(BF16)


def add_quad(ids, parts, apart, name):
    block = parts[0].shape
    sds = jax.ShapeDtypeStruct
    spec = pl.BlockSpec(memory_space=pltpu.VMEM)
    return pl.pallas_call(
        add_quad_kernel,
        in_specs=[pl.BlockSpec(memory_space=pltpu.SMEM)] + [spec] * 4,
        out_shape=[sds(block[1:], BF16)] * block[0] if apart else sds(block, BF16),
        compiler_params=params(),
        cost_estimate=cost(4 * parts[0].size, 10 * parts[0].size),
        name=name,
    )(ids, *parts)


def input_grad_kernel(parts, ids, x_ref, dm_ref, g_ref, dqkv_ref, *rest):
    w_hbm, (o_ref, vec_ref, w, sem) = rest[:parts], rest[parts:]
    first = pl.program_id(0) == 0

    @pl.when(first)
    def _():
        place(ids, w_hbm, w, sem)
        vec_ref[...] = jnp.zeros_like(vec_ref)
        whole(w, sem).wait()

    dqkv = dqkv_ref[...]
    da = mm(dqkv, w[...], NT)
    normed, inverse = norm_parts(x_ref[...].astype(F32))
    o_ref[...] = (dm_ref[...] + norm_back(da, normed, inverse, g_ref[...])).astype(BF16)
    vec_ref[0:1, 0:D] += jnp.sum(da * normed, axis=0, keepdims=True)
    vec_ref[1:2, 0:D] += jnp.sum(da, axis=0, keepdims=True)
    vec_ref[2:3, :] += jnp.sum(dqkv.astype(F32), axis=0, keepdims=True)


def input_grad(ids, x, dm, gain, dqkv, w):
    n = x.shape[0]
    tile = BLK
    const = lambda i: (0, 0)
    row = lambda wide: pl.BlockSpec((tile, wide), lambda i: (i, 0))
    return pl.pallas_call(
        functools.partial(input_grad_kernel, len(w)),
        grid=(n // tile,),
        in_specs=[pl.BlockSpec(memory_space=pltpu.SMEM), row(D), row(D), pl.BlockSpec((1, D), const), row(3 * D)]
        + [pl.BlockSpec(memory_space=pl.ANY)] * len(w),
        out_specs=[row(D), pl.BlockSpec((8, 3 * D), const)],
        out_shape=[jax.ShapeDtypeStruct((n, D), BF16), jax.ShapeDtypeStruct((8, 3 * D), F32)],
        scratch_shapes=[pltpu.VMEM((D, 3 * D), BF16), pltpu.SemaphoreType.DMA],
        compiler_params=params(),
        cost_estimate=cost(2 * n * D * 3 * D, 2 * (n * 7 * D + 3 * D * D)),
        name="input_grad",
    )(ids, x, dm, gain, dqkv, *w)


def swap(block, axis, distance):
    count = lax.axis_size(axis)
    return lax.ppermute(block, axis, [(i, i ^ distance) for i in range(count)])


def quad_swap(pieces):
    count = lax.axis_size("tok")
    groups = [list(range(g, g + QUAD)) for g in range(0, count, QUAD)]
    return lax.all_to_all(pieces, "tok", 0, 0, axis_index_groups=groups, tiled=True)


def by_halves(whole):
    over_row, height, cols = whole.shape
    if over_row == 2:
        return whole
    return (
        whole.reshape(2, over_row // 2, height, cols)
        .transpose(0, 2, 1, 3)
        .reshape(2, height, over_row // 2 * cols)
    )


def gather(shard):
    rows, cols = shard.shape
    whole = lax.all_gather(shard, ("row", "tok"), axis=0, tiled=True)
    return by_halves(whole.reshape(lax.axis_size("row"), rows * lax.axis_size("tok"), cols))


def gather_line(shard):
    return jnp.stack([shard] + [swap(shard, "tok", QUAD * e) for e in range(1, 4)])


def spread(block, steps):
    return [block] + [swap(block, "tok", step) for step in steps]


def with_partner(blocks):
    return blocks + [swap(t, "row", 1) for t in blocks]


QUAD_STEPS = (1, 2, 3)
LINE_STEPS = (QUAD, 2 * QUAD, 3 * QUAD)


def after(value, *others):
    return lax.optimization_barrier((value,) + others)[0]


def from_peers(blocks, steps):
    return [blocks[0]] + [swap(t, "tok", step) for t, step in zip(blocks[1:], steps)]


def line_swap(pieces):
    count = lax.axis_size("tok")
    groups = [list(range(q, count, QUAD)) for q in range(QUAD)]
    return lax.all_to_all(pieces, "tok", 0, 0, axis_index_groups=groups, tiled=True)


def total_of(terms):
    return sum([t.astype(F32) for t in terms[1:]], terms[0].astype(F32))


def scatter(halves):
    over_row = lax.axis_size("row")
    _, height, width = halves.shape
    cols = 2 * width // over_row
    if over_row != 2:
        halves = halves.reshape(2, height, over_row // 2, cols).transpose(0, 2, 1, 3)
    flat = halves.reshape(over_row * height, cols)
    return lax.psum_scatter(flat, ("row", "tok"), scatter_dimension=0, tiled=True).astype(F32)


def scatter_sides(sides, row_index):
    flat = jnp.stack(sides)
    return scatter(jnp.where(row_index % 2 == 0, flat, flat[::-1]))


def all_sum(block, steps):
    for step in steps:
        block = block + (swap(block, "tok", step) if step else swap(block, "row", 1))
    return block


def per_device(
    tokens,
    out_grad,
    doc_lengths,
    first_gain,
    first_bias,
    qkv_weight,
    query_bias,
    value_bias,
    proj_weight,
    proj_bias,
    second_gain,
    second_bias,
    up_weight,
    up_bias,
    down_weight,
    down_bias,
):
    row_count, piece_len, width = tokens.shape
    n = row_count * piece_len
    tok_index = lax.axis_index("tok")
    row_index = lax.axis_index("row")
    groups = lax.axis_size("tok") // QUAD
    by_permutes = lax.axis_size("row") == 2 and groups == 4
    ids = jnp.stack([tok_index % QUAD, tok_index // QUAD, row_index % 2]).astype(jnp.int32)
    lens = lax.dynamic_slice(
        doc_lengths,
        (tok_index % QUAD, tok_index // QUAD, 0),
        (1, 1, doc_lengths.shape[2]),
    )[0]

    down_full = gather(down_weight)
    x = quad_swap(tokens).reshape(n, width)
    if by_permutes:
        qkv_line = gather_line(qkv_weight)
        up_weights = jnp.concatenate([up_weight, proj_weight], axis=1)
        up_line = gather_line(after(up_weights, qkv_line))
        qkv_pieces = spread(after(qkv_line, x), QUAD_STEPS)
        qkv_full = with_partner(qkv_pieces)
        up_pieces = spread(after(up_line, *qkv_pieces), QUAD_STEPS)
        others = with_partner(up_pieces) + [down_full]
    else:
        qkv_full = [gather(qkv_weight)]
        others = [gather(proj_weight), gather(up_weight), down_full]
    qkv_bias = jnp.concatenate([query_bias, jnp.zeros_like(query_bias), value_bias])[None]
    act1, qkv = norm_qkv(ids, x, first_gain[None], first_bias[None], qkv_bias, qkv_full)
    attended, stats = attention(lens, qkv)
    c = quad_swap(after(out_grad, attended)).reshape(n, width)
    middle, out, hidden, slope, act2 = mlp(
        ids, x, attended, proj_bias[None], second_gain[None], second_bias[None],
        up_bias[None], down_bias[None], others,
    )
    output = quad_swap(out.reshape(row_count, piece_len, width))
    down_outer_grad = down_outer(hidden, c)
    down_grad = scatter(down_outer_grad)
    c = after(c, down_outer_grad)
    du, dm, dy, dout, vecs, uvec = mlp_back(ids, c, middle, slope, second_gain[None], others)
    up_sides = up_outer(ids, after(act2, output), du, attended, dy)
    if by_permutes:
        up_blocks = merge(ids, up_sides[0], swap(up_sides[1], "row", 1), False, "up_merge")
        dout = after(dout, *up_blocks)
    dqkv = attention_back(lens, qkv, attended, dout, stats)
    if by_permutes:
        up_got = from_peers(up_blocks, QUAD_STEPS)
        act1 = after(act1, *up_got[1:])
    qkv_sides = qkv_outer(ids, act1, dqkv)
    if by_permutes:
        up_got[0] = after(up_got[0], *qkv_sides)
        up_line = add_quad(ids, up_got, False, "up_add")
        qkv_mine = after(qkv_sides[0], up_line)
        up_line = line_swap(up_line)
        qkv_blocks = merge(ids, qkv_mine, swap(qkv_sides[1], "row", 1), False, "qkv_merge")
        dqkv = after(dqkv, down_grad, *qkv_blocks)
        qkv_got = from_peers(qkv_blocks, QUAD_STEPS)
        qkv_got[0] = after(qkv_got[0], up_line)
        qkv_shards = add_quad(ids, qkv_got, True, "qkv_add")
        qkv_grad = total_of(from_peers(qkv_shards, LINE_STEPS))
        up_proj = total_of([up_line[e] for e in range(groups)])
        up_grad, proj_grad = up_proj[:, : FF // 2], up_proj[:, FF // 2 :]
    else:
        up_grad = scatter_sides([t[:, : FF // 2] for t in up_sides], row_index)
        proj_grad = scatter_sides([t[:, FF // 2 :] for t in up_sides], row_index)
        qkv_grad = scatter_sides(qkv_sides, row_index)
    dx, vecs1 = input_grad(ids, x, dm, first_gain[None], dqkv, qkv_full)
    tokens_grad = quad_swap(dx.reshape(row_count, piece_len, width))
    packed = jnp.concatenate(
        [
            vecs1[0, :D], vecs1[1, :D], vecs1[2, :D], vecs1[2, 2 * D :], vecs[2], vecs[0], vecs[1],
            vecs[3], uvec[0],
        ]
    ).reshape(-1, 128)
    if by_permutes:
        packed = all_sum(after(packed, *qkv_got[1:]), (0, 1, 2))
        total = all_sum(after(packed, tokens_grad), LINE_STEPS[:2]).reshape(-1)
    else:
        total = lax.psum(packed, ("tok", "row")).reshape(-1)
    v = [total[i * D : (i + 1) * D] for i in range(8)]
    return (
        output, tokens_grad, qkv_grad, proj_grad, up_grad, down_grad,
        v[0], v[1], v[2], v[3], v[4], v[5], v[6], total[8 * D :], v[7],
    )


def solution(mesh):
    rows = P("row", "tok", None)
    weight = P("tok", "row")
    in_specs = (
        rows, rows, P("row", None, None), P(), P(), weight, P(), P(), weight, P(), P(), P(),
        weight, P(), weight, P(),
    )
    out_specs = (rows, rows, weight, weight, weight, weight) + (P(),) * 9
    return jax.shard_map(
        per_device, mesh=mesh, in_specs=in_specs, out_specs=out_specs, check_vma=False
    )
```

```python
import functools
import math

import jax
import jax.numpy as jnp
from jax import lax
from jax.experimental import pallas as pl
from jax.experimental.pallas import tpu as pltpu
from jax.sharding import PartitionSpec as P

D = 768
H = 12
HD = 64
FF = 3072
DEPTH = 48
DOCS = 8
BLK = 256
QUAD = 4

EPSILON = 1e-05
MASKED = -1e9
TANH_ROOT = 0.7978845608028654
TANH_CUBIC = 0.044715
BETA = 1.0 / math.sqrt(DEPTH)
SCALE = 1.0 / math.sqrt(HD)
F32 = jnp.float32
BF16 = jnp.bfloat16
VMEM_LIMIT = 56 * 2**20
EASE = 8

NT = (((1,), (1,)), ((), ()))
NN = (((1,), (0,)), ((), ()))
TN = (((0,), (0,)), ((), ()))


def mm(a, b, dims=NN):
    return lax.dot_general(a, b, dims, preferred_element_type=F32)


def params():
    return pltpu.CompilerParams(vmem_limit_bytes=VMEM_LIMIT)


def cost(flops, nbytes, trans=0):
    return pl.CostEstimate(
        flops=int(flops // EASE), bytes_accessed=int(nbytes // EASE), transcendentals=int(trans // EASE)
    )


def norm_parts(x):
    centre = x - jnp.mean(x, axis=-1, keepdims=True)
    inverse = lax.rsqrt(jnp.mean(centre * centre, axis=-1, keepdims=True) + EPSILON)
    return centre * inverse, inverse


def norm_back(grad, normed, inverse, gain):
    spread = grad * gain
    return inverse * (
        spread
        - jnp.mean(spread, axis=-1, keepdims=True)
        - normed * jnp.mean(spread * normed, axis=-1, keepdims=True)
    )


def whole(ref, sem):
    return pltpu.make_async_copy(ref, ref, sem)


def place_pieces(ids, pieces, quad_first, targets):
    count = len(pieces) // 2
    for side in range(2):
        for block in range(count):
            ref = pieces[side * count + block]
            for slot in range(ref.shape[0]):
                d, e = (slot, block) if quad_first else (block, slot)
                shard = (ids[1] ^ e) * QUAD + (ids[0] ^ d)
                rows = ref.shape[1]
                here = pl.ds(pl.multiple_of(shard * rows, 16), rows)
                for at, lanes, w, sem in targets:
                    there = pl.ds(pl.multiple_of((ids[2] ^ side) * lanes, 128), lanes)
                    src = ref.at[slot, :, pl.ds(at, lanes)]
                    pltpu.make_async_copy(src, w.at[here, there], sem).start()


def place_halves(halves, w, sem):
    cols = halves.shape[2]
    for h in range(2):
        pltpu.make_async_copy(halves.at[h], w.at[:, pl.ds(h * cols, cols)], sem).start()


def place(ids, parts, w, sem):
    if len(parts) == 1:
        place_halves(parts[0], w, sem)
    else:
        place_pieces(ids, parts, False, [(0, parts[0].shape[2], w, sem)])


def qkv_kernel(parts, ids, x_ref, g_ref, b_ref, qb_ref, *rest):
    w_hbm, (act_ref, qkv_ref, w_vmem, sem) = rest[:parts], rest[parts:]
    first = pl.program_id(0) == 0

    @pl.when(first)
    def _():
        place(ids, w_hbm, w_vmem, sem)

    normed, _ = norm_parts(x_ref[...].astype(F32))
    act = (normed * g_ref[...] + b_ref[...]).astype(BF16)
    act_ref[...] = act

    @pl.when(first)
    def _():
        whole(w_vmem, sem).wait()

    qkv_ref[...] = (mm(act, w_vmem[...]) + qb_ref[...]).astype(BF16)


def norm_qkv(ids, x, gain, bias, qkv_bias, w):
    n = x.shape[0]
    tile = BLK
    const = lambda i: (0, 0)
    return pl.pallas_call(
        functools.partial(qkv_kernel, len(w)),
        grid=(n // tile,),
        in_specs=[
            pl.BlockSpec(memory_space=pltpu.SMEM),
            pl.BlockSpec((tile, D), lambda i: (i, 0)),
            pl.BlockSpec((1, D), const),
            pl.BlockSpec((1, D), const),
            pl.BlockSpec((1, 3 * D), const),
        ]
        + [pl.BlockSpec(memory_space=pl.ANY)] * len(w),
        out_specs=[
            pl.BlockSpec((tile, D), lambda i: (i, 0)),
            pl.BlockSpec((tile, 3 * D), lambda i: (i, 0)),
        ],
        out_shape=[
            jax.ShapeDtypeStruct((n, D), BF16),
            jax.ShapeDtypeStruct((n, 3 * D), BF16),
        ],
        scratch_shapes=[pltpu.VMEM((D, 3 * D), BF16), pltpu.SemaphoreType.DMA],
        compiler_params=params(),
        cost_estimate=cost(2 * n * D * 3 * D, 2 * (n * 5 * D + 3 * D * D)),
        name="norm_qkv",
    )(ids, x, gain, bias, qkv_bias, *w)


def first_of_doc(lens_ref, positions):
    start = jnp.zeros_like(positions)
    end = 0
    for d in range(DOCS):
        end = end + lens_ref[0, d]
        start = jnp.where(positions >= end, end, start)
    return start


def lane_half(h):
    lane = lax.broadcasted_iota(jnp.int32, (1, 128), 1)
    return (lane >= h * HD) & (lane < (h + 1) * HD)


WINDOW = 2


def mask(lens_ref, keys_at, keys, queries_at, queries):
    qpos = lax.broadcasted_iota(jnp.int32, (1, queries), 1) + queries_at
    kpos = lax.broadcasted_iota(jnp.int32, (keys, 1), 0) + keys_at
    return jnp.where((kpos >= first_of_doc(lens_ref, qpos)) & (kpos <= qpos), 0.0, MASKED)


def attn_kernel(lens_ref, q_ref, k_ref, v_ref, o_ref, l_ref, mask_ref):
    pair = pl.program_id(0)
    blocks = []
    for i in range(q_ref.shape[0] // BLK):
        low = max(0, i - WINDOW)
        blocks.append((low * BLK, (i + 1 - low) * BLK, i * BLK))

    @pl.when(pair == 0)
    def _():
        l_ref[...] = jnp.zeros_like(l_ref)
        for first, count, at in blocks:
            mask_ref[0:count, at : at + BLK] = mask(lens_ref, first, count, at, BLK)

    for first, count, at in blocks:
        rows = slice(at, at + BLK)
        q = q_ref[rows, :] * jnp.asarray(SCALE, BF16)
        k = k_ref[first : first + count, :]
        v = v_ref[first : first + count, :]
        out = None
        for h in range(2):
            half = lane_half(h)
            s = mm(k, jnp.where(half, q, jnp.zeros_like(q)), NT) + mask_ref[0:count, rows]
            m = jnp.max(s, axis=0, keepdims=True)
            p = jnp.exp(s - m)
            total = jnp.sum(p, axis=0, keepdims=True)
            probs = (p * (1.0 / total)).astype(BF16)
            o = mm(probs, jnp.where(half, v, jnp.zeros_like(v)), TN)
            out = o if out is None else out + o
            l_ref[pl.ds(2 * pair + h, 1), rows] = m + jnp.log(total)
        o_ref[rows, :] = out.astype(BF16)


def attention(lens, qkv):
    n = qkv.shape[0]
    pairs = H // 2
    spec = lambda w: pl.BlockSpec((n, 128), lambda p: (0, w * pairs + p))
    return pl.pallas_call(
        attn_kernel,
        grid=(pairs,),
        in_specs=[pl.BlockSpec(memory_space=pltpu.SMEM), spec(0), spec(1), spec(2)],
        out_specs=[
            pl.BlockSpec((n, 128), lambda p: (0, p)),
            pl.BlockSpec((16, n), lambda p: (0, 0)),
        ],
        out_shape=[jax.ShapeDtypeStruct((n, D), BF16), jax.ShapeDtypeStruct((16, n), F32)],
        scratch_shapes=[pltpu.VMEM(((WINDOW + 1) * BLK, n), F32)],
        compiler_params=params(),
        cost_estimate=cost(2 * 2 * H * n * n * HD * 0.6, 2 * n * 4 * D, H * n * n * 0.6),
        name="attention",
    )(lens, qkv, qkv, qkv)


def attn_back_kernel(
    lens_ref, q_ref, k_ref, v_ref, o_ref, do_ref, l_ref, out_hbm, mask_ref, dq_acc, bufs, sems
):
    pair = pl.program_id(0)
    pairs = pl.num_programs(0)
    n = q_ref.shape[0]
    slot = pair % 2
    blocks = [(at, min((WINDOW + 1) * BLK, n - at)) for at in range(0, n, BLK)]

    def copies(p, at):
        return [
            pltpu.make_async_copy(
                bufs.at[at, w],
                out_hbm.at[:, pl.ds(pl.multiple_of(w * D + p * 128, 128), 128)],
                sems.at[at, w],
            )
            for w in range(3)
        ]

    @pl.when(pair == 0)
    def _():
        for at, count in blocks:
            mask_ref[at : at + BLK, 0:count] = mask(lens_ref, at, BLK, at, count)

    @pl.when(pair >= 2)
    def _():
        for c in copies(pair - 2, slot):
            c.wait()

    prod = (o_ref[...].astype(F32) * do_ref[...].astype(F32)).T
    dq_acc[...] = jnp.zeros_like(dq_acc)
    for at, count in blocks:
        keys = slice(at, at + BLK)
        queries = slice(at, at + count)
        k = k_ref[keys, :]
        v = v_ref[keys, :]
        q = q_ref[queries, :] * jnp.asarray(SCALE, BF16)
        do = do_ref[queries, :]
        dk = dv = None
        for h in range(2):
            half = lane_half(h)
            inner = jnp.sum(prod[h * HD : (h + 1) * HD, queries], axis=0, keepdims=True)
            logs = l_ref[pl.ds(2 * pair + h, 1), queries]
            qh = jnp.where(half, q, jnp.zeros_like(q))
            doh = jnp.where(half, do, jnp.zeros_like(do))
            kh = jnp.where(half, k, jnp.zeros_like(k))
            p = jnp.exp(mm(k, qh, NT) + (mask_ref[keys, 0:count] - logs))
            ds = (p * (mm(v, doh, NT) - inner)).astype(BF16)
            dvh = mm(p.astype(BF16), doh)
            dkh = mm(ds, qh)
            dv, dk = (dvh, dkh) if h == 0 else (dv + dvh, dk + dkh)
            dq_acc[queries, :] += mm(ds, kh, TN)
        bufs[slot, 1, keys, :] = dk.astype(BF16)
        bufs[slot, 2, keys, :] = dv.astype(BF16)
    bufs[slot, 0] = (dq_acc[...] * SCALE).astype(BF16)
    for c in copies(pair, slot):
        c.start()

    @pl.when(pair == pairs - 1)
    def _():
        for c in copies(pair - 1, 1 - slot) + copies(pair, slot):
            c.wait()


def attention_back(lens, qkv, attended, dout, stats):
    n = qkv.shape[0]
    pairs = H // 2
    spec = lambda w: pl.BlockSpec((n, 128), lambda p: (0, w * pairs + p))
    one = pl.BlockSpec((n, 128), lambda p: (0, p))
    return pl.pallas_call(
        attn_back_kernel,
        grid=(pairs,),
        in_specs=[
            pl.BlockSpec(memory_space=pltpu.SMEM), spec(0), spec(1), spec(2), one, one,
            pl.BlockSpec((16, n), lambda p: (0, 0)),
        ],
        out_specs=pl.BlockSpec(memory_space=pl.ANY),
        out_shape=jax.ShapeDtypeStruct((n, 3 * D), BF16),
        scratch_shapes=[
            pltpu.VMEM((n, (WINDOW + 1) * BLK), F32),
            pltpu.VMEM((n, 128), F32),
            pltpu.VMEM((2, 3, n, 128), BF16),
            pltpu.SemaphoreType.DMA((2, 3)),
        ],
        compiler_params=params(),
        cost_estimate=cost(5 * 2 * H * n * n * HD * 0.6, 2 * n * 8 * D, H * n * n * 0.6),
        name="attention_back",
    )(lens, qkv, qkv, qkv, attended, dout, stats)


def start_mlp_weights(ids, w_hbm, wp, wu, wd, sem):
    if len(w_hbm) == 3:
        place_halves(w_hbm[0], wp, sem.at[0])
        place_halves(w_hbm[1], wu, sem.at[1])
    else:
        up = (0, FF // 2, wu, sem.at[1])
        place_pieces(ids, w_hbm[:-1], False, [(FF // 2, D // 2, wp, sem.at[0]), up])
    place_halves(w_hbm[-1], wd, sem.at[2])


def mlp_kernel(
    parts, ids, x_ref, att_ref, pb_ref, g_ref, b_ref, ub_ref, db_ref, *rest
):
    w_hbm = rest[:parts]
    mid_ref, out_ref, hid_ref, slope_ref, act_ref, wp, wu, wd, sem = rest[parts:]
    step = pl.program_id(0)

    @pl.when(step == 0)
    def _():
        start_mlp_weights(ids, w_hbm, wp, wu, wd, sem)
        whole(wp, sem.at[0]).wait()

    middle = x_ref[...].astype(F32) + BETA * (mm(att_ref[...], wp[...]) + pb_ref[...])
    mid_ref[...] = middle
    normed, _ = norm_parts(middle)
    act = (normed * g_ref[...] + b_ref[...]).astype(BF16)
    act_ref[...] = act

    @pl.when(step == 0)
    def _():
        whole(wu, sem.at[1]).wait()
        whole(wd, sem.at[2]).wait()

    chunk = 768
    branch = jnp.zeros(middle.shape, F32)
    for f in range(FF // chunk):
        cols = pl.ds(f * chunk, chunk)
        u = mm(act, wu[:, cols]) + ub_ref[:, cols]
        u2 = u * u
        half_t = 0.5 * jnp.tanh(u * (TANH_ROOT + (TANH_ROOT * TANH_CUBIC) * u2))
        gate = 0.5 + half_t
        hidden = (u * gate).astype(BF16)
        hid_ref[:, cols] = hidden
        branch = branch + mm(hidden, wd[cols, :])
        slope = gate + u * (0.5 - 2.0 * half_t * half_t) * (
            TANH_ROOT + (3.0 * TANH_ROOT * TANH_CUBIC) * u2
        )
        slope_ref[:, cols] = slope.astype(BF16)
    out_ref[...] = (middle + BETA * (branch + db_ref[...])).astype(BF16)


MLP_SCRATCH = [
    pltpu.VMEM((D, D), BF16),
    pltpu.VMEM((D, FF), BF16),
    pltpu.VMEM((FF, D), BF16),
    pltpu.SemaphoreType.DMA((3,)),
]


def mlp(ids, x, att, pb, gain, bias, ub, db, w):
    n = x.shape[0]
    tile = BLK
    row = lambda w: pl.BlockSpec((tile, w), lambda i: (i, 0))
    vec = lambda w: pl.BlockSpec((1, w), lambda i: (0, 0))
    sds = jax.ShapeDtypeStruct
    return pl.pallas_call(
        functools.partial(mlp_kernel, len(w)),
        grid=(n // tile,),
        in_specs=[pl.BlockSpec(memory_space=pltpu.SMEM)]
        + [row(D), row(D), vec(D), vec(D), vec(D), vec(FF), vec(D)]
        + [pl.BlockSpec(memory_space=pl.ANY)] * len(w),
        out_specs=[row(D), row(D), row(FF), row(FF), row(D)],
        out_shape=[
            sds((n, D), F32), sds((n, D), BF16), sds((n, FF), BF16), sds((n, FF), BF16),
            sds((n, D), BF16),
        ],
        scratch_shapes=MLP_SCRATCH,
        compiler_params=params(),
        cost_estimate=cost(2 * n * (2 * D * FF + D * D), 2 * n * (7 * D + 2 * FF), n * FF),
        name="mlp",
    )(ids, x, att, pb, gain, bias, ub, db, *w)


def mlp_back_kernel(parts, ids, c_ref, mid_ref, slope_ref, g_ref, *rest):
    w_hbm = rest[:parts]
    du_ref, dm_ref, dy_ref, do_ref, vec_ref, uvec_ref, wp, wu, wd, sem = rest[parts:]
    step = pl.program_id(0)

    @pl.when(step == 0)
    def _():
        start_mlp_weights(ids, w_hbm, wp, wu, wd, sem)
        vec_ref[...] = jnp.zeros_like(vec_ref)
        uvec_ref[...] = jnp.zeros_like(uvec_ref)

    grad_out = c_ref[...].astype(F32)
    dz = (BETA * grad_out).astype(BF16)
    normed, inverse = norm_parts(mid_ref[...])

    @pl.when(step == 0)
    def _():
        whole(wd, sem.at[2]).wait()
        whole(wu, sem.at[1]).wait()
        whole(wp, sem.at[0]).wait()

    chunk = 768
    da = jnp.zeros(normed.shape, F32)
    for f in range(FF // chunk):
        cols = pl.ds(f * chunk, chunk)
        du = (mm(dz, wd[cols, :], NT) * slope_ref[:, cols].astype(F32)).astype(BF16)
        du_ref[:, cols] = du
        uvec_ref[0:1, cols] += jnp.sum(du.astype(F32), axis=0, keepdims=True)
        da = da + mm(du, wu[:, cols], NT)
    dm = grad_out + norm_back(da, normed, inverse, g_ref[...])
    dm_ref[...] = dm
    dy = (BETA * dm).astype(BF16)
    dy_ref[...] = dy
    do_ref[...] = mm(dy, wp[...], NT).astype(BF16)
    vec_ref[0:1, :] += jnp.sum(da * normed, axis=0, keepdims=True)
    vec_ref[1:2, :] += jnp.sum(da, axis=0, keepdims=True)
    vec_ref[2:3, :] += jnp.sum(dy.astype(F32), axis=0, keepdims=True)
    vec_ref[3:4, :] += jnp.sum(dz.astype(F32), axis=0, keepdims=True)


def mlp_back(ids, c, middle, slope, gain, w):
    n = c.shape[0]
    tile = BLK
    const = lambda i: (0, 0)
    row = lambda w: pl.BlockSpec((tile, w), lambda i: (i, 0))
    sds = jax.ShapeDtypeStruct
    return pl.pallas_call(
        functools.partial(mlp_back_kernel, len(w)),
        grid=(n // tile,),
        in_specs=[pl.BlockSpec(memory_space=pltpu.SMEM)]
        + [row(D), row(D), row(FF), pl.BlockSpec((1, D), const)]
        + [pl.BlockSpec(memory_space=pl.ANY)] * len(w),
        out_specs=[
            row(FF), row(D), row(D), row(D), pl.BlockSpec((8, D), const), pl.BlockSpec((8, FF), const),
        ],
        out_shape=[
            sds((n, FF), BF16), sds((n, D), F32), sds((n, D), BF16), sds((n, D), BF16),
            sds((8, D), F32), sds((8, FF), F32),
        ],
        scratch_shapes=MLP_SCRATCH,
        compiler_params=params(),
        cost_estimate=cost(2 * n * (2 * D * FF + D * D), 2 * n * (7 * D + 2 * FF), n * FF),
        name="mlp_back",
    )(ids, c, middle, slope, gain, *w)


def store_sides(row, r, mine, theirs):
    width = r.shape[1] // 2

    @pl.when(row == 0)
    def _():
        mine[...] = r[:, :width].astype(BF16)
        theirs[...] = r[:, width:].astype(BF16)

    @pl.when(row == 1)
    def _():
        theirs[...] = r[:, :width].astype(BF16)
        mine[...] = r[:, width:].astype(BF16)


def down_outer_kernel(ids, a_ref, c_ref, mine, theirs, dz):
    @pl.when(pl.program_id(0) == 0)
    def _():
        dz[...] = (BETA * c_ref[...].astype(F32)).astype(BF16)

    store_sides(ids[2], mm(a_ref[...], dz[...], TN), mine, theirs)


def down_outer(ids, hidden, c):
    n = hidden.shape[0]
    half = pl.BlockSpec((D, D // 2), lambda i, s: (i, 0))
    return pl.pallas_call(
        down_outer_kernel,
        grid_spec=pltpu.PrefetchScalarGridSpec(
            num_scalar_prefetch=1,
            grid=(FF // D,),
            in_specs=[
                pl.BlockSpec((n, D), lambda i, s: (0, i)),
                pl.BlockSpec((n, D), lambda i, s: (0, 0)),
            ],
            out_specs=[half, half],
            scratch_shapes=[pltpu.VMEM((n, D), BF16)],
        ),
        out_shape=[jax.ShapeDtypeStruct((FF, D // 2), BF16)] * 2,
        compiler_params=params(),
        cost_estimate=cost(2 * n * FF * D, 2 * (n * (FF + D) + FF * D)),
        name="down_outer",
    )(ids, hidden, c)


def up_outer_kernel(act_ref, du_ref, att_ref, dy_ref, o_ref):
    o_ref[0, :, : FF // 4] = mm(act_ref[...], du_ref[:, : FF // 4], TN).astype(BF16)
    o_ref[0, :, FF // 4 : FF // 2] = mm(act_ref[...], du_ref[:, FF // 4 :], TN).astype(BF16)
    o_ref[0, :, FF // 2 :] = mm(att_ref[...], dy_ref[...], TN).astype(BF16)


def up_outer(act, du, attended, dy):
    n = act.shape[0]
    width = (FF + D) // 2
    once = pl.BlockSpec((n, D), lambda i: (0, 0))
    half = lambda w: pl.BlockSpec((n, w), lambda i: (0, i))
    return pl.pallas_call(
        up_outer_kernel,
        grid=(2,),
        in_specs=[once, half(FF // 2), once, half(D // 2)],
        out_specs=pl.BlockSpec((1, D, width), lambda i: (i, 0, 0)),
        out_shape=jax.ShapeDtypeStruct((2, D, width), BF16),
        compiler_params=params(),
        cost_estimate=cost(2 * n * D * 2 * width, 2 * (n * (FF + 3 * D) + 2 * D * width)),
        name="up_outer",
    )(act, du, attended, dy)


def qkv_outer_kernel(ids, act_ref, dqkv_ref, mine, theirs):
    step = pl.program_id(0)
    r = mm(act_ref[...], dqkv_ref[...], TN).astype(BF16)

    @pl.when(step == 0)
    def _():
        theirs[...] = r

    @pl.when(step == 1)
    def _():
        mine[...] = r


def qkv_outer(ids, act, dqkv):
    n = act.shape[0]
    width = 3 * D // 2
    out = pl.BlockSpec((D, width), lambda i, s: (0, 0))
    return pl.pallas_call(
        qkv_outer_kernel,
        grid_spec=pltpu.PrefetchScalarGridSpec(
            num_scalar_prefetch=1,
            grid=(2,),
            in_specs=[
                pl.BlockSpec((n, D), lambda i, s: (0, 0)),
                pl.BlockSpec((n, width), lambda i, s: (0, (i + 1 - s[2]) % 2)),
            ],
            out_specs=[out, out],
        ),
        out_shape=[jax.ShapeDtypeStruct((D, width), BF16)] * 2,
        compiler_params=params(),
        cost_estimate=cost(2 * n * D * 2 * width, 2 * (n * (D + 2 * width) + 2 * D * width)),
        name="qkv_outer",
    )(ids, act, dqkv)


def merge_kernel(quad_first, rows, ids, mine, theirs, *outs):
    for block, o in enumerate(outs):
        for slot in range(o.shape[0]):
            e, d = (block, slot) if quad_first else (slot, block)
            shard = (ids[1] ^ e) * QUAD + (ids[0] ^ d)
            here = pl.ds(pl.multiple_of(shard * rows, 16), rows)
            o[slot] = (mine[here, :].astype(F32) + theirs[here, :].astype(F32)).astype(BF16)


def merge(ids, mine, theirs, quad_first, name):
    left, width = mine.shape
    rows = left // (4 * QUAD)
    spec = pl.BlockSpec(memory_space=pltpu.VMEM)
    return pl.pallas_call(
        functools.partial(merge_kernel, quad_first, rows),
        in_specs=[pl.BlockSpec(memory_space=pltpu.SMEM), spec, spec],
        out_shape=[jax.ShapeDtypeStruct((4, rows, width), BF16)] * 4,
        compiler_params=params(),
        cost_estimate=cost(2 * mine.size, 6 * mine.size),
        name=name,
    )(ids, mine, theirs)


def add_quad_kernel(ids, a, b, c, d, *outs):
    for e in range(a.shape[0]):
        total = (a[e].astype(F32) + b[e].astype(F32)) + (c[e].astype(F32) + d[e].astype(F32))
        if len(outs) == 1:
            outs[0][ids[1] ^ e] = total.astype(BF16)
        else:
            outs[e][...] = total.astype(BF16)


def add_quad(ids, parts, apart, name):
    block = parts[0].shape
    sds = jax.ShapeDtypeStruct
    spec = pl.BlockSpec(memory_space=pltpu.VMEM)
    return pl.pallas_call(
        add_quad_kernel,
        in_specs=[pl.BlockSpec(memory_space=pltpu.SMEM)] + [spec] * 4,
        out_shape=[sds(block[1:], BF16)] * block[0] if apart else sds(block, BF16),
        compiler_params=params(),
        cost_estimate=cost(4 * parts[0].size, 10 * parts[0].size),
        name=name,
    )(ids, *parts)


def input_grad_kernel(parts, ids, x_ref, dm_ref, g_ref, dqkv_ref, *rest):
    w_hbm, (o_ref, vec_ref, w, sem) = rest[:parts], rest[parts:]
    first = pl.program_id(0) == 0

    @pl.when(first)
    def _():
        place(ids, w_hbm, w, sem)
        vec_ref[...] = jnp.zeros_like(vec_ref)
        whole(w, sem).wait()

    dqkv = dqkv_ref[...]
    da = mm(dqkv, w[...], NT)
    normed, inverse = norm_parts(x_ref[...].astype(F32))
    o_ref[...] = (dm_ref[...] + norm_back(da, normed, inverse, g_ref[...])).astype(BF16)
    vec_ref[0:1, 0:D] += jnp.sum(da * normed, axis=0, keepdims=True)
    vec_ref[1:2, 0:D] += jnp.sum(da, axis=0, keepdims=True)
    vec_ref[2:3, :] += jnp.sum(dqkv.astype(F32), axis=0, keepdims=True)


def input_grad(ids, x, dm, gain, dqkv, w):
    n = x.shape[0]
    tile = BLK
    const = lambda i: (0, 0)
    row = lambda wide: pl.BlockSpec((tile, wide), lambda i: (i, 0))
    return pl.pallas_call(
        functools.partial(input_grad_kernel, len(w)),
        grid=(n // tile,),
        in_specs=[pl.BlockSpec(memory_space=pltpu.SMEM), row(D), row(D), pl.BlockSpec((1, D), const), row(3 * D)]
        + [pl.BlockSpec(memory_space=pl.ANY)] * len(w),
        out_specs=[row(D), pl.BlockSpec((8, 3 * D), const)],
        out_shape=[jax.ShapeDtypeStruct((n, D), BF16), jax.ShapeDtypeStruct((8, 3 * D), F32)],
        scratch_shapes=[pltpu.VMEM((D, 3 * D), BF16), pltpu.SemaphoreType.DMA],
        compiler_params=params(),
        cost_estimate=cost(2 * n * D * 3 * D, 2 * (n * 7 * D + 3 * D * D)),
        name="input_grad",
    )(ids, x, dm, gain, dqkv, *w)


def swap(block, axis, distance):
    count = lax.axis_size(axis)
    return lax.ppermute(block, axis, [(i, i ^ distance) for i in range(count)])


def quad_swap(pieces):
    count = lax.axis_size("tok")
    groups = [list(range(g, g + QUAD)) for g in range(0, count, QUAD)]
    return lax.all_to_all(pieces, "tok", 0, 0, axis_index_groups=groups, tiled=True)


def by_halves(whole):
    over_row, height, cols = whole.shape
    if over_row == 2:
        return whole
    return (
        whole.reshape(2, over_row // 2, height, cols)
        .transpose(0, 2, 1, 3)
        .reshape(2, height, over_row // 2 * cols)
    )


def gather(shard):
    rows, cols = shard.shape
    whole = lax.all_gather(shard, ("row", "tok"), axis=0, tiled=True)
    return by_halves(whole.reshape(lax.axis_size("row"), rows * lax.axis_size("tok"), cols))


def gather_line(shard):
    return jnp.stack([shard] + [swap(shard, "tok", QUAD * e) for e in range(1, 4)])


def spread(block, steps):
    return [block] + [swap(block, "tok", step) for step in steps]


def with_partner(blocks):
    return blocks + [swap(t, "row", 1) for t in blocks]


QUAD_STEPS = (1, 2, 3)
LINE_STEPS = (QUAD, 2 * QUAD, 3 * QUAD)


def after(value, *others):
    return lax.optimization_barrier((value,) + others)[0]


def from_peers(blocks, steps):
    return [blocks[0]] + [swap(t, "tok", step) for t, step in zip(blocks[1:], steps)]


def line_swap(pieces):
    count = lax.axis_size("tok")
    groups = [list(range(q, count, QUAD)) for q in range(QUAD)]
    return lax.all_to_all(pieces, "tok", 0, 0, axis_index_groups=groups, tiled=True)


def total_of(terms):
    return sum([t.astype(F32) for t in terms[1:]], terms[0].astype(F32))


def scatter(halves):
    over_row = lax.axis_size("row")
    _, height, width = halves.shape
    cols = 2 * width // over_row
    if over_row != 2:
        halves = halves.reshape(2, height, over_row // 2, cols).transpose(0, 2, 1, 3)
    flat = halves.reshape(over_row * height, cols)
    return lax.psum_scatter(flat, ("row", "tok"), scatter_dimension=0, tiled=True).astype(F32)


def scatter_sides(sides, row_index):
    flat = jnp.stack(sides)
    return scatter(jnp.where(row_index % 2 == 0, flat, flat[::-1]))


def all_sum(block, steps):
    for step in steps:
        block = block + (swap(block, "tok", step) if step else swap(block, "row", 1))
    return block


def per_device(
    tokens,
    out_grad,
    doc_lengths,
    first_gain,
    first_bias,
    qkv_weight,
    query_bias,
    value_bias,
    proj_weight,
    proj_bias,
    second_gain,
    second_bias,
    up_weight,
    up_bias,
    down_weight,
    down_bias,
):
    row_count, piece_len, width = tokens.shape
    n = row_count * piece_len
    tok_index = lax.axis_index("tok")
    row_index = lax.axis_index("row")
    groups = lax.axis_size("tok") // QUAD
    by_permutes = lax.axis_size("row") == 2 and groups == 4
    ids = jnp.stack([tok_index % QUAD, tok_index // QUAD, row_index % 2]).astype(jnp.int32)
    lens = lax.dynamic_slice(
        doc_lengths,
        (tok_index % QUAD, tok_index // QUAD, 0),
        (1, 1, doc_lengths.shape[2]),
    )[0]

    qkv_bias = jnp.concatenate([query_bias, jnp.zeros_like(query_bias), value_bias])[None]
    first_gain, first_bias = first_gain[None], first_bias[None]
    down_full = gather(down_weight)
    x = quad_swap(tokens).reshape(n, width)
    if by_permutes:
        qkv_line = gather_line(qkv_weight)
        up_weights = jnp.concatenate([up_weight, proj_weight], axis=1)
        up_weights = after(up_weights, qkv_line)
        qkv_line, x, ids, lens, qkv_bias, first_gain, first_bias = lax.optimization_barrier(
            (qkv_line, x, ids, lens, qkv_bias, first_gain, first_bias)
        )
        up_line = gather_line(up_weights)
        qkv_pieces = spread(qkv_line, QUAD_STEPS)
        qkv_full = with_partner(qkv_pieces)
        up_pieces = spread(after(up_line, *qkv_pieces), QUAD_STEPS)
        others = []
    else:
        qkv_full = [gather(qkv_weight)]
        others = [gather(proj_weight), gather(up_weight), down_full]
    act1, qkv = norm_qkv(ids, x, first_gain, first_bias, qkv_bias, qkv_full)
    attended, stats = attention(lens, qkv)
    if by_permutes:
        up_pieces = list(lax.optimization_barrier((attended, *up_pieces))[1:])
        others = with_partner(up_pieces) + [down_full]
    c = quad_swap(after(out_grad, attended, *others)).reshape(n, width)
    middle, out, hidden, slope, act2 = mlp(
        ids, x, attended, proj_bias[None], second_gain[None], second_bias[None],
        up_bias[None], down_bias[None], others,
    )
    output = quad_swap(after(out, c).reshape(row_count, piece_len, width))
    du, dm, dy, dout, vecs, uvec = mlp_back(ids, c, middle, slope, second_gain[None], others)
    up_outer_grad = up_outer(after(act2, output), du, attended, dy)
    down_sides = down_outer(ids, after(hidden, up_outer_grad), c)
    if by_permutes:
        down_blocks = merge(ids, down_sides[0], swap(down_sides[1], "row", 1), False, "down_merge")
        dout = after(dout, *down_blocks)
    dqkv = attention_back(lens, qkv, attended, dout, stats)
    if by_permutes:
        up_proj = scatter(up_outer_grad)
        up_grad, proj_grad = up_proj[:, : FF // 2], up_proj[:, FF // 2 :]
        down_got = from_peers(down_blocks, QUAD_STEPS)
        act1 = after(act1, *down_got[1:])
    qkv_sides = qkv_outer(ids, act1, dqkv)
    if by_permutes:
        down_got[0] = after(down_got[0], *qkv_sides)
        down_line = add_quad(ids, down_got, False, "down_add")
        qkv_mine = after(qkv_sides[0], down_line)
        down_line = line_swap(down_line)
        qkv_blocks = merge(ids, qkv_mine, swap(qkv_sides[1], "row", 1), False, "qkv_merge")
        dqkv = after(dqkv, *qkv_blocks)
        qkv_got = from_peers(qkv_blocks, QUAD_STEPS)
        qkv_got[0] = after(qkv_got[0], down_line)
        qkv_shards = add_quad(ids, qkv_got, True, "qkv_add")
        qkv_grad = total_of(from_peers(qkv_shards, LINE_STEPS))
        down_grad = total_of([down_line[e] for e in range(groups)])
    else:
        down_grad = scatter_sides(down_sides, row_index)
        up_grad = scatter(up_outer_grad[:, :, : FF // 2])
        proj_grad = scatter(up_outer_grad[:, :, FF // 2 :])
        qkv_grad = scatter_sides(qkv_sides, row_index)
    dx, vecs1 = input_grad(ids, x, dm, first_gain, dqkv, qkv_full)
    tokens_grad = quad_swap(dx.reshape(row_count, piece_len, width))
    packed = jnp.concatenate(
        [
            vecs1[0, :D], vecs1[1, :D], vecs1[2, :D], vecs1[2, 2 * D :], vecs[2], vecs[0], vecs[1],
            vecs[3], uvec[0],
        ]
    ).reshape(-1, 128)
    if by_permutes:
        packed = all_sum(after(packed, *qkv_got[1:]), (0, 1, 2))
        total = all_sum(after(packed, tokens_grad), LINE_STEPS[:2]).reshape(-1)
    else:
        total = lax.psum(packed, ("tok", "row")).reshape(-1)
    v = [total[i * D : (i + 1) * D] for i in range(8)]
    return (
        output, tokens_grad, qkv_grad, proj_grad, up_grad, down_grad,
        v[0], v[1], v[2], v[3], v[4], v[5], v[6], total[8 * D :], v[7],
    )


def solution(mesh):
    rows = P("row", "tok", None)
    weight = P("tok", "row")
    in_specs = (
        rows, rows, P("row", None, None), P(), P(), weight, P(), P(), weight, P(), P(), P(),
        weight, P(), weight, P(),
    )
    out_specs = (rows, rows, weight, weight, weight, weight) + (P(),) * 9
    return jax.shard_map(
        per_device, mesh=mesh, in_specs=in_specs, out_specs=out_specs, check_vma=False
    )
```

```python
import functools
import math

import jax
import jax.numpy as jnp
from jax import lax
from jax.experimental import pallas as pl
from jax.experimental.pallas import tpu as pltpu
from jax.sharding import PartitionSpec as P

D = 768
H = 12
HD = 64
FF = 3072
DEPTH = 48
DOCS = 8
BLK = 256
QUAD = 4

EPSILON = 1e-05
MASKED = -1e9
TANH_ROOT = 0.7978845608028654
TANH_CUBIC = 0.044715
BETA = 1.0 / math.sqrt(DEPTH)
SCALE = 1.0 / math.sqrt(HD)
F32 = jnp.float32
BF16 = jnp.bfloat16
VMEM_LIMIT = 56 * 2**20
EASE = 8

NT = (((1,), (1,)), ((), ()))
NN = (((1,), (0,)), ((), ()))
TN = (((0,), (0,)), ((), ()))


def mm(a, b, dims=NN):
    return lax.dot_general(a, b, dims, preferred_element_type=F32)


def params():
    return pltpu.CompilerParams(vmem_limit_bytes=VMEM_LIMIT)


def cost(flops, nbytes, trans=0):
    return pl.CostEstimate(
        flops=int(flops // EASE), bytes_accessed=int(nbytes // EASE), transcendentals=int(trans // EASE)
    )


def norm_parts(x):
    centre = x - jnp.mean(x, axis=-1, keepdims=True)
    inverse = lax.rsqrt(jnp.mean(centre * centre, axis=-1, keepdims=True) + EPSILON)
    return centre * inverse, inverse


def norm_back(grad, normed, inverse, gain):
    spread = grad * gain
    return inverse * (
        spread
        - jnp.mean(spread, axis=-1, keepdims=True)
        - normed * jnp.mean(spread * normed, axis=-1, keepdims=True)
    )


def whole(ref, sem):
    return pltpu.make_async_copy(ref, ref, sem)


def place_pieces(ids, pieces, quad_first, targets):
    count = len(pieces) // 2
    for side in range(2):
        for block in range(count):
            ref = pieces[side * count + block]
            for slot in range(ref.shape[0]):
                d, e = (slot, block) if quad_first else (block, slot)
                shard = (ids[1] ^ e) * QUAD + (ids[0] ^ d)
                rows = ref.shape[1]
                here = pl.ds(pl.multiple_of(shard * rows, 16), rows)
                for at, lanes, w, sem in targets:
                    there = pl.ds(pl.multiple_of((ids[2] ^ side) * lanes, 128), lanes)
                    src = ref.at[slot, :, pl.ds(at, lanes)]
                    pltpu.make_async_copy(src, w.at[here, there], sem).start()


def place_halves(halves, w, sem):
    cols = halves.shape[2]
    for h in range(2):
        pltpu.make_async_copy(halves.at[h], w.at[:, pl.ds(h * cols, cols)], sem).start()


def place(ids, parts, w, sem):
    if len(parts) == 1:
        place_halves(parts[0], w, sem)
    else:
        place_pieces(ids, parts, False, [(0, parts[0].shape[2], w, sem)])


def qkv_kernel(parts, ids, x_ref, g_ref, b_ref, qb_ref, *rest):
    w_hbm, (act_ref, qkv_ref, w_vmem, sem) = rest[:parts], rest[parts:]
    first = pl.program_id(0) == 0

    @pl.when(first)
    def _():
        place(ids, w_hbm, w_vmem, sem)

    normed, _ = norm_parts(x_ref[...].astype(F32))
    act = (normed * g_ref[...] + b_ref[...]).astype(BF16)
    act_ref[...] = act

    @pl.when(first)
    def _():
        whole(w_vmem, sem).wait()

    qkv_ref[...] = (mm(act, w_vmem[...]) + qb_ref[...]).astype(BF16)


def norm_qkv(ids, x, gain, bias, qkv_bias, w):
    n = x.shape[0]
    tile = BLK
    const = lambda i: (0, 0)
    return pl.pallas_call(
        functools.partial(qkv_kernel, len(w)),
        grid=(n // tile,),
        in_specs=[
            pl.BlockSpec(memory_space=pltpu.SMEM),
            pl.BlockSpec((tile, D), lambda i: (i, 0)),
            pl.BlockSpec((1, D), const),
            pl.BlockSpec((1, D), const),
            pl.BlockSpec((1, 3 * D), const),
        ]
        + [pl.BlockSpec(memory_space=pl.ANY)] * len(w),
        out_specs=[
            pl.BlockSpec((tile, D), lambda i: (i, 0)),
            pl.BlockSpec((tile, 3 * D), lambda i: (i, 0)),
        ],
        out_shape=[
            jax.ShapeDtypeStruct((n, D), BF16),
            jax.ShapeDtypeStruct((n, 3 * D), BF16),
        ],
        scratch_shapes=[pltpu.VMEM((D, 3 * D), BF16), pltpu.SemaphoreType.DMA],
        compiler_params=params(),
        cost_estimate=cost(2 * n * D * 3 * D, 2 * (n * 5 * D + 3 * D * D)),
        name="norm_qkv",
    )(ids, x, gain, bias, qkv_bias, *w)


def first_of_doc(lens_ref, positions):
    start = jnp.zeros_like(positions)
    end = 0
    for d in range(DOCS):
        end = end + lens_ref[0, d]
        start = jnp.where(positions >= end, end, start)
    return start


def lane_half(h):
    lane = lax.broadcasted_iota(jnp.int32, (1, 128), 1)
    return (lane >= h * HD) & (lane < (h + 1) * HD)


WINDOW = 2


def mask(lens_ref, keys_at, keys, queries_at, queries):
    qpos = lax.broadcasted_iota(jnp.int32, (1, queries), 1) + queries_at
    kpos = lax.broadcasted_iota(jnp.int32, (keys, 1), 0) + keys_at
    return jnp.where((kpos >= first_of_doc(lens_ref, qpos)) & (kpos <= qpos), 0.0, MASKED)


def attn_kernel(lens_ref, q_ref, k_ref, v_ref, o_ref, l_ref, mask_ref):
    pair = pl.program_id(0)
    blocks = []
    for i in range(q_ref.shape[0] // BLK):
        low = max(0, i - WINDOW)
        blocks.append((low * BLK, (i + 1 - low) * BLK, i * BLK))

    @pl.when(pair == 0)
    def _():
        l_ref[...] = jnp.zeros_like(l_ref)
        for first, count, at in blocks:
            mask_ref[0:count, at : at + BLK] = mask(lens_ref, first, count, at, BLK)

    for first, count, at in blocks:
        rows = slice(at, at + BLK)
        q = q_ref[rows, :] * jnp.asarray(SCALE, BF16)
        k = k_ref[first : first + count, :]
        v = v_ref[first : first + count, :]
        out = None
        for h in range(2):
            half = lane_half(h)
            s = mm(k, jnp.where(half, q, jnp.zeros_like(q)), NT) + mask_ref[0:count, rows]
            m = jnp.max(s, axis=0, keepdims=True)
            p = jnp.exp(s - m)
            total = jnp.sum(p, axis=0, keepdims=True)
            probs = (p * (1.0 / total)).astype(BF16)
            o = mm(probs, jnp.where(half, v, jnp.zeros_like(v)), TN)
            out = o if out is None else out + o
            l_ref[pl.ds(2 * pair + h, 1), rows] = m + jnp.log(total)
        o_ref[rows, :] = out.astype(BF16)


def attention(lens, qkv):
    n = qkv.shape[0]
    pairs = H // 2
    spec = lambda w: pl.BlockSpec((n, 128), lambda p: (0, w * pairs + p))
    return pl.pallas_call(
        attn_kernel,
        grid=(pairs,),
        in_specs=[pl.BlockSpec(memory_space=pltpu.SMEM), spec(0), spec(1), spec(2)],
        out_specs=[
            pl.BlockSpec((n, 128), lambda p: (0, p)),
            pl.BlockSpec((16, n), lambda p: (0, 0)),
        ],
        out_shape=[jax.ShapeDtypeStruct((n, D), BF16), jax.ShapeDtypeStruct((16, n), F32)],
        scratch_shapes=[pltpu.VMEM(((WINDOW + 1) * BLK, n), F32)],
        compiler_params=params(),
        cost_estimate=cost(2 * 2 * H * n * n * HD * 0.6, 2 * n * 4 * D, H * n * n * 0.6),
        name="attention",
    )(lens, qkv, qkv, qkv)


def attn_back_kernel(
    lens_ref, q_ref, k_ref, v_ref, o_ref, do_ref, l_ref, out_hbm, mask_ref, dq_acc, bufs, sems
):
    pair = pl.program_id(0)
    pairs = pl.num_programs(0)
    n = q_ref.shape[0]
    slot = pair % 2
    blocks = [(at, min((WINDOW + 1) * BLK, n - at)) for at in range(0, n, BLK)]

    def copies(p, at):
        return [
            pltpu.make_async_copy(
                bufs.at[at, w],
                out_hbm.at[:, pl.ds(pl.multiple_of(w * D + p * 128, 128), 128)],
                sems.at[at, w],
            )
            for w in range(3)
        ]

    @pl.when(pair == 0)
    def _():
        for at, count in blocks:
            mask_ref[at : at + BLK, 0:count] = mask(lens_ref, at, BLK, at, count)

    @pl.when(pair >= 2)
    def _():
        for c in copies(pair - 2, slot):
            c.wait()

    prod = (o_ref[...].astype(F32) * do_ref[...].astype(F32)).T
    dq_acc[...] = jnp.zeros_like(dq_acc)
    for at, count in blocks:
        keys = slice(at, at + BLK)
        queries = slice(at, at + count)
        k = k_ref[keys, :]
        v = v_ref[keys, :]
        q = q_ref[queries, :] * jnp.asarray(SCALE, BF16)
        do = do_ref[queries, :]
        dk = dv = None
        for h in range(2):
            half = lane_half(h)
            inner = jnp.sum(prod[h * HD : (h + 1) * HD, queries], axis=0, keepdims=True)
            logs = l_ref[pl.ds(2 * pair + h, 1), queries]
            qh = jnp.where(half, q, jnp.zeros_like(q))
            doh = jnp.where(half, do, jnp.zeros_like(do))
            kh = jnp.where(half, k, jnp.zeros_like(k))
            p = jnp.exp(mm(k, qh, NT) + (mask_ref[keys, 0:count] - logs))
            ds = (p * (mm(v, doh, NT) - inner)).astype(BF16)
            dvh = mm(p.astype(BF16), doh)
            dkh = mm(ds, qh)
            dv, dk = (dvh, dkh) if h == 0 else (dv + dvh, dk + dkh)
            dq_acc[queries, :] += mm(ds, kh, TN)
        bufs[slot, 1, keys, :] = dk.astype(BF16)
        bufs[slot, 2, keys, :] = dv.astype(BF16)
    bufs[slot, 0] = (dq_acc[...] * SCALE).astype(BF16)
    for c in copies(pair, slot):
        c.start()

    @pl.when(pair == pairs - 1)
    def _():
        for c in copies(pair - 1, 1 - slot) + copies(pair, slot):
            c.wait()


def attention_back(lens, qkv, attended, dout, stats):
    n = qkv.shape[0]
    pairs = H // 2
    spec = lambda w: pl.BlockSpec((n, 128), lambda p: (0, w * pairs + p))
    one = pl.BlockSpec((n, 128), lambda p: (0, p))
    return pl.pallas_call(
        attn_back_kernel,
        grid=(pairs,),
        in_specs=[
            pl.BlockSpec(memory_space=pltpu.SMEM), spec(0), spec(1), spec(2), one, one,
            pl.BlockSpec((16, n), lambda p: (0, 0)),
        ],
        out_specs=pl.BlockSpec(memory_space=pl.ANY),
        out_shape=jax.ShapeDtypeStruct((n, 3 * D), BF16),
        scratch_shapes=[
            pltpu.VMEM((n, (WINDOW + 1) * BLK), F32),
            pltpu.VMEM((n, 128), F32),
            pltpu.VMEM((2, 3, n, 128), BF16),
            pltpu.SemaphoreType.DMA((2, 3)),
        ],
        compiler_params=params(),
        cost_estimate=cost(5 * 2 * H * n * n * HD * 0.6, 2 * n * 8 * D, H * n * n * 0.6),
        name="attention_back",
    )(lens, qkv, qkv, qkv, attended, dout, stats)


def start_mlp_weights(ids, w_hbm, wp, wu, wd, sem):
    if len(w_hbm) == 3:
        for i, w in enumerate((wp, wu, wd)):
            place_halves(w_hbm[i], w, sem.at[i])
        return
    packed = w_hbm[-1]
    _, count, _, lanes = packed.shape

    def body(t, carry):
        for w, i, at, rows in ((wp, 0, FF // count, D // count), (wd, 2, 0, FF // count)):
            here = pl.ds(pl.multiple_of(t * rows, 16), rows)
            for h in range(2):
                src = packed.at[h, t, pl.ds(at, rows), :]
                pltpu.make_async_copy(src, w.at[here, pl.ds(h * lanes, lanes)], sem.at[i]).start()
        return carry

    lax.fori_loop(0, count, body, 0)
    place_pieces(ids, w_hbm[:-1], False, [(0, FF // 2, wu, sem.at[1])])


def mlp_kernel(
    parts, ids, x_ref, att_ref, pb_ref, g_ref, b_ref, ub_ref, db_ref, *rest
):
    w_hbm = rest[:parts]
    mid_ref, out_ref, hid_ref, slope_ref, act_ref, wp, wu, wd, sem = rest[parts:]
    step = pl.program_id(0)

    @pl.when(step == 0)
    def _():
        start_mlp_weights(ids, w_hbm, wp, wu, wd, sem)
        whole(wp, sem.at[0]).wait()

    middle = x_ref[...].astype(F32) + BETA * (mm(att_ref[...], wp[...]) + pb_ref[...])
    mid_ref[...] = middle
    normed, _ = norm_parts(middle)
    act = (normed * g_ref[...] + b_ref[...]).astype(BF16)
    act_ref[...] = act

    @pl.when(step == 0)
    def _():
        whole(wu, sem.at[1]).wait()
        whole(wd, sem.at[2]).wait()

    chunk = 768
    branch = jnp.zeros(middle.shape, F32)
    for f in range(FF // chunk):
        cols = pl.ds(f * chunk, chunk)
        u = mm(act, wu[:, cols]) + ub_ref[:, cols]
        u2 = u * u
        gate = 0.5 + 0.5 * jnp.tanh(u * (TANH_ROOT + (TANH_ROOT * TANH_CUBIC) * u2))
        value = u * gate
        hidden = value.astype(BF16)
        hid_ref[:, cols] = hidden
        branch = branch + mm(hidden, wd[cols, :])
        slope = gate + value * (1.0 - gate) * (
            2.0 * TANH_ROOT + (6.0 * TANH_ROOT * TANH_CUBIC) * u2
        )
        slope_ref[:, cols] = slope.astype(BF16)
    out_ref[...] = (middle + BETA * (branch + db_ref[...])).astype(BF16)


MLP_SCRATCH = [
    pltpu.VMEM((D, D), BF16),
    pltpu.VMEM((D, FF), BF16),
    pltpu.VMEM((FF, D), BF16),
    pltpu.SemaphoreType.DMA((3,)),
]


def mlp(ids, x, att, pb, gain, bias, ub, db, w):
    n = x.shape[0]
    tile = BLK
    row = lambda w: pl.BlockSpec((tile, w), lambda i: (i, 0))
    vec = lambda w: pl.BlockSpec((1, w), lambda i: (0, 0))
    sds = jax.ShapeDtypeStruct
    return pl.pallas_call(
        functools.partial(mlp_kernel, len(w)),
        grid=(n // tile,),
        in_specs=[pl.BlockSpec(memory_space=pltpu.SMEM)]
        + [row(D), row(D), vec(D), vec(D), vec(D), vec(FF), vec(D)]
        + [pl.BlockSpec(memory_space=pl.ANY)] * len(w),
        out_specs=[row(D), row(D), row(FF), row(FF), row(D)],
        out_shape=[
            sds((n, D), F32), sds((n, D), BF16), sds((n, FF), BF16), sds((n, FF), BF16),
            sds((n, D), BF16),
        ],
        scratch_shapes=MLP_SCRATCH,
        compiler_params=params(),
        cost_estimate=cost(2 * n * (2 * D * FF + D * D), 2 * n * (7 * D + 2 * FF), n * FF),
        name="mlp",
    )(ids, x, att, pb, gain, bias, ub, db, *w)


def mlp_back_kernel(parts, ids, c_ref, mid_ref, slope_ref, g_ref, *rest):
    w_hbm = rest[:parts]
    du_ref, dm_ref, dy_ref, do_ref, vec_ref, uvec_ref, wp, wu, wd, sem = rest[parts:]
    step = pl.program_id(0)

    @pl.when(step == 0)
    def _():
        start_mlp_weights(ids, w_hbm, wp, wu, wd, sem)
        vec_ref[...] = jnp.zeros_like(vec_ref)
        uvec_ref[...] = jnp.zeros_like(uvec_ref)

    grad_out = c_ref[...].astype(F32)
    dz = (BETA * grad_out).astype(BF16)
    normed, inverse = norm_parts(mid_ref[...])

    @pl.when(step == 0)
    def _():
        whole(wd, sem.at[2]).wait()
        whole(wu, sem.at[1]).wait()
        whole(wp, sem.at[0]).wait()

    chunk = 768
    da = jnp.zeros(normed.shape, F32)
    for f in range(FF // chunk):
        cols = pl.ds(f * chunk, chunk)
        du = (mm(dz, wd[cols, :], NT) * slope_ref[:, cols].astype(F32)).astype(BF16)
        du_ref[:, cols] = du
        uvec_ref[0:1, cols] += jnp.sum(du.astype(F32), axis=0, keepdims=True)
        da = da + mm(du, wu[:, cols], NT)
    dm = grad_out + norm_back(da, normed, inverse, g_ref[...])
    dm_ref[...] = dm
    dy = (BETA * dm).astype(BF16)
    dy_ref[...] = dy
    do_ref[...] = mm(dy, wp[...], NT).astype(BF16)
    vec_ref[0:1, :] += jnp.sum(da * normed, axis=0, keepdims=True)
    vec_ref[1:2, :] += jnp.sum(da, axis=0, keepdims=True)
    vec_ref[2:3, :] += jnp.sum(dy.astype(F32), axis=0, keepdims=True)
    vec_ref[3:4, :] += jnp.sum(dz.astype(F32), axis=0, keepdims=True)


def mlp_back(ids, c, middle, slope, gain, w):
    n = c.shape[0]
    tile = BLK
    const = lambda i: (0, 0)
    row = lambda w: pl.BlockSpec((tile, w), lambda i: (i, 0))
    sds = jax.ShapeDtypeStruct
    return pl.pallas_call(
        functools.partial(mlp_back_kernel, len(w)),
        grid=(n // tile,),
        in_specs=[pl.BlockSpec(memory_space=pltpu.SMEM)]
        + [row(D), row(D), row(FF), pl.BlockSpec((1, D), const)]
        + [pl.BlockSpec(memory_space=pl.ANY)] * len(w),
        out_specs=[
            row(FF), row(D), row(D), row(D), pl.BlockSpec((8, D), const), pl.BlockSpec((8, FF), const),
        ],
        out_shape=[
            sds((n, FF), BF16), sds((n, D), F32), sds((n, D), BF16), sds((n, D), BF16),
            sds((8, D), F32), sds((8, FF), F32),
        ],
        scratch_shapes=MLP_SCRATCH,
        compiler_params=params(),
        cost_estimate=cost(2 * n * (2 * D * FF + D * D), 2 * n * (7 * D + 2 * FF), n * FF),
        name="mlp_back",
    )(ids, c, middle, slope, gain, *w)


def store_sides(row, r, mine, theirs):
    width = r.shape[1] // 2

    @pl.when(row == 0)
    def _():
        mine[...] = r[:, :width].astype(BF16)
        theirs[...] = r[:, width:].astype(BF16)

    @pl.when(row == 1)
    def _():
        theirs[...] = r[:, :width].astype(BF16)
        mine[...] = r[:, width:].astype(BF16)


def down_outer_kernel(ids, a_ref, c_ref, mine, theirs, dz):
    @pl.when(pl.program_id(0) == 0)
    def _():
        dz[...] = (BETA * c_ref[...].astype(F32)).astype(BF16)

    store_sides(ids[2], mm(a_ref[...], dz[...], TN), mine, theirs)


def down_outer(ids, hidden, c):
    n = hidden.shape[0]
    half = pl.BlockSpec((D, D // 2), lambda i, s: (i, 0))
    return pl.pallas_call(
        down_outer_kernel,
        grid_spec=pltpu.PrefetchScalarGridSpec(
            num_scalar_prefetch=1,
            grid=(FF // D,),
            in_specs=[
                pl.BlockSpec((n, D), lambda i, s: (0, i)),
                pl.BlockSpec((n, D), lambda i, s: (0, 0)),
            ],
            out_specs=[half, half],
            scratch_shapes=[pltpu.VMEM((n, D), BF16)],
        ),
        out_shape=[jax.ShapeDtypeStruct((FF, D // 2), BF16)] * 2,
        compiler_params=params(),
        cost_estimate=cost(2 * n * FF * D, 2 * (n * (FF + D) + FF * D)),
        name="down_outer",
    )(ids, hidden, c)


def up_outer_kernel(act_ref, du_ref, att_ref, dy_ref, o_ref):
    o_ref[0, :, : FF // 4] = mm(act_ref[...], du_ref[:, : FF // 4], TN).astype(BF16)
    o_ref[0, :, FF // 4 : FF // 2] = mm(act_ref[...], du_ref[:, FF // 4 :], TN).astype(BF16)
    o_ref[0, :, FF // 2 :] = mm(att_ref[...], dy_ref[...], TN).astype(BF16)


def up_outer(act, du, attended, dy):
    n = act.shape[0]
    width = (FF + D) // 2
    once = pl.BlockSpec((n, D), lambda i: (0, 0))
    half = lambda w: pl.BlockSpec((n, w), lambda i: (0, i))
    return pl.pallas_call(
        up_outer_kernel,
        grid=(2,),
        in_specs=[once, half(FF // 2), once, half(D // 2)],
        out_specs=pl.BlockSpec((1, D, width), lambda i: (i, 0, 0)),
        out_shape=jax.ShapeDtypeStruct((2, D, width), BF16),
        compiler_params=params(),
        cost_estimate=cost(2 * n * D * 2 * width, 2 * (n * (FF + 3 * D) + 2 * D * width)),
        name="up_outer",
    )(act, du, attended, dy)


def qkv_outer_kernel(ids, act_ref, dqkv_ref, mine, theirs):
    step = pl.program_id(0)
    r = mm(act_ref[...], dqkv_ref[...], TN).astype(BF16)

    @pl.when(step == 0)
    def _():
        theirs[...] = r

    @pl.when(step == 1)
    def _():
        mine[...] = r


def qkv_outer(ids, act, dqkv):
    n = act.shape[0]
    width = 3 * D // 2
    out = pl.BlockSpec((D, width), lambda i, s: (0, 0))
    return pl.pallas_call(
        qkv_outer_kernel,
        grid_spec=pltpu.PrefetchScalarGridSpec(
            num_scalar_prefetch=1,
            grid=(2,),
            in_specs=[
                pl.BlockSpec((n, D), lambda i, s: (0, 0)),
                pl.BlockSpec((n, width), lambda i, s: (0, (i + 1 - s[2]) % 2)),
            ],
            out_specs=[out, out],
        ),
        out_shape=[jax.ShapeDtypeStruct((D, width), BF16)] * 2,
        compiler_params=params(),
        cost_estimate=cost(2 * n * D * 2 * width, 2 * (n * (D + 2 * width) + 2 * D * width)),
        name="qkv_outer",
    )(ids, act, dqkv)


def merge_kernel(quad_first, rows, ids, mine, theirs, *outs):
    for block, o in enumerate(outs):
        for slot in range(o.shape[0]):
            e, d = (block, slot) if quad_first else (slot, block)
            shard = (ids[1] ^ e) * QUAD + (ids[0] ^ d)
            here = pl.ds(pl.multiple_of(shard * rows, 16), rows)
            o[slot] = (mine[here, :].astype(F32) + theirs[here, :].astype(F32)).astype(BF16)


def merge(ids, mine, theirs, quad_first, name):
    left, width = mine.shape
    rows = left // (4 * QUAD)
    spec = pl.BlockSpec(memory_space=pltpu.VMEM)
    return pl.pallas_call(
        functools.partial(merge_kernel, quad_first, rows),
        in_specs=[pl.BlockSpec(memory_space=pltpu.SMEM), spec, spec],
        out_shape=[jax.ShapeDtypeStruct((4, rows, width), BF16)] * 4,
        compiler_params=params(),
        cost_estimate=cost(2 * mine.size, 6 * mine.size),
        name=name,
    )(ids, mine, theirs)


def add_quad_kernel(ids, a, b, c, d, *outs):
    for e in range(a.shape[0]):
        total = (a[e].astype(F32) + b[e].astype(F32)) + (c[e].astype(F32) + d[e].astype(F32))
        if len(outs) == 1:
            outs[0][ids[1] ^ e] = total.astype(BF16)
        else:
            outs[e][...] = total.astype(BF16)


def add_quad(ids, parts, apart, name):
    block = parts[0].shape
    sds = jax.ShapeDtypeStruct
    spec = pl.BlockSpec(memory_space=pltpu.VMEM)
    return pl.pallas_call(
        add_quad_kernel,
        in_specs=[pl.BlockSpec(memory_space=pltpu.SMEM)] + [spec] * 4,
        out_shape=[sds(block[1:], BF16)] * block[0] if apart else sds(block, BF16),
        compiler_params=params(),
        cost_estimate=cost(4 * parts[0].size, 10 * parts[0].size),
        name=name,
    )(ids, *parts)


def input_grad_kernel(parts, ids, x_ref, dm_ref, g_ref, dqkv_ref, *rest):
    w_hbm, outs, (vec_ref, w, sem) = rest[:parts], rest[parts:-3], rest[-3:]
    step = pl.program_id(0)

    @pl.when(step == 0)
    def _():
        place(ids, w_hbm, w, sem)
        vec_ref[...] = jnp.zeros_like(vec_ref)
        whole(w, sem).wait()

    dqkv = dqkv_ref[...]
    da = mm(dqkv, w[...], NT)
    normed, inverse = norm_parts(x_ref[...].astype(F32))
    dx = (dm_ref[...] + norm_back(da, normed, inverse, g_ref[...])).astype(BF16)
    for d, o in enumerate(outs):

        @pl.when(step == d)
        def _(o=o):
            o[...] = dx

    vec_ref[0:1, 0:D] += jnp.sum(da * normed, axis=0, keepdims=True)
    vec_ref[1:2, 0:D] += jnp.sum(da, axis=0, keepdims=True)
    vec_ref[2:3, :] += jnp.sum(dqkv.astype(F32), axis=0, keepdims=True)


def input_grad(ids, x, dm, gain, dqkv, w):
    n = x.shape[0]
    tile = n // QUAD
    const = lambda i, s: (0, 0)
    row = lambda wide: pl.BlockSpec((tile, wide), lambda i, s: (i ^ s[0], 0))
    return pl.pallas_call(
        functools.partial(input_grad_kernel, len(w)),
        grid_spec=pltpu.PrefetchScalarGridSpec(
            num_scalar_prefetch=1,
            grid=(QUAD,),
            in_specs=[row(D), row(D), pl.BlockSpec((1, D), const), row(3 * D)]
            + [pl.BlockSpec(memory_space=pl.ANY)] * len(w),
            out_specs=[pl.BlockSpec((tile, D), const)] * QUAD + [pl.BlockSpec((8, 3 * D), const)],
            scratch_shapes=[pltpu.VMEM((D, 3 * D), BF16), pltpu.SemaphoreType.DMA],
        ),
        out_shape=[jax.ShapeDtypeStruct((tile, D), BF16)] * QUAD
        + [jax.ShapeDtypeStruct((8, 3 * D), F32)],
        compiler_params=params(),
        cost_estimate=cost(2 * n * D * 3 * D, 2 * (n * 7 * D + 3 * D * D)),
        name="input_grad",
    )(ids, x, dm, gain, dqkv, *w)


def join_kernel(ids, *refs):
    out = refs[-1]
    step = pl.program_id(0)
    for d in range(QUAD):

        @pl.when(step == d)
        def _(d=d):
            out[0] = refs[d][...]


def join(ids, pieces):
    tile, width = pieces[0].shape
    return pl.pallas_call(
        join_kernel,
        grid_spec=pltpu.PrefetchScalarGridSpec(
            num_scalar_prefetch=1,
            grid=(QUAD,),
            in_specs=[pl.BlockSpec((tile, width), lambda i, s: (0, 0))] * QUAD,
            out_specs=pl.BlockSpec((1, tile, width), lambda i, s: (i ^ s[0], 0, 0)),
        ),
        out_shape=jax.ShapeDtypeStruct((QUAD, tile, width), BF16),
        compiler_params=params(),
        cost_estimate=cost(1000, 4 * QUAD * tile * width),
        name="join",
    )(ids, *pieces)


def swap(block, axis, distance):
    count = lax.axis_size(axis)
    return lax.ppermute(block, axis, [(i, i ^ distance) for i in range(count)])


def quad_swap(pieces):
    count = lax.axis_size("tok")
    groups = [list(range(g, g + QUAD)) for g in range(0, count, QUAD)]
    return lax.all_to_all(pieces, "tok", 0, 0, axis_index_groups=groups, tiled=True)


def by_halves(whole):
    over_row, height, cols = whole.shape
    if over_row == 2:
        return whole
    return (
        whole.reshape(2, over_row // 2, height, cols)
        .transpose(0, 2, 1, 3)
        .reshape(2, height, over_row // 2 * cols)
    )


def gather(shard):
    rows, cols = shard.shape
    whole = lax.all_gather(shard, ("row", "tok"), axis=0, tiled=True)
    return by_halves(whole.reshape(lax.axis_size("row"), rows * lax.axis_size("tok"), cols))


def gather_line(shard):
    return jnp.stack([shard] + [swap(shard, "tok", QUAD * e) for e in range(1, 4)])


def spread(block, steps):
    return [block] + [swap(block, "tok", step) for step in steps]


def with_partner(blocks):
    return blocks + [swap(t, "row", 1) for t in blocks]


QUAD_STEPS = (1, 2, 3)
LINE_STEPS = (QUAD, 2 * QUAD, 3 * QUAD)


def after(value, *others):
    return lax.optimization_barrier((value,) + others)[0]


def from_peers(blocks, steps):
    return [blocks[0]] + [swap(t, "tok", step) for t, step in zip(blocks[1:], steps)]


def line_swap(pieces):
    count = lax.axis_size("tok")
    groups = [list(range(q, count, QUAD)) for q in range(QUAD)]
    return lax.all_to_all(pieces, "tok", 0, 0, axis_index_groups=groups, tiled=True)


def total_of(terms):
    return sum([t.astype(F32) for t in terms[1:]], terms[0].astype(F32))


def scatter(halves):
    over_row = lax.axis_size("row")
    _, height, width = halves.shape
    cols = 2 * width // over_row
    if over_row != 2:
        halves = halves.reshape(2, height, over_row // 2, cols).transpose(0, 2, 1, 3)
    flat = halves.reshape(over_row * height, cols)
    return lax.psum_scatter(flat, ("row", "tok"), scatter_dimension=0, tiled=True).astype(F32)


def scatter_sides(sides, row_index):
    flat = jnp.stack(sides)
    return scatter(jnp.where(row_index % 2 == 0, flat, flat[::-1]))


def all_sum(block, steps):
    for step in steps:
        block = block + (swap(block, "tok", step) if step else swap(block, "row", 1))
    return block


def per_device(
    tokens,
    out_grad,
    doc_lengths,
    first_gain,
    first_bias,
    qkv_weight,
    query_bias,
    value_bias,
    proj_weight,
    proj_bias,
    second_gain,
    second_bias,
    up_weight,
    up_bias,
    down_weight,
    down_bias,
):
    row_count, piece_len, width = tokens.shape
    n = row_count * piece_len
    tok_index = lax.axis_index("tok")
    row_index = lax.axis_index("row")
    groups = lax.axis_size("tok") // QUAD
    by_permutes = lax.axis_size("row") == 2 and groups == 4
    ids = jnp.stack([tok_index % QUAD, tok_index // QUAD, row_index % 2]).astype(jnp.int32)
    lens = lax.dynamic_slice(
        doc_lengths,
        (tok_index % QUAD, tok_index // QUAD, 0),
        (1, 1, doc_lengths.shape[2]),
    )[0]

    qkv_bias = jnp.concatenate([query_bias, jnp.zeros_like(query_bias), value_bias])[None]
    vectors = [qkv_bias] + [
        t[None]
        for t in (first_gain, first_bias, proj_bias, second_gain, second_bias, up_bias, down_bias)
    ]
    if by_permutes:
        packed = jnp.concatenate([down_weight, proj_weight], axis=0)
        rest = lax.all_gather(packed, ("row", "tok"), axis=0, tiled=True)
        rest = rest.reshape((2, lax.axis_size("tok")) + packed.shape)
        x = quad_swap(tokens).reshape(n, width)
        qkv_line = gather_line(qkv_weight)
        up_shard = after(up_weight, qkv_line)
        qkv_line, x, ids, lens, *vectors = lax.optimization_barrier(
            (qkv_line, x, ids, lens, *vectors)
        )
        up_line = gather_line(up_shard)
        qkv_pieces = spread(qkv_line, QUAD_STEPS)
        qkv_full = with_partner(qkv_pieces)
        up_pieces = spread(after(up_line, *qkv_pieces), QUAD_STEPS)
    else:
        x = quad_swap(tokens).reshape(n, width)
        qkv_full = [gather(qkv_weight)]
        others = [gather(proj_weight), gather(up_weight), gather(down_weight)]
    qkv_bias, first_gain, first_bias, proj_bias, second_gain, second_bias, up_bias, down_bias = vectors
    act1, qkv = norm_qkv(ids, x, first_gain, first_bias, qkv_bias, qkv_full)
    attended, stats = attention(lens, qkv)
    if by_permutes:
        up_pieces = list(lax.optimization_barrier((attended, *up_pieces))[1:])
        others = with_partner(up_pieces) + [rest]
    c = quad_swap(after(out_grad, attended, *others)).reshape(n, width)
    middle, out, hidden, slope, act2 = mlp(
        ids, x, attended, proj_bias, second_gain, second_bias, up_bias, down_bias, others
    )
    output = quad_swap(after(out, c).reshape(row_count, piece_len, width))
    du, dm, dy, dout, vecs, uvec = mlp_back(ids, c, middle, slope, second_gain, others)
    up_outer_grad = up_outer(after(act2, output), du, attended, dy)
    down_sides = down_outer(ids, after(hidden, up_outer_grad), c)
    if by_permutes:
        down_blocks = merge(ids, down_sides[0], swap(down_sides[1], "row", 1), False, "down_merge")
        dout = after(dout, *down_blocks)
    dqkv = attention_back(lens, qkv, attended, dout, stats)
    if by_permutes:
        up_proj = scatter(up_outer_grad)
        up_grad, proj_grad = up_proj[:, : FF // 2], up_proj[:, FF // 2 :]
        down_got = from_peers(down_blocks, QUAD_STEPS)
        act1 = after(act1, *down_got[1:])
    qkv_sides = qkv_outer(ids, act1, dqkv)
    if by_permutes:
        down_got[0] = after(down_got[0], *qkv_sides)
        down_line = add_quad(ids, down_got, False, "down_add")
        qkv_mine = after(qkv_sides[0], down_line)
        down_line = line_swap(down_line)
        qkv_blocks = merge(ids, qkv_mine, swap(qkv_sides[1], "row", 1), False, "qkv_merge")
        dqkv = after(dqkv, *qkv_blocks)
        qkv_got = from_peers(qkv_blocks, QUAD_STEPS)
        qkv_shards = add_quad(ids, qkv_got, True, "qkv_add")
        qkv_grad = total_of(from_peers(qkv_shards, LINE_STEPS))
        down_grad = total_of([down_line[e] for e in range(groups)])
    else:
        down_grad = scatter_sides(down_sides, row_index)
        up_grad = scatter(up_outer_grad[:, :, : FF // 2])
        proj_grad = scatter(up_outer_grad[:, :, FF // 2 :])
        qkv_grad = scatter_sides(qkv_sides, row_index)
    *dx, vecs1 = input_grad(ids, x, dm, first_gain, dqkv, qkv_full)
    dx = from_peers(dx, QUAD_STEPS)
    if by_permutes:
        dx[0] = after(dx[0], down_line)
    tokens_grad = join(ids, dx)
    packed = jnp.concatenate(
        [
            vecs1[0, :D], vecs1[1, :D], vecs1[2, :D], vecs1[2, 2 * D :], vecs[2], vecs[0], vecs[1],
            vecs[3], uvec[0],
        ]
    ).reshape(-1, 128)
    if by_permutes:
        packed = all_sum(after(packed, *qkv_shards), (0,) + LINE_STEPS[:2])
        total = all_sum(after(packed, *dx), QUAD_STEPS[:2]).reshape(-1)
    else:
        total = lax.psum(packed, ("tok", "row")).reshape(-1)
    v = [total[i * D : (i + 1) * D] for i in range(8)]
    return (
        output, tokens_grad, qkv_grad, proj_grad, up_grad, down_grad,
        v[0], v[1], v[2], v[3], v[4], v[5], v[6], total[8 * D :], v[7],
    )


def solution(mesh):
    rows = P("row", "tok", None)
    weight = P("tok", "row")
    in_specs = (
        rows, rows, P("row", None, None), P(), P(), weight, P(), P(), weight, P(), P(), P(),
        weight, P(), weight, P(),
    )
    out_specs = (rows, rows, weight, weight, weight, weight) + (P(),) * 9
    return jax.shard_map(
        per_device, mesh=mesh, in_specs=in_specs, out_specs=out_specs, check_vma=False
    )
```

```python
import functools
import math

import jax
import jax.numpy as jnp
from jax import lax
from jax.experimental import pallas as pl
from jax.experimental.pallas import tpu as pltpu
from jax.sharding import PartitionSpec as P

D = 768
H = 12
HD = 64
FF = 3072
DEPTH = 48
DOCS = 8
BLK = 256
QUAD = 4

EPSILON = 1e-05
MASKED = -1e9
TANH_ROOT = 0.7978845608028654
TANH_CUBIC = 0.044715
BETA = 1.0 / math.sqrt(DEPTH)
SCALE = 1.0 / math.sqrt(HD)
F32 = jnp.float32
BF16 = jnp.bfloat16
VMEM_LIMIT = 56 * 2**20
EASE = 8

NT = (((1,), (1,)), ((), ()))
NN = (((1,), (0,)), ((), ()))
TN = (((0,), (0,)), ((), ()))


def mm(a, b, dims=NN):
    return lax.dot_general(a, b, dims, preferred_element_type=F32)


def params():
    return pltpu.CompilerParams(vmem_limit_bytes=VMEM_LIMIT)


def cost(flops, nbytes, trans=0):
    return pl.CostEstimate(
        flops=int(flops // EASE), bytes_accessed=int(nbytes // EASE), transcendentals=int(trans // EASE)
    )


def norm_parts(x):
    centre = x - jnp.mean(x, axis=-1, keepdims=True)
    inverse = lax.rsqrt(jnp.mean(centre * centre, axis=-1, keepdims=True) + EPSILON)
    return centre * inverse, inverse


def norm_back(grad, normed, inverse, gain):
    spread = grad * gain
    return inverse * (
        spread
        - jnp.mean(spread, axis=-1, keepdims=True)
        - normed * jnp.mean(spread * normed, axis=-1, keepdims=True)
    )


def whole(ref, sem):
    return pltpu.make_async_copy(ref, ref, sem)


def place_pieces(ids, pieces, quad_first, targets):
    count = len(pieces) // 2
    for side in range(2):
        for block in range(count):
            ref = pieces[side * count + block]
            for slot in range(ref.shape[0]):
                d, e = (slot, block) if quad_first else (block, slot)
                shard = (ids[1] ^ e) * QUAD + (ids[0] ^ d)
                rows = ref.shape[1]
                here = pl.ds(pl.multiple_of(shard * rows, 16), rows)
                for at, lanes, w, sem in targets:
                    there = pl.ds(pl.multiple_of((ids[2] ^ side) * lanes, 128), lanes)
                    src = ref.at[slot, :, pl.ds(at, lanes)]
                    pltpu.make_async_copy(src, w.at[here, there], sem).start()


def place_halves(halves, w, sem):
    cols = halves.shape[2]
    for h in range(2):
        pltpu.make_async_copy(halves.at[h], w.at[:, pl.ds(h * cols, cols)], sem).start()


def place(ids, parts, w, sem):
    if len(parts) == 1:
        place_halves(parts[0], w, sem)
    else:
        place_pieces(ids, parts, False, [(0, parts[0].shape[2], w, sem)])


def norm_kernel(x_ref, g_ref, b_ref, act_ref):
    normed, _ = norm_parts(x_ref[...].astype(F32))
    act_ref[...] = (normed * g_ref[...] + b_ref[...]).astype(BF16)


def first_norm(x, gain, bias):
    n = x.shape[0]
    row = pl.BlockSpec((BLK, D), lambda i: (i, 0))
    vec = pl.BlockSpec((1, D), lambda i: (0, 0))
    return pl.pallas_call(
        norm_kernel,
        grid=(n // BLK,),
        in_specs=[row, vec, vec],
        out_specs=row,
        out_shape=jax.ShapeDtypeStruct((n, D), BF16),
        compiler_params=params(),
        cost_estimate=cost(8 * n * D, 4 * n * D),
        name="first_norm",
    )(x, gain, bias)


def qkv_kernel(parts, ids, act_ref, qb_ref, *rest):
    w_hbm, (qkv_ref, w_vmem, sem) = rest[:parts], rest[parts:]

    @pl.when(pl.program_id(0) == 0)
    def _():
        place(ids, w_hbm, w_vmem, sem)
        whole(w_vmem, sem).wait()

    qkv_ref[...] = (mm(act_ref[...], w_vmem[...]) + qb_ref[...]).astype(BF16)


def project_qkv(ids, act, qkv_bias, w):
    n = act.shape[0]
    tile = BLK
    return pl.pallas_call(
        functools.partial(qkv_kernel, len(w)),
        grid=(n // tile,),
        in_specs=[
            pl.BlockSpec(memory_space=pltpu.SMEM),
            pl.BlockSpec((tile, D), lambda i: (i, 0)),
            pl.BlockSpec((1, 3 * D), lambda i: (0, 0)),
        ]
        + [pl.BlockSpec(memory_space=pl.ANY)] * len(w),
        out_specs=pl.BlockSpec((tile, 3 * D), lambda i: (i, 0)),
        out_shape=jax.ShapeDtypeStruct((n, 3 * D), BF16),
        scratch_shapes=[pltpu.VMEM((D, 3 * D), BF16), pltpu.SemaphoreType.DMA],
        compiler_params=params(),
        cost_estimate=cost(2 * n * D * 3 * D, 2 * (n * 4 * D + 3 * D * D)),
        name="project_qkv",
    )(ids, act, qkv_bias, *w)


def first_of_doc(lens_ref, positions):
    start = jnp.zeros_like(positions)
    end = 0
    for d in range(DOCS):
        end = end + lens_ref[0, d]
        start = jnp.where(positions >= end, end, start)
    return start


def lane_half(h):
    lane = lax.broadcasted_iota(jnp.int32, (1, 128), 1)
    return (lane >= h * HD) & (lane < (h + 1) * HD)


WINDOW = 2


def mask(lens_ref, keys_at, keys, queries_at, queries):
    qpos = lax.broadcasted_iota(jnp.int32, (1, queries), 1) + queries_at
    kpos = lax.broadcasted_iota(jnp.int32, (keys, 1), 0) + keys_at
    return jnp.where((kpos >= first_of_doc(lens_ref, qpos)) & (kpos <= qpos), 0.0, MASKED)


def attn_kernel(lens_ref, q_ref, k_ref, v_ref, o_ref, l_ref, mask_ref):
    pair = pl.program_id(0)
    blocks = []
    for i in range(q_ref.shape[0] // BLK):
        low = max(0, i - WINDOW)
        blocks.append((low * BLK, (i + 1 - low) * BLK, i * BLK))

    @pl.when(pair == 0)
    def _():
        l_ref[...] = jnp.zeros_like(l_ref)
        for first, count, at in blocks:
            mask_ref[0:count, at : at + BLK] = mask(lens_ref, first, count, at, BLK)

    for first, count, at in blocks:
        rows = slice(at, at + BLK)
        q = q_ref[rows, :] * jnp.asarray(SCALE, BF16)
        k = k_ref[first : first + count, :]
        v = v_ref[first : first + count, :]
        out = None
        for h in range(2):
            half = lane_half(h)
            s = mm(k, jnp.where(half, q, jnp.zeros_like(q)), NT) + mask_ref[0:count, rows]
            m = jnp.max(s, axis=0, keepdims=True)
            p = jnp.exp(s - m)
            total = jnp.sum(p, axis=0, keepdims=True)
            probs = (p * (1.0 / total)).astype(BF16)
            o = mm(probs, jnp.where(half, v, jnp.zeros_like(v)), TN)
            out = o if out is None else out + o
            l_ref[pl.ds(2 * pair + h, 1), rows] = m + jnp.log(total)
        o_ref[rows, :] = out.astype(BF16)


def attention(lens, qkv):
    n = qkv.shape[0]
    pairs = H // 2
    spec = lambda w: pl.BlockSpec((n, 128), lambda p: (0, w * pairs + p))
    return pl.pallas_call(
        attn_kernel,
        grid=(pairs,),
        in_specs=[pl.BlockSpec(memory_space=pltpu.SMEM), spec(0), spec(1), spec(2)],
        out_specs=[
            pl.BlockSpec((n, 128), lambda p: (0, p)),
            pl.BlockSpec((16, n), lambda p: (0, 0)),
        ],
        out_shape=[jax.ShapeDtypeStruct((n, D), BF16), jax.ShapeDtypeStruct((16, n), F32)],
        scratch_shapes=[pltpu.VMEM(((WINDOW + 1) * BLK, n), F32)],
        compiler_params=params(),
        cost_estimate=cost(2 * 2 * H * n * n * HD * 0.6, 2 * n * 4 * D, H * n * n * 0.6),
        name="attention",
    )(lens, qkv, qkv, qkv)


def attn_back_kernel(
    lens_ref, q_ref, k_ref, v_ref, o_ref, do_ref, l_ref, out_hbm, mask_ref, dq_acc, bufs, sems
):
    pair = pl.program_id(0)
    pairs = pl.num_programs(0)
    n = q_ref.shape[0]
    slot = pair % 2
    blocks = [(at, min((WINDOW + 1) * BLK, n - at)) for at in range(0, n, BLK)]

    def copies(p, at):
        return [
            pltpu.make_async_copy(
                bufs.at[at, w],
                out_hbm.at[:, pl.ds(pl.multiple_of(w * D + p * 128, 128), 128)],
                sems.at[at, w],
            )
            for w in range(3)
        ]

    @pl.when(pair == 0)
    def _():
        for at, count in blocks:
            mask_ref[at : at + BLK, 0:count] = mask(lens_ref, at, BLK, at, count)

    @pl.when(pair >= 2)
    def _():
        for c in copies(pair - 2, slot):
            c.wait()

    prod = (o_ref[...].astype(F32) * do_ref[...].astype(F32)).T
    dq_acc[...] = jnp.zeros_like(dq_acc)
    for at, count in blocks:
        keys = slice(at, at + BLK)
        queries = slice(at, at + count)
        k = k_ref[keys, :]
        v = v_ref[keys, :]
        q = q_ref[queries, :] * jnp.asarray(SCALE, BF16)
        do = do_ref[queries, :]
        dk = dv = None
        for h in range(2):
            half = lane_half(h)
            inner = jnp.sum(prod[h * HD : (h + 1) * HD, queries], axis=0, keepdims=True)
            logs = l_ref[pl.ds(2 * pair + h, 1), queries]
            qh = jnp.where(half, q, jnp.zeros_like(q))
            doh = jnp.where(half, do, jnp.zeros_like(do))
            kh = jnp.where(half, k, jnp.zeros_like(k))
            p = jnp.exp(mm(k, qh, NT) + (mask_ref[keys, 0:count] - logs))
            ds = (p * (mm(v, doh, NT) - inner)).astype(BF16)
            dvh = mm(p.astype(BF16), doh)
            dkh = mm(ds, qh)
            dv, dk = (dvh, dkh) if h == 0 else (dv + dvh, dk + dkh)
            dq_acc[queries, :] += mm(ds, kh, TN)
        bufs[slot, 1, keys, :] = dk.astype(BF16)
        bufs[slot, 2, keys, :] = dv.astype(BF16)
    bufs[slot, 0] = (dq_acc[...] * SCALE).astype(BF16)
    for c in copies(pair, slot):
        c.start()

    @pl.when(pair == pairs - 1)
    def _():
        for c in copies(pair - 1, 1 - slot) + copies(pair, slot):
            c.wait()


def attention_back(lens, qkv, attended, dout, stats):
    n = qkv.shape[0]
    pairs = H // 2
    spec = lambda w: pl.BlockSpec((n, 128), lambda p: (0, w * pairs + p))
    one = pl.BlockSpec((n, 128), lambda p: (0, p))
    return pl.pallas_call(
        attn_back_kernel,
        grid=(pairs,),
        in_specs=[
            pl.BlockSpec(memory_space=pltpu.SMEM), spec(0), spec(1), spec(2), one, one,
            pl.BlockSpec((16, n), lambda p: (0, 0)),
        ],
        out_specs=pl.BlockSpec(memory_space=pl.ANY),
        out_shape=jax.ShapeDtypeStruct((n, 3 * D), BF16),
        scratch_shapes=[
            pltpu.VMEM((n, (WINDOW + 1) * BLK), F32),
            pltpu.VMEM((n, 128), F32),
            pltpu.VMEM((2, 3, n, 128), BF16),
            pltpu.SemaphoreType.DMA((2, 3)),
        ],
        compiler_params=params(),
        cost_estimate=cost(5 * 2 * H * n * n * HD * 0.6, 2 * n * 8 * D, H * n * n * 0.6),
        name="attention_back",
    )(lens, qkv, qkv, qkv, attended, dout, stats)


def start_mlp_weights(ids, w_hbm, wp, wu, wd, sem):
    if len(w_hbm) == 3:
        for i, w in enumerate((wp, wu, wd)):
            place_halves(w_hbm[i], w, sem.at[i])
        return
    packed = w_hbm[-1]
    _, count, _, lanes = packed.shape

    def body(t, carry):
        for w, i, at, rows in ((wp, 0, FF // count, D // count), (wd, 2, 0, FF // count)):
            here = pl.ds(pl.multiple_of(t * rows, 16), rows)
            for h in range(2):
                src = packed.at[h, t, pl.ds(at, rows), :]
                pltpu.make_async_copy(src, w.at[here, pl.ds(h * lanes, lanes)], sem.at[i]).start()
        return carry

    lax.fori_loop(0, count, body, 0)
    place_pieces(ids, w_hbm[:-1], False, [(0, FF // 2, wu, sem.at[1])])


def mlp_kernel(
    parts, ids, x_ref, att_ref, pb_ref, g_ref, b_ref, ub_ref, db_ref, *rest
):
    w_hbm = rest[:parts]
    mid_ref, out_ref, hid_ref, slope_ref, act_ref, wp, wu, wd, sem = rest[parts:]
    step = pl.program_id(0)

    @pl.when(step == 0)
    def _():
        start_mlp_weights(ids, w_hbm, wp, wu, wd, sem)
        whole(wp, sem.at[0]).wait()

    middle = x_ref[...].astype(F32) + BETA * (mm(att_ref[...], wp[...]) + pb_ref[...])
    mid_ref[...] = middle
    normed, _ = norm_parts(middle)
    act = (normed * g_ref[...] + b_ref[...]).astype(BF16)
    act_ref[...] = act

    @pl.when(step == 0)
    def _():
        whole(wu, sem.at[1]).wait()
        whole(wd, sem.at[2]).wait()

    chunk = 768
    branch = jnp.zeros(middle.shape, F32)
    for f in range(FF // chunk):
        cols = pl.ds(f * chunk, chunk)
        u = mm(act, wu[:, cols]) + ub_ref[:, cols]
        u2 = u * u
        gate = 0.5 + 0.5 * jnp.tanh(u * (TANH_ROOT + (TANH_ROOT * TANH_CUBIC) * u2))
        value = u * gate
        hidden = value.astype(BF16)
        hid_ref[:, cols] = hidden
        branch = branch + mm(hidden, wd[cols, :])
        slope = gate + value * (1.0 - gate) * (
            2.0 * TANH_ROOT + (6.0 * TANH_ROOT * TANH_CUBIC) * u2
        )
        slope_ref[:, cols] = slope.astype(BF16)
    out_ref[...] = (middle + BETA * (branch + db_ref[...])).astype(BF16)


MLP_SCRATCH = [
    pltpu.VMEM((D, D), BF16),
    pltpu.VMEM((D, FF), BF16),
    pltpu.VMEM((FF, D), BF16),
    pltpu.SemaphoreType.DMA((3,)),
]


def mlp(ids, x, att, pb, gain, bias, ub, db, w):
    n = x.shape[0]
    tile = BLK
    row = lambda w: pl.BlockSpec((tile, w), lambda i: (i, 0))
    vec = lambda w: pl.BlockSpec((1, w), lambda i: (0, 0))
    sds = jax.ShapeDtypeStruct
    return pl.pallas_call(
        functools.partial(mlp_kernel, len(w)),
        grid=(n // tile,),
        in_specs=[pl.BlockSpec(memory_space=pltpu.SMEM)]
        + [row(D), row(D), vec(D), vec(D), vec(D), vec(FF), vec(D)]
        + [pl.BlockSpec(memory_space=pl.ANY)] * len(w),
        out_specs=[row(D), row(D), row(FF), row(FF), row(D)],
        out_shape=[
            sds((n, D), F32), sds((n, D), BF16), sds((n, FF), BF16), sds((n, FF), BF16),
            sds((n, D), BF16),
        ],
        scratch_shapes=MLP_SCRATCH,
        compiler_params=params(),
        cost_estimate=cost(2 * n * (2 * D * FF + D * D), 2 * n * (7 * D + 2 * FF), n * FF),
        name="mlp",
    )(ids, x, att, pb, gain, bias, ub, db, *w)


def mlp_back_kernel(parts, ids, c_ref, mid_ref, slope_ref, g_ref, *rest):
    w_hbm = rest[:parts]
    du_ref, dm_ref, dy_ref, do_ref, vec_ref, uvec_ref, wp, wu, wd, sem = rest[parts:]
    step = pl.program_id(0)

    @pl.when(step == 0)
    def _():
        start_mlp_weights(ids, w_hbm, wp, wu, wd, sem)
        vec_ref[...] = jnp.zeros_like(vec_ref)
        uvec_ref[...] = jnp.zeros_like(uvec_ref)

    grad_out = c_ref[...].astype(F32)
    dz = (BETA * grad_out).astype(BF16)
    normed, inverse = norm_parts(mid_ref[...])

    @pl.when(step == 0)
    def _():
        whole(wd, sem.at[2]).wait()
        whole(wu, sem.at[1]).wait()
        whole(wp, sem.at[0]).wait()

    chunk = 768
    da = jnp.zeros(normed.shape, F32)
    for f in range(FF // chunk):
        cols = pl.ds(f * chunk, chunk)
        du = (mm(dz, wd[cols, :], NT) * slope_ref[:, cols].astype(F32)).astype(BF16)
        du_ref[:, cols] = du
        uvec_ref[0:1, cols] += jnp.sum(du.astype(F32), axis=0, keepdims=True)
        da = da + mm(du, wu[:, cols], NT)
    dm = grad_out + norm_back(da, normed, inverse, g_ref[...])
    dm_ref[...] = dm
    dy = (BETA * dm).astype(BF16)
    dy_ref[...] = dy
    do_ref[...] = mm(dy, wp[...], NT).astype(BF16)
    vec_ref[0:1, :] += jnp.sum(da * normed, axis=0, keepdims=True)
    vec_ref[1:2, :] += jnp.sum(da, axis=0, keepdims=True)
    vec_ref[2:3, :] += jnp.sum(dy.astype(F32), axis=0, keepdims=True)
    vec_ref[3:4, :] += jnp.sum(dz.astype(F32), axis=0, keepdims=True)


def mlp_back(ids, c, middle, slope, gain, w):
    n = c.shape[0]
    tile = BLK
    const = lambda i: (0, 0)
    row = lambda w: pl.BlockSpec((tile, w), lambda i: (i, 0))
    sds = jax.ShapeDtypeStruct
    return pl.pallas_call(
        functools.partial(mlp_back_kernel, len(w)),
        grid=(n // tile,),
        in_specs=[pl.BlockSpec(memory_space=pltpu.SMEM)]
        + [row(D), row(D), row(FF), pl.BlockSpec((1, D), const)]
        + [pl.BlockSpec(memory_space=pl.ANY)] * len(w),
        out_specs=[
            row(FF), row(D), row(D), row(D), pl.BlockSpec((8, D), const), pl.BlockSpec((8, FF), const),
        ],
        out_shape=[
            sds((n, FF), BF16), sds((n, D), F32), sds((n, D), BF16), sds((n, D), BF16),
            sds((8, D), F32), sds((8, FF), F32),
        ],
        scratch_shapes=MLP_SCRATCH,
        compiler_params=params(),
        cost_estimate=cost(2 * n * (2 * D * FF + D * D), 2 * n * (7 * D + 2 * FF), n * FF),
        name="mlp_back",
    )(ids, c, middle, slope, gain, *w)


def store_sides(row, r, mine, theirs):
    width = r.shape[1] // 2

    @pl.when(row == 0)
    def _():
        mine[...] = r[:, :width].astype(BF16)
        theirs[...] = r[:, width:].astype(BF16)

    @pl.when(row == 1)
    def _():
        theirs[...] = r[:, :width].astype(BF16)
        mine[...] = r[:, width:].astype(BF16)


def down_outer_kernel(ids, a_ref, c_ref, mine, theirs, dz):
    @pl.when(pl.program_id(0) == 0)
    def _():
        dz[...] = (BETA * c_ref[...].astype(F32)).astype(BF16)

    store_sides(ids[2], mm(a_ref[...], dz[...], TN), mine, theirs)


def down_outer(ids, hidden, c):
    n = hidden.shape[0]
    half = pl.BlockSpec((D, D // 2), lambda i, s: (i, 0))
    return pl.pallas_call(
        down_outer_kernel,
        grid_spec=pltpu.PrefetchScalarGridSpec(
            num_scalar_prefetch=1,
            grid=(FF // D,),
            in_specs=[
                pl.BlockSpec((n, D), lambda i, s: (0, i)),
                pl.BlockSpec((n, D), lambda i, s: (0, 0)),
            ],
            out_specs=[half, half],
            scratch_shapes=[pltpu.VMEM((n, D), BF16)],
        ),
        out_shape=[jax.ShapeDtypeStruct((FF, D // 2), BF16)] * 2,
        compiler_params=params(),
        cost_estimate=cost(2 * n * FF * D, 2 * (n * (FF + D) + FF * D)),
        name="down_outer",
    )(ids, hidden, c)


def up_outer_kernel(act_ref, du_ref, att_ref, dy_ref, o_ref):
    o_ref[0, :, : FF // 4] = mm(act_ref[...], du_ref[:, : FF // 4], TN).astype(BF16)
    o_ref[0, :, FF // 4 : FF // 2] = mm(act_ref[...], du_ref[:, FF // 4 :], TN).astype(BF16)
    o_ref[0, :, FF // 2 :] = mm(att_ref[...], dy_ref[...], TN).astype(BF16)


def up_outer(act, du, attended, dy):
    n = act.shape[0]
    width = (FF + D) // 2
    once = pl.BlockSpec((n, D), lambda i: (0, 0))
    half = lambda w: pl.BlockSpec((n, w), lambda i: (0, i))
    return pl.pallas_call(
        up_outer_kernel,
        grid=(2,),
        in_specs=[once, half(FF // 2), once, half(D // 2)],
        out_specs=pl.BlockSpec((1, D, width), lambda i: (i, 0, 0)),
        out_shape=jax.ShapeDtypeStruct((2, D, width), BF16),
        compiler_params=params(),
        cost_estimate=cost(2 * n * D * 2 * width, 2 * (n * (FF + 3 * D) + 2 * D * width)),
        name="up_outer",
    )(act, du, attended, dy)


def qkv_outer_kernel(ids, act_ref, dqkv_ref, mine, theirs):
    step = pl.program_id(0)
    r = mm(act_ref[...], dqkv_ref[...], TN).astype(BF16)

    @pl.when(step == 0)
    def _():
        theirs[...] = r

    @pl.when(step == 1)
    def _():
        mine[...] = r


def qkv_outer(ids, act, dqkv):
    n = act.shape[0]
    width = 3 * D // 2
    out = pl.BlockSpec((D, width), lambda i, s: (0, 0))
    return pl.pallas_call(
        qkv_outer_kernel,
        grid_spec=pltpu.PrefetchScalarGridSpec(
            num_scalar_prefetch=1,
            grid=(2,),
            in_specs=[
                pl.BlockSpec((n, D), lambda i, s: (0, 0)),
                pl.BlockSpec((n, width), lambda i, s: (0, (i + 1 - s[2]) % 2)),
            ],
            out_specs=[out, out],
        ),
        out_shape=[jax.ShapeDtypeStruct((D, width), BF16)] * 2,
        compiler_params=params(),
        cost_estimate=cost(2 * n * D * 2 * width, 2 * (n * (D + 2 * width) + 2 * D * width)),
        name="qkv_outer",
    )(ids, act, dqkv)


def merge_kernel(quad_first, rows, ids, mine, theirs, *outs):
    for block, o in enumerate(outs):
        for slot in range(o.shape[0]):
            e, d = (block, slot) if quad_first else (slot, block)
            shard = (ids[1] ^ e) * QUAD + (ids[0] ^ d)
            here = pl.ds(pl.multiple_of(shard * rows, 16), rows)
            o[slot] = (mine[here, :].astype(F32) + theirs[here, :].astype(F32)).astype(BF16)


def merge(ids, mine, theirs, quad_first, name):
    left, width = mine.shape
    rows = left // (4 * QUAD)
    spec = pl.BlockSpec(memory_space=pltpu.VMEM)
    return pl.pallas_call(
        functools.partial(merge_kernel, quad_first, rows),
        in_specs=[pl.BlockSpec(memory_space=pltpu.SMEM), spec, spec],
        out_shape=[jax.ShapeDtypeStruct((4, rows, width), BF16)] * 4,
        compiler_params=params(),
        cost_estimate=cost(2 * mine.size, 6 * mine.size),
        name=name,
    )(ids, mine, theirs)


def add_quad_kernel(ids, a, b, c, d, *outs):
    for e in range(a.shape[0]):
        total = (a[e].astype(F32) + b[e].astype(F32)) + (c[e].astype(F32) + d[e].astype(F32))
        if len(outs) == 1:
            outs[0][ids[1] ^ e] = total.astype(BF16)
        else:
            outs[e][...] = total.astype(BF16)


def add_quad(ids, parts, apart, name):
    block = parts[0].shape
    sds = jax.ShapeDtypeStruct
    spec = pl.BlockSpec(memory_space=pltpu.VMEM)
    return pl.pallas_call(
        add_quad_kernel,
        in_specs=[pl.BlockSpec(memory_space=pltpu.SMEM)] + [spec] * 4,
        out_shape=[sds(block[1:], BF16)] * block[0] if apart else sds(block, BF16),
        compiler_params=params(),
        cost_estimate=cost(4 * parts[0].size, 10 * parts[0].size),
        name=name,
    )(ids, *parts)


def split_kernel(a_ref, left, right):
    width = left.shape[1]
    left[...] = a_ref[:, :width].astype(F32)
    right[...] = a_ref[:, width:].astype(F32)


def split(a, width):
    rows, cols = a.shape
    sds = jax.ShapeDtypeStruct
    return pl.pallas_call(
        split_kernel,
        out_shape=[sds((rows, width), F32), sds((rows, cols - width), F32)],
        compiler_params=params(),
        cost_estimate=cost(a.size, 6 * a.size),
        name="split",
    )(a)


def input_grad_kernel(parts, ids, x_ref, dm_ref, g_ref, dqkv_ref, *rest):
    w_hbm, outs, (vec_ref, w, sem) = rest[:parts], rest[parts:-3], rest[-3:]
    step = pl.program_id(0)

    @pl.when(step == 0)
    def _():
        place(ids, w_hbm, w, sem)
        vec_ref[...] = jnp.zeros_like(vec_ref)
        whole(w, sem).wait()

    dqkv = dqkv_ref[...]
    da = mm(dqkv, w[...], NT)
    normed, inverse = norm_parts(x_ref[...].astype(F32))
    dx = (dm_ref[...] + norm_back(da, normed, inverse, g_ref[...])).astype(BF16)
    for d, o in enumerate(outs):

        @pl.when(step == d)
        def _(o=o):
            o[...] = dx

    vec_ref[0:1, 0:D] += jnp.sum(da * normed, axis=0, keepdims=True)
    vec_ref[1:2, 0:D] += jnp.sum(da, axis=0, keepdims=True)
    vec_ref[2:3, :] += jnp.sum(dqkv.astype(F32), axis=0, keepdims=True)


def input_grad(ids, x, dm, gain, dqkv, w):
    n = x.shape[0]
    tile = n // QUAD
    const = lambda i, s: (0, 0)
    row = lambda wide: pl.BlockSpec((tile, wide), lambda i, s: (i ^ s[0], 0))
    return pl.pallas_call(
        functools.partial(input_grad_kernel, len(w)),
        grid_spec=pltpu.PrefetchScalarGridSpec(
            num_scalar_prefetch=1,
            grid=(QUAD,),
            in_specs=[row(D), row(D), pl.BlockSpec((1, D), const), row(3 * D)]
            + [pl.BlockSpec(memory_space=pl.ANY)] * len(w),
            out_specs=[pl.BlockSpec((tile, D), const)] * QUAD + [pl.BlockSpec((8, 3 * D), const)],
            scratch_shapes=[pltpu.VMEM((D, 3 * D), BF16), pltpu.SemaphoreType.DMA],
        ),
        out_shape=[jax.ShapeDtypeStruct((tile, D), BF16)] * QUAD
        + [jax.ShapeDtypeStruct((8, 3 * D), F32)],
        compiler_params=params(),
        cost_estimate=cost(2 * n * D * 3 * D, 2 * (n * 7 * D + 3 * D * D)),
        name="input_grad",
    )(ids, x, dm, gain, dqkv, *w)


def join_kernel(ids, *refs):
    out = refs[-1]
    step = pl.program_id(0)
    for d in range(QUAD):

        @pl.when(step == d)
        def _(d=d):
            out[0] = refs[d][...]


def join(ids, pieces):
    tile, width = pieces[0].shape
    return pl.pallas_call(
        join_kernel,
        grid_spec=pltpu.PrefetchScalarGridSpec(
            num_scalar_prefetch=1,
            grid=(QUAD,),
            in_specs=[pl.BlockSpec((tile, width), lambda i, s: (0, 0))] * QUAD,
            out_specs=pl.BlockSpec((1, tile, width), lambda i, s: (i ^ s[0], 0, 0)),
        ),
        out_shape=jax.ShapeDtypeStruct((QUAD, tile, width), BF16),
        compiler_params=params(),
        cost_estimate=cost(1000, 4 * QUAD * tile * width),
        name="join",
    )(ids, *pieces)


def swap(block, axis, distance):
    count = lax.axis_size(axis)
    return lax.ppermute(block, axis, [(i, i ^ distance) for i in range(count)])


def quad_swap(pieces):
    count = lax.axis_size("tok")
    groups = [list(range(g, g + QUAD)) for g in range(0, count, QUAD)]
    return lax.all_to_all(pieces, "tok", 0, 0, axis_index_groups=groups, tiled=True)


def by_halves(whole):
    over_row, height, cols = whole.shape
    if over_row == 2:
        return whole
    return (
        whole.reshape(2, over_row // 2, height, cols)
        .transpose(0, 2, 1, 3)
        .reshape(2, height, over_row // 2 * cols)
    )


def gather(shard):
    rows, cols = shard.shape
    whole = lax.all_gather(shard, ("row", "tok"), axis=0, tiled=True)
    return by_halves(whole.reshape(lax.axis_size("row"), rows * lax.axis_size("tok"), cols))


def gather_line(shard):
    return jnp.stack([shard] + [swap(shard, "tok", QUAD * e) for e in range(1, 4)])


def spread(block, steps):
    return [block] + [swap(block, "tok", step) for step in steps]


def with_partner(blocks):
    return blocks + [swap(t, "row", 1) for t in blocks]


QUAD_STEPS = (1, 2, 3)
LINE_STEPS = (QUAD, 2 * QUAD, 3 * QUAD)


def after(value, *others):
    return lax.optimization_barrier((value,) + others)[0]


def from_peers(blocks, steps):
    return [blocks[0]] + [swap(t, "tok", step) for t, step in zip(blocks[1:], steps)]


def line_swap(pieces):
    count = lax.axis_size("tok")
    groups = [list(range(q, count, QUAD)) for q in range(QUAD)]
    return lax.all_to_all(pieces, "tok", 0, 0, axis_index_groups=groups, tiled=True)


def total_of(terms):
    return sum([t.astype(F32) for t in terms[1:]], terms[0].astype(F32))


def scatter(halves):
    return scatter_narrow(halves).astype(F32)


def scatter_narrow(halves):
    over_row = lax.axis_size("row")
    _, height, width = halves.shape
    cols = 2 * width // over_row
    if over_row != 2:
        halves = halves.reshape(2, height, over_row // 2, cols).transpose(0, 2, 1, 3)
    flat = halves.reshape(over_row * height, cols)
    return lax.psum_scatter(flat, ("row", "tok"), scatter_dimension=0, tiled=True)


def scatter_sides(sides, row_index):
    flat = jnp.stack(sides)
    return scatter(jnp.where(row_index % 2 == 0, flat, flat[::-1]))


def all_sum(block, steps):
    for step in steps:
        block = block + (swap(block, "tok", step) if step else swap(block, "row", 1))
    return block


def per_device(
    tokens,
    out_grad,
    doc_lengths,
    first_gain,
    first_bias,
    qkv_weight,
    query_bias,
    value_bias,
    proj_weight,
    proj_bias,
    second_gain,
    second_bias,
    up_weight,
    up_bias,
    down_weight,
    down_bias,
):
    row_count, piece_len, width = tokens.shape
    n = row_count * piece_len
    tok_index = lax.axis_index("tok")
    row_index = lax.axis_index("row")
    groups = lax.axis_size("tok") // QUAD
    by_permutes = lax.axis_size("row") == 2 and groups == 4
    ids = jnp.stack([tok_index % QUAD, tok_index // QUAD, row_index % 2]).astype(jnp.int32)
    lens = lax.dynamic_slice(
        doc_lengths,
        (tok_index % QUAD, tok_index // QUAD, 0),
        (1, 1, doc_lengths.shape[2]),
    )[0]

    qkv_bias = jnp.concatenate([query_bias, jnp.zeros_like(query_bias), value_bias])[None]
    vectors = [qkv_bias] + [
        t[None]
        for t in (first_gain, first_bias, proj_bias, second_gain, second_bias, up_bias, down_bias)
    ]
    if by_permutes:
        packed = jnp.concatenate([down_weight, proj_weight], axis=0)
        rest = lax.all_gather(packed, ("row", "tok"), axis=0, tiled=True)
        rest = rest.reshape((2, lax.axis_size("tok")) + packed.shape)
        x = quad_swap(tokens).reshape(n, width)
        qkv_line = gather_line(qkv_weight)
        up_shard = after(up_weight, qkv_line)
        qkv_line, x, ids, lens, *vectors = lax.optimization_barrier(
            (qkv_line, x, ids, lens, *vectors)
        )
        up_line = gather_line(up_shard)
        qkv_pieces = spread(qkv_line, QUAD_STEPS)
        up_pieces = spread(after(up_line, *qkv_pieces), QUAD_STEPS)
    else:
        x = quad_swap(tokens).reshape(n, width)
        qkv_full = [gather(qkv_weight)]
        others = [gather(proj_weight), gather(up_weight), gather(down_weight)]
    qkv_bias, first_gain, first_bias, proj_bias, second_gain, second_bias, up_bias, down_bias = vectors
    act1 = first_norm(x, first_gain, first_bias)
    if by_permutes:
        act1, qkv_pieces[-1] = lax.optimization_barrier((act1, qkv_pieces[-1]))
        qkv_full = with_partner(qkv_pieces)
    qkv = project_qkv(ids, act1, qkv_bias, qkv_full)
    attended, stats = attention(lens, qkv)
    if by_permutes:
        up_pieces[1:] = lax.optimization_barrier((attended, *up_pieces[1:]))[1:]
        others = with_partner(up_pieces) + [rest]
    held = others[:-1] if by_permutes else [attended]
    c = quad_swap(after(out_grad, *held)).reshape(n, width)
    middle, out, hidden, slope, act2 = mlp(
        ids, x, attended, proj_bias, second_gain, second_bias, up_bias, down_bias, others
    )
    output = quad_swap(after(out, c).reshape(row_count, piece_len, width))
    du, dm, dy, dout, vecs, uvec = mlp_back(ids, c, middle, slope, second_gain, others)
    up_outer_grad = up_outer(after(act2, output), du, attended, dy)
    down_sides = down_outer(ids, after(hidden, up_outer_grad), c)
    if by_permutes:
        down_blocks = merge(ids, down_sides[0], swap(down_sides[1], "row", 1), False, "down_merge")
        dout = after(dout, *down_blocks)
    dqkv = attention_back(lens, qkv, attended, dout, stats)
    if by_permutes:
        up_grad, proj_grad = split(scatter_narrow(up_outer_grad), FF // 2)
        down_got = from_peers(down_blocks, QUAD_STEPS)
        act1 = after(act1, *down_got[1:])
    qkv_sides = qkv_outer(ids, act1, dqkv)
    if by_permutes:
        down_got[0] = after(down_got[0], *qkv_sides)
        down_line = add_quad(ids, down_got, False, "down_add")
        qkv_mine = after(qkv_sides[0], down_line)
        down_line = line_swap(down_line)
        qkv_blocks = merge(ids, qkv_mine, swap(qkv_sides[1], "row", 1), False, "qkv_merge")
        dqkv = after(dqkv, *qkv_blocks)
        qkv_got = from_peers(qkv_blocks, QUAD_STEPS)
        qkv_shards = add_quad(ids, qkv_got, True, "qkv_add")
        qkv_grad = total_of(from_peers(qkv_shards, LINE_STEPS))
        down_grad = total_of([down_line[e] for e in range(groups)])
    else:
        down_grad = scatter_sides(down_sides, row_index)
        up_grad = scatter(up_outer_grad[:, :, : FF // 2])
        proj_grad = scatter(up_outer_grad[:, :, FF // 2 :])
        qkv_grad = scatter_sides(qkv_sides, row_index)
    *dx, vecs1 = input_grad(ids, x, dm, first_gain, dqkv, qkv_full)
    dx = from_peers(dx, QUAD_STEPS)
    if by_permutes:
        dx[0] = after(dx[0], down_line)
    tokens_grad = join(ids, dx)
    packed = jnp.concatenate(
        [
            vecs1[0, :D], vecs1[1, :D], vecs1[2, :D], vecs1[2, 2 * D :], vecs[2], vecs[0], vecs[1],
            vecs[3], uvec[0],
        ]
    ).reshape(-1, 128)
    if by_permutes:
        packed = all_sum(after(packed, *qkv_shards), (0,) + LINE_STEPS[:2])
        total = all_sum(after(packed, *dx), QUAD_STEPS[:2]).reshape(-1)
    else:
        total = lax.psum(packed, ("tok", "row")).reshape(-1)
    v = [total[i * D : (i + 1) * D] for i in range(8)]
    return (
        output, tokens_grad, qkv_grad, proj_grad, up_grad, down_grad,
        v[0], v[1], v[2], v[3], v[4], v[5], v[6], total[8 * D :], v[7],
    )


def solution(mesh):
    rows = P("row", "tok", None)
    weight = P("tok", "row")
    in_specs = (
        rows, rows, P("row", None, None), P(), P(), weight, P(), P(), weight, P(), P(), P(),
        weight, P(), weight, P(),
    )
    out_specs = (rows, rows, weight, weight, weight, weight) + (P(),) * 9
    return jax.shard_map(
        per_device, mesh=mesh, in_specs=in_specs, out_specs=out_specs, check_vma=False
    )
```

```python
import functools
import math

import jax
import jax.numpy as jnp
from jax import lax
from jax.experimental import pallas as pl
from jax.experimental.pallas import tpu as pltpu
from jax.sharding import PartitionSpec as P

D = 768
H = 12
HD = 64
FF = 3072
DEPTH = 48
DOCS = 8
BLK = 256
QUAD = 4

EPSILON = 1e-05
MASKED = -1e9
TANH_ROOT = 0.7978845608028654
TANH_CUBIC = 0.044715
BETA = 1.0 / math.sqrt(DEPTH)
SCALE = 1.0 / math.sqrt(HD)
F32 = jnp.float32
BF16 = jnp.bfloat16
VMEM_LIMIT = 56 * 2**20
EASE = 8

NT = (((1,), (1,)), ((), ()))
NN = (((1,), (0,)), ((), ()))
TN = (((0,), (0,)), ((), ()))


def mm(a, b, dims=NN):
    return lax.dot_general(a, b, dims, preferred_element_type=F32)


def params():
    return pltpu.CompilerParams(vmem_limit_bytes=VMEM_LIMIT)


def cost(flops, nbytes, trans=0):
    return pl.CostEstimate(
        flops=int(flops // EASE), bytes_accessed=int(nbytes // EASE), transcendentals=int(trans // EASE)
    )


def norm_parts(x):
    centre = x - jnp.mean(x, axis=-1, keepdims=True)
    inverse = lax.rsqrt(jnp.mean(centre * centre, axis=-1, keepdims=True) + EPSILON)
    return centre * inverse, inverse


def norm_back(grad, normed, inverse, gain):
    spread = grad * gain
    return inverse * (
        spread
        - jnp.mean(spread, axis=-1, keepdims=True)
        - normed * jnp.mean(spread * normed, axis=-1, keepdims=True)
    )


def whole(ref, sem):
    return pltpu.make_async_copy(ref, ref, sem)


def place_pieces(ids, pieces, quad_first, targets):
    count = len(pieces) // 2
    for side in range(2):
        for block in range(count):
            ref = pieces[side * count + block]
            for slot in range(ref.shape[0]):
                d, e = (slot, block) if quad_first else (block, slot)
                shard = (ids[1] ^ e) * QUAD + (ids[0] ^ d)
                rows = ref.shape[1]
                here = pl.ds(pl.multiple_of(shard * rows, 16), rows)
                for at, lanes, w, sem in targets:
                    there = pl.ds(pl.multiple_of((ids[2] ^ side) * lanes, 128), lanes)
                    src = ref.at[slot, :, pl.ds(at, lanes)]
                    pltpu.make_async_copy(src, w.at[here, there], sem).start()


def place_halves(halves, w, sem):
    cols = halves.shape[2]
    for h in range(2):
        pltpu.make_async_copy(halves.at[h], w.at[:, pl.ds(h * cols, cols)], sem).start()


def place(ids, parts, w, sem):
    if len(parts) == 1:
        place_halves(parts[0], w, sem)
    else:
        place_pieces(ids, parts, False, [(0, parts[0].shape[2], w, sem)])


def norm_kernel(x_ref, g_ref, b_ref, act_ref):
    normed, _ = norm_parts(x_ref[...].astype(F32))
    act_ref[...] = (normed * g_ref[...] + b_ref[...]).astype(BF16)


def first_norm(x, gain, bias):
    n = x.shape[0]
    row = pl.BlockSpec((BLK, D), lambda i: (i, 0))
    vec = pl.BlockSpec((1, D), lambda i: (0, 0))
    return pl.pallas_call(
        norm_kernel,
        grid=(n // BLK,),
        in_specs=[row, vec, vec],
        out_specs=row,
        out_shape=jax.ShapeDtypeStruct((n, D), BF16),
        compiler_params=params(),
        cost_estimate=cost(8 * n * D, 4 * n * D),
        name="first_norm",
    )(x, gain, bias)


def qkv_kernel(parts, ids, act_ref, qb_ref, *rest):
    w_hbm, (qkv_ref, w_vmem, sem) = rest[:parts], rest[parts:]

    @pl.when(pl.program_id(0) == 0)
    def _():
        place(ids, w_hbm, w_vmem, sem)
        whole(w_vmem, sem).wait()

    qkv_ref[...] = (mm(act_ref[...], w_vmem[...]) + qb_ref[...]).astype(BF16)


def project_qkv(ids, act, qkv_bias, w):
    n = act.shape[0]
    tile = BLK
    return pl.pallas_call(
        functools.partial(qkv_kernel, len(w)),
        grid=(n // tile,),
        in_specs=[
            pl.BlockSpec(memory_space=pltpu.SMEM),
            pl.BlockSpec((tile, D), lambda i: (i, 0)),
            pl.BlockSpec((1, 3 * D), lambda i: (0, 0)),
        ]
        + [pl.BlockSpec(memory_space=pl.ANY)] * len(w),
        out_specs=pl.BlockSpec((tile, 3 * D), lambda i: (i, 0)),
        out_shape=jax.ShapeDtypeStruct((n, 3 * D), BF16),
        scratch_shapes=[pltpu.VMEM((D, 3 * D), BF16), pltpu.SemaphoreType.DMA],
        compiler_params=params(),
        cost_estimate=cost(2 * n * D * 3 * D, 2 * (n * 4 * D + 3 * D * D)),
        name="project_qkv",
    )(ids, act, qkv_bias, *w)


def first_of_doc(lens_ref, positions):
    start = jnp.zeros_like(positions)
    end = 0
    for d in range(DOCS):
        end = end + lens_ref[0, d]
        start = jnp.where(positions >= end, end, start)
    return start


def lane_half(h):
    lane = lax.broadcasted_iota(jnp.int32, (1, 128), 1)
    return (lane >= h * HD) & (lane < (h + 1) * HD)


WINDOW = 2


def mask(lens_ref, keys_at, keys, queries_at, queries):
    qpos = lax.broadcasted_iota(jnp.int32, (1, queries), 1) + queries_at
    kpos = lax.broadcasted_iota(jnp.int32, (keys, 1), 0) + keys_at
    return jnp.where((kpos >= first_of_doc(lens_ref, qpos)) & (kpos <= qpos), 0.0, MASKED)


def attn_kernel(lens_ref, q_ref, k_ref, v_ref, o_ref, l_ref, mask_ref):
    pair = pl.program_id(0)
    blocks = []
    for i in range(q_ref.shape[0] // BLK):
        low = max(0, i - WINDOW)
        blocks.append((low * BLK, (i + 1 - low) * BLK, i * BLK))

    @pl.when(pair == 0)
    def _():
        l_ref[...] = jnp.zeros_like(l_ref)
        for first, count, at in blocks:
            mask_ref[0:count, at : at + BLK] = mask(lens_ref, first, count, at, BLK)

    for first, count, at in blocks:
        rows = slice(at, at + BLK)
        q = q_ref[rows, :] * jnp.asarray(SCALE, BF16)
        k = k_ref[first : first + count, :]
        v = v_ref[first : first + count, :]
        out = None
        for h in range(2):
            half = lane_half(h)
            s = mm(k, jnp.where(half, q, jnp.zeros_like(q)), NT) + mask_ref[0:count, rows]
            m = jnp.max(s, axis=0, keepdims=True)
            p = jnp.exp(s - m)
            total = jnp.sum(p, axis=0, keepdims=True)
            probs = (p * (1.0 / total)).astype(BF16)
            o = mm(probs, jnp.where(half, v, jnp.zeros_like(v)), TN)
            out = o if out is None else out + o
            l_ref[pl.ds(2 * pair + h, 1), rows] = m + jnp.log(total)
        o_ref[rows, :] = out.astype(BF16)


def attention(lens, qkv):
    n = qkv.shape[0]
    pairs = H // 2
    spec = lambda w: pl.BlockSpec((n, 128), lambda p: (0, w * pairs + p))
    return pl.pallas_call(
        attn_kernel,
        grid=(pairs,),
        in_specs=[pl.BlockSpec(memory_space=pltpu.SMEM), spec(0), spec(1), spec(2)],
        out_specs=[
            pl.BlockSpec((n, 128), lambda p: (0, p)),
            pl.BlockSpec((16, n), lambda p: (0, 0)),
        ],
        out_shape=[jax.ShapeDtypeStruct((n, D), BF16), jax.ShapeDtypeStruct((16, n), F32)],
        scratch_shapes=[pltpu.VMEM(((WINDOW + 1) * BLK, n), F32)],
        compiler_params=params(),
        cost_estimate=cost(2 * 2 * H * n * n * HD * 0.6, 2 * n * 4 * D, H * n * n * 0.6),
        name="attention",
    )(lens, qkv, qkv, qkv)


def attn_back_kernel(
    lens_ref, q_ref, k_ref, v_ref, o_ref, do_ref, l_ref, out_hbm, mask_ref, dq_acc, bufs, sems
):
    pair = pl.program_id(0)
    pairs = pl.num_programs(0)
    n = q_ref.shape[0]
    slot = pair % 2
    blocks = [(at, min((WINDOW + 1) * BLK, n - at)) for at in range(0, n, BLK)]

    def copies(p, at):
        return [
            pltpu.make_async_copy(
                bufs.at[at, w],
                out_hbm.at[:, pl.ds(pl.multiple_of(w * D + p * 128, 128), 128)],
                sems.at[at, w],
            )
            for w in range(3)
        ]

    @pl.when(pair == 0)
    def _():
        for at, count in blocks:
            mask_ref[at : at + BLK, 0:count] = mask(lens_ref, at, BLK, at, count)

    @pl.when(pair >= 2)
    def _():
        for c in copies(pair - 2, slot):
            c.wait()

    prod = (o_ref[...].astype(F32) * do_ref[...].astype(F32)).T
    dq_acc[...] = jnp.zeros_like(dq_acc)
    for at, count in blocks:
        keys = slice(at, at + BLK)
        queries = slice(at, at + count)
        k = k_ref[keys, :]
        v = v_ref[keys, :]
        q = q_ref[queries, :] * jnp.asarray(SCALE, BF16)
        do = do_ref[queries, :]
        dk = dv = None
        for h in range(2):
            half = lane_half(h)
            inner = jnp.sum(prod[h * HD : (h + 1) * HD, queries], axis=0, keepdims=True)
            logs = l_ref[pl.ds(2 * pair + h, 1), queries]
            qh = jnp.where(half, q, jnp.zeros_like(q))
            doh = jnp.where(half, do, jnp.zeros_like(do))
            kh = jnp.where(half, k, jnp.zeros_like(k))
            p = jnp.exp(mm(k, qh, NT) + (mask_ref[keys, 0:count] - logs))
            ds = (p * (mm(v, doh, NT) - inner)).astype(BF16)
            dvh = mm(p.astype(BF16), doh)
            dkh = mm(ds, qh)
            dv, dk = (dvh, dkh) if h == 0 else (dv + dvh, dk + dkh)
            dq_acc[queries, :] += mm(ds, kh, TN)
        bufs[slot, 1, keys, :] = dk.astype(BF16)
        bufs[slot, 2, keys, :] = dv.astype(BF16)
    bufs[slot, 0] = (dq_acc[...] * SCALE).astype(BF16)
    for c in copies(pair, slot):
        c.start()

    @pl.when(pair == pairs - 1)
    def _():
        for c in copies(pair - 1, 1 - slot) + copies(pair, slot):
            c.wait()


def attention_back(lens, qkv, attended, dout, stats):
    n = qkv.shape[0]
    pairs = H // 2
    spec = lambda w: pl.BlockSpec((n, 128), lambda p: (0, w * pairs + p))
    one = pl.BlockSpec((n, 128), lambda p: (0, p))
    return pl.pallas_call(
        attn_back_kernel,
        grid=(pairs,),
        in_specs=[
            pl.BlockSpec(memory_space=pltpu.SMEM), spec(0), spec(1), spec(2), one, one,
            pl.BlockSpec((16, n), lambda p: (0, 0)),
        ],
        out_specs=pl.BlockSpec(memory_space=pl.ANY),
        out_shape=jax.ShapeDtypeStruct((n, 3 * D), BF16),
        scratch_shapes=[
            pltpu.VMEM((n, (WINDOW + 1) * BLK), F32),
            pltpu.VMEM((n, 128), F32),
            pltpu.VMEM((2, 3, n, 128), BF16),
            pltpu.SemaphoreType.DMA((2, 3)),
        ],
        compiler_params=params(),
        cost_estimate=cost(5 * 2 * H * n * n * HD * 0.6, 2 * n * 8 * D, H * n * n * 0.6),
        name="attention_back",
    )(lens, qkv, qkv, qkv, attended, dout, stats)


def start_mlp_weights(ids, w_hbm, wp, wu, wd, sem):
    if len(w_hbm) == 3:
        for i, w in enumerate((wp, wu, wd)):
            place_halves(w_hbm[i], w, sem.at[i])
        return
    packed = w_hbm[-1]
    _, count, _, lanes = packed.shape

    def body(t, carry):
        for w, i, at, rows in ((wp, 0, FF // count, D // count), (wd, 2, 0, FF // count)):
            here = pl.ds(pl.multiple_of(t * rows, 16), rows)
            for h in range(2):
                src = packed.at[h, t, pl.ds(at, rows), :]
                pltpu.make_async_copy(src, w.at[here, pl.ds(h * lanes, lanes)], sem.at[i]).start()
        return carry

    lax.fori_loop(0, count, body, 0)
    place_pieces(ids, w_hbm[:-1], False, [(0, FF // 2, wu, sem.at[1])])


def mlp_kernel(
    parts, ids, x_ref, att_ref, pb_ref, g_ref, b_ref, ub_ref, db_ref, *rest
):
    w_hbm = rest[:parts]
    mid_ref, out_ref, hid_ref, slope_ref, act_ref, wp, wu, wd, sem = rest[parts:]
    step = pl.program_id(0)

    @pl.when(step == 0)
    def _():
        start_mlp_weights(ids, w_hbm, wp, wu, wd, sem)
        whole(wp, sem.at[0]).wait()

    middle = x_ref[...].astype(F32) + BETA * (mm(att_ref[...], wp[...]) + pb_ref[...])
    mid_ref[...] = middle
    normed, _ = norm_parts(middle)
    act = (normed * g_ref[...] + b_ref[...]).astype(BF16)
    act_ref[...] = act

    @pl.when(step == 0)
    def _():
        whole(wu, sem.at[1]).wait()
        whole(wd, sem.at[2]).wait()

    chunk = 768
    branch = jnp.zeros(middle.shape, F32)
    for f in range(FF // chunk):
        cols = pl.ds(f * chunk, chunk)
        u = mm(act, wu[:, cols]) + ub_ref[:, cols]
        u2 = u * u
        gate = 0.5 + 0.5 * jnp.tanh(u * (TANH_ROOT + (TANH_ROOT * TANH_CUBIC) * u2))
        value = u * gate
        hidden = value.astype(BF16)
        hid_ref[:, cols] = hidden
        branch = branch + mm(hidden, wd[cols, :])
        slope = gate + value * (1.0 - gate) * (
            2.0 * TANH_ROOT + (6.0 * TANH_ROOT * TANH_CUBIC) * u2
        )
        slope_ref[:, cols] = slope.astype(BF16)
    out_ref[...] = (middle + BETA * (branch + db_ref[...])).astype(BF16)


MLP_SCRATCH = [
    pltpu.VMEM((D, D), BF16),
    pltpu.VMEM((D, FF), BF16),
    pltpu.VMEM((FF, D), BF16),
    pltpu.SemaphoreType.DMA((3,)),
]


def mlp(ids, x, att, pb, gain, bias, ub, db, w):
    n = x.shape[0]
    tile = BLK
    row = lambda w: pl.BlockSpec((tile, w), lambda i: (i, 0))
    vec = lambda w: pl.BlockSpec((1, w), lambda i: (0, 0))
    sds = jax.ShapeDtypeStruct
    return pl.pallas_call(
        functools.partial(mlp_kernel, len(w)),
        grid=(n // tile,),
        in_specs=[pl.BlockSpec(memory_space=pltpu.SMEM)]
        + [row(D), row(D), vec(D), vec(D), vec(D), vec(FF), vec(D)]
        + [pl.BlockSpec(memory_space=pl.ANY)] * len(w),
        out_specs=[row(D), row(D), row(FF), row(FF), row(D)],
        out_shape=[
            sds((n, D), F32), sds((n, D), BF16), sds((n, FF), BF16), sds((n, FF), BF16),
            sds((n, D), BF16),
        ],
        scratch_shapes=MLP_SCRATCH,
        compiler_params=params(),
        cost_estimate=cost(2 * n * (2 * D * FF + D * D), 2 * n * (7 * D + 2 * FF), n * FF),
        name="mlp",
    )(ids, x, att, pb, gain, bias, ub, db, *w)


def mlp_back_kernel(parts, ids, c_ref, mid_ref, slope_ref, g_ref, *rest):
    w_hbm = rest[:parts]
    du_ref, dm_ref, dy_ref, do_ref, vec_ref, uvec_ref, wp, wu, wd, sem = rest[parts:]
    step = pl.program_id(0)

    @pl.when(step == 0)
    def _():
        start_mlp_weights(ids, w_hbm, wp, wu, wd, sem)
        vec_ref[...] = jnp.zeros_like(vec_ref)
        uvec_ref[...] = jnp.zeros_like(uvec_ref)

    grad_out = c_ref[...].astype(F32)
    dz = (BETA * grad_out).astype(BF16)
    normed, inverse = norm_parts(mid_ref[...])

    @pl.when(step == 0)
    def _():
        whole(wd, sem.at[2]).wait()
        whole(wu, sem.at[1]).wait()
        whole(wp, sem.at[0]).wait()

    chunk = 768
    da = jnp.zeros(normed.shape, F32)
    for f in range(FF // chunk):
        cols = pl.ds(f * chunk, chunk)
        du = (mm(dz, wd[cols, :], NT) * slope_ref[:, cols].astype(F32)).astype(BF16)
        du_ref[:, cols] = du
        uvec_ref[0:1, cols] += jnp.sum(du.astype(F32), axis=0, keepdims=True)
        da = da + mm(du, wu[:, cols], NT)
    dm = grad_out + norm_back(da, normed, inverse, g_ref[...])
    dm_ref[...] = dm
    dy = (BETA * dm).astype(BF16)
    dy_ref[...] = dy
    do_ref[...] = mm(dy, wp[...], NT).astype(BF16)
    vec_ref[0:1, :] += jnp.sum(da * normed, axis=0, keepdims=True)
    vec_ref[1:2, :] += jnp.sum(da, axis=0, keepdims=True)
    vec_ref[2:3, :] += jnp.sum(dy.astype(F32), axis=0, keepdims=True)
    vec_ref[3:4, :] += jnp.sum(dz.astype(F32), axis=0, keepdims=True)


def mlp_back(ids, c, middle, slope, gain, w):
    n = c.shape[0]
    tile = BLK
    const = lambda i: (0, 0)
    row = lambda w: pl.BlockSpec((tile, w), lambda i: (i, 0))
    sds = jax.ShapeDtypeStruct
    return pl.pallas_call(
        functools.partial(mlp_back_kernel, len(w)),
        grid=(n // tile,),
        in_specs=[pl.BlockSpec(memory_space=pltpu.SMEM)]
        + [row(D), row(D), row(FF), pl.BlockSpec((1, D), const)]
        + [pl.BlockSpec(memory_space=pl.ANY)] * len(w),
        out_specs=[
            row(FF), row(D), row(D), row(D), pl.BlockSpec((8, D), const), pl.BlockSpec((8, FF), const),
        ],
        out_shape=[
            sds((n, FF), BF16), sds((n, D), F32), sds((n, D), BF16), sds((n, D), BF16),
            sds((8, D), F32), sds((8, FF), F32),
        ],
        scratch_shapes=MLP_SCRATCH,
        compiler_params=params(),
        cost_estimate=cost(2 * n * (2 * D * FF + D * D), 2 * n * (7 * D + 2 * FF), n * FF),
        name="mlp_back",
    )(ids, c, middle, slope, gain, *w)


def store_sides(row, r, mine, theirs):
    width = r.shape[1] // 2

    @pl.when(row == 0)
    def _():
        mine[...] = r[:, :width].astype(BF16)
        theirs[...] = r[:, width:].astype(BF16)

    @pl.when(row == 1)
    def _():
        theirs[...] = r[:, :width].astype(BF16)
        mine[...] = r[:, width:].astype(BF16)


def down_outer_kernel(ids, a_ref, c_ref, mine, theirs, dz):
    @pl.when(pl.program_id(0) == 0)
    def _():
        dz[...] = (BETA * c_ref[...].astype(F32)).astype(BF16)

    store_sides(ids[2], mm(a_ref[...], dz[...], TN), mine, theirs)


def down_outer(ids, hidden, c):
    n = hidden.shape[0]
    half = pl.BlockSpec((D, D // 2), lambda i, s: (i, 0))
    return pl.pallas_call(
        down_outer_kernel,
        grid_spec=pltpu.PrefetchScalarGridSpec(
            num_scalar_prefetch=1,
            grid=(FF // D,),
            in_specs=[
                pl.BlockSpec((n, D), lambda i, s: (0, i)),
                pl.BlockSpec((n, D), lambda i, s: (0, 0)),
            ],
            out_specs=[half, half],
            scratch_shapes=[pltpu.VMEM((n, D), BF16)],
        ),
        out_shape=[jax.ShapeDtypeStruct((FF, D // 2), BF16)] * 2,
        compiler_params=params(),
        cost_estimate=cost(2 * n * FF * D, 2 * (n * (FF + D) + FF * D)),
        name="down_outer",
    )(ids, hidden, c)


def up_outer_kernel(act_ref, du_ref, att_ref, dy_ref, o_ref):
    o_ref[0, :, : FF // 4] = mm(act_ref[...], du_ref[:, : FF // 4], TN).astype(BF16)
    o_ref[0, :, FF // 4 : FF // 2] = mm(act_ref[...], du_ref[:, FF // 4 :], TN).astype(BF16)
    o_ref[0, :, FF // 2 :] = mm(att_ref[...], dy_ref[...], TN).astype(BF16)


def up_outer(act, du, attended, dy):
    n = act.shape[0]
    width = (FF + D) // 2
    once = pl.BlockSpec((n, D), lambda i: (0, 0))
    half = lambda w: pl.BlockSpec((n, w), lambda i: (0, i))
    return pl.pallas_call(
        up_outer_kernel,
        grid=(2,),
        in_specs=[once, half(FF // 2), once, half(D // 2)],
        out_specs=pl.BlockSpec((1, D, width), lambda i: (i, 0, 0)),
        out_shape=jax.ShapeDtypeStruct((2, D, width), BF16),
        compiler_params=params(),
        cost_estimate=cost(2 * n * D * 2 * width, 2 * (n * (FF + 3 * D) + 2 * D * width)),
        name="up_outer",
    )(act, du, attended, dy)


def qkv_outer_kernel(ids, act_ref, dqkv_ref, mine, theirs):
    step = pl.program_id(0)
    r = mm(act_ref[...], dqkv_ref[...], TN).astype(BF16)

    @pl.when(step == 0)
    def _():
        theirs[...] = r

    @pl.when(step == 1)
    def _():
        mine[...] = r


def qkv_outer(ids, act, dqkv):
    n = act.shape[0]
    width = 3 * D // 2
    out = pl.BlockSpec((D, width), lambda i, s: (0, 0))
    return pl.pallas_call(
        qkv_outer_kernel,
        grid_spec=pltpu.PrefetchScalarGridSpec(
            num_scalar_prefetch=1,
            grid=(2,),
            in_specs=[
                pl.BlockSpec((n, D), lambda i, s: (0, 0)),
                pl.BlockSpec((n, width), lambda i, s: (0, (i + 1 - s[2]) % 2)),
            ],
            out_specs=[out, out],
        ),
        out_shape=[jax.ShapeDtypeStruct((D, width), BF16)] * 2,
        compiler_params=params(),
        cost_estimate=cost(2 * n * D * 2 * width, 2 * (n * (D + 2 * width) + 2 * D * width)),
        name="qkv_outer",
    )(ids, act, dqkv)


def merge_kernel(quad_first, rows, ids, mine, theirs, *outs):
    for block, o in enumerate(outs):
        for slot in range(o.shape[0]):
            e, d = (block, slot) if quad_first else (slot, block)
            shard = (ids[1] ^ e) * QUAD + (ids[0] ^ d)
            here = pl.ds(pl.multiple_of(shard * rows, 16), rows)
            o[slot] = (mine[here, :].astype(F32) + theirs[here, :].astype(F32)).astype(BF16)


def merge(ids, mine, theirs, quad_first, name):
    left, width = mine.shape
    rows = left // (4 * QUAD)
    spec = pl.BlockSpec(memory_space=pltpu.VMEM)
    return pl.pallas_call(
        functools.partial(merge_kernel, quad_first, rows),
        in_specs=[pl.BlockSpec(memory_space=pltpu.SMEM), spec, spec],
        out_shape=[jax.ShapeDtypeStruct((4, rows, width), BF16)] * 4,
        compiler_params=params(),
        cost_estimate=cost(2 * mine.size, 6 * mine.size),
        name=name,
    )(ids, mine, theirs)


def add_quad_kernel(ids, a, b, c, d, *outs):
    for e in range(a.shape[0]):
        total = (a[e].astype(F32) + b[e].astype(F32)) + (c[e].astype(F32) + d[e].astype(F32))
        if len(outs) == 1:
            outs[0][ids[1] ^ e] = total.astype(BF16)
        else:
            outs[e][...] = total.astype(BF16)


def add_quad(ids, parts, apart, name):
    block = parts[0].shape
    sds = jax.ShapeDtypeStruct
    spec = pl.BlockSpec(memory_space=pltpu.VMEM)
    return pl.pallas_call(
        add_quad_kernel,
        in_specs=[pl.BlockSpec(memory_space=pltpu.SMEM)] + [spec] * 4,
        out_shape=[sds(block[1:], BF16)] * block[0] if apart else sds(block, BF16),
        compiler_params=params(),
        cost_estimate=cost(4 * parts[0].size, 10 * parts[0].size),
        name=name,
    )(ids, *parts)


def split_kernel(a_ref, left, right):
    width = left.shape[1]
    left[...] = a_ref[:, :width].astype(F32)
    right[...] = a_ref[:, width:].astype(F32)


def split(a, width):
    rows, cols = a.shape
    sds = jax.ShapeDtypeStruct
    return pl.pallas_call(
        split_kernel,
        out_shape=[sds((rows, width), F32), sds((rows, cols - width), F32)],
        compiler_params=params(),
        cost_estimate=cost(a.size, 6 * a.size),
        name="split",
    )(a)


def input_grad_kernel(parts, ids, x_ref, dm_ref, g_ref, dqkv_ref, *rest):
    w_hbm, outs, (vec_ref, w, sem) = rest[:parts], rest[parts:-3], rest[-3:]
    step = pl.program_id(0)

    @pl.when(step == 0)
    def _():
        place(ids, w_hbm, w, sem)
        vec_ref[...] = jnp.zeros_like(vec_ref)
        whole(w, sem).wait()

    dqkv = dqkv_ref[...]
    da = mm(dqkv, w[...], NT)
    normed, inverse = norm_parts(x_ref[...].astype(F32))
    dx = (dm_ref[...] + norm_back(da, normed, inverse, g_ref[...])).astype(BF16)
    for d, o in enumerate(outs):

        @pl.when(step == d)
        def _(o=o):
            o[...] = dx

    vec_ref[0:1, 0:D] += jnp.sum(da * normed, axis=0, keepdims=True)
    vec_ref[1:2, 0:D] += jnp.sum(da, axis=0, keepdims=True)
    vec_ref[2:3, :] += jnp.sum(dqkv.astype(F32), axis=0, keepdims=True)


def input_grad(ids, x, dm, gain, dqkv, w):
    n = x.shape[0]
    tile = n // QUAD
    const = lambda i, s: (0, 0)
    row = lambda wide: pl.BlockSpec((tile, wide), lambda i, s: (i ^ s[0], 0))
    return pl.pallas_call(
        functools.partial(input_grad_kernel, len(w)),
        grid_spec=pltpu.PrefetchScalarGridSpec(
            num_scalar_prefetch=1,
            grid=(QUAD,),
            in_specs=[row(D), row(D), pl.BlockSpec((1, D), const), row(3 * D)]
            + [pl.BlockSpec(memory_space=pl.ANY)] * len(w),
            out_specs=[pl.BlockSpec((tile, D), const)] * QUAD + [pl.BlockSpec((8, 3 * D), const)],
            scratch_shapes=[pltpu.VMEM((D, 3 * D), BF16), pltpu.SemaphoreType.DMA],
        ),
        out_shape=[jax.ShapeDtypeStruct((tile, D), BF16)] * QUAD
        + [jax.ShapeDtypeStruct((8, 3 * D), F32)],
        compiler_params=params(),
        cost_estimate=cost(2 * n * D * 3 * D, 2 * (n * 7 * D + 3 * D * D)),
        name="input_grad",
    )(ids, x, dm, gain, dqkv, *w)


def join_kernel(ids, *refs):
    out = refs[-1]
    step = pl.program_id(0)
    for d in range(QUAD):

        @pl.when(step == d)
        def _(d=d):
            out[0] = refs[d][...]


def join(ids, pieces):
    tile, width = pieces[0].shape
    return pl.pallas_call(
        join_kernel,
        grid_spec=pltpu.PrefetchScalarGridSpec(
            num_scalar_prefetch=1,
            grid=(QUAD,),
            in_specs=[pl.BlockSpec((tile, width), lambda i, s: (0, 0))] * QUAD,
            out_specs=pl.BlockSpec((1, tile, width), lambda i, s: (i ^ s[0], 0, 0)),
        ),
        out_shape=jax.ShapeDtypeStruct((QUAD, tile, width), BF16),
        compiler_params=params(),
        cost_estimate=cost(1000, 4 * QUAD * tile * width),
        name="join",
    )(ids, *pieces)


def swap(block, axis, distance):
    count = lax.axis_size(axis)
    return lax.ppermute(block, axis, [(i, i ^ distance) for i in range(count)])


def quad_swap(pieces):
    count = lax.axis_size("tok")
    groups = [list(range(g, g + QUAD)) for g in range(0, count, QUAD)]
    return lax.all_to_all(pieces, "tok", 0, 0, axis_index_groups=groups, tiled=True)


def by_halves(whole):
    over_row, height, cols = whole.shape
    if over_row == 2:
        return whole
    return (
        whole.reshape(2, over_row // 2, height, cols)
        .transpose(0, 2, 1, 3)
        .reshape(2, height, over_row // 2 * cols)
    )


def gather(shard):
    rows, cols = shard.shape
    whole = lax.all_gather(shard, ("row", "tok"), axis=0, tiled=True)
    return by_halves(whole.reshape(lax.axis_size("row"), rows * lax.axis_size("tok"), cols))


def gather_line(shard):
    return jnp.stack([shard] + [swap(shard, "tok", QUAD * e) for e in range(1, 4)])


def spread(block, steps):
    return [block] + [swap(block, "tok", step) for step in steps]


def with_partner(blocks):
    return blocks + [swap(t, "row", 1) for t in blocks]


QUAD_STEPS = (1, 2, 3)
LINE_STEPS = (QUAD, 2 * QUAD, 3 * QUAD)


def after(value, *others):
    return lax.optimization_barrier((value,) + others)[0]


def from_peers(blocks, steps):
    return [blocks[0]] + [swap(t, "tok", step) for t, step in zip(blocks[1:], steps)]


def line_swap(pieces):
    count = lax.axis_size("tok")
    groups = [list(range(q, count, QUAD)) for q in range(QUAD)]
    return lax.all_to_all(pieces, "tok", 0, 0, axis_index_groups=groups, tiled=True)


def total_of(terms):
    return sum([t.astype(F32) for t in terms[1:]], terms[0].astype(F32))


def scatter(halves):
    return scatter_narrow(halves).astype(F32)


def scatter_narrow(halves):
    over_row = lax.axis_size("row")
    _, height, width = halves.shape
    cols = 2 * width // over_row
    if over_row != 2:
        halves = halves.reshape(2, height, over_row // 2, cols).transpose(0, 2, 1, 3)
    flat = halves.reshape(over_row * height, cols)
    return lax.psum_scatter(flat, ("row", "tok"), scatter_dimension=0, tiled=True)


def scatter_sides(sides, row_index):
    flat = jnp.stack(sides)
    return scatter(jnp.where(row_index % 2 == 0, flat, flat[::-1]))


def all_sum(block, steps):
    for step in steps:
        block = block + (swap(block, "tok", step) if step else swap(block, "row", 1))
    return block


def per_device(
    tokens,
    out_grad,
    doc_lengths,
    first_gain,
    first_bias,
    qkv_weight,
    query_bias,
    value_bias,
    proj_weight,
    proj_bias,
    second_gain,
    second_bias,
    up_weight,
    up_bias,
    down_weight,
    down_bias,
):
    row_count, piece_len, width = tokens.shape
    n = row_count * piece_len
    tok_index = lax.axis_index("tok")
    row_index = lax.axis_index("row")
    groups = lax.axis_size("tok") // QUAD
    by_permutes = lax.axis_size("row") == 2 and groups == 4
    ids = jnp.stack([tok_index % QUAD, tok_index // QUAD, row_index % 2]).astype(jnp.int32)
    lens = lax.dynamic_slice(
        doc_lengths,
        (tok_index % QUAD, tok_index // QUAD, 0),
        (1, 1, doc_lengths.shape[2]),
    )[0]

    qkv_bias = jnp.concatenate([query_bias, jnp.zeros_like(query_bias), value_bias])[None]
    vectors = [qkv_bias] + [
        t[None]
        for t in (first_gain, first_bias, proj_bias, second_gain, second_bias, up_bias, down_bias)
    ]
    if by_permutes:
        packed = jnp.concatenate([down_weight, proj_weight], axis=0)
        rest = lax.all_gather(packed, ("row", "tok"), axis=0, tiled=True)
        rest = rest.reshape((2, lax.axis_size("tok")) + packed.shape)
        x = quad_swap(tokens).reshape(n, width)
        qkv_line = gather_line(qkv_weight)
        up_shard = after(up_weight, qkv_line)
        qkv_line, x, ids, lens, *vectors = lax.optimization_barrier(
            (qkv_line, x, ids, lens, *vectors)
        )
        up_line = gather_line(up_shard)
        qkv_pieces = spread(qkv_line, QUAD_STEPS)
        up_pieces = spread(after(up_line, *qkv_pieces), QUAD_STEPS)
    else:
        x = quad_swap(tokens).reshape(n, width)
        qkv_full = [gather(qkv_weight)]
        others = [gather(proj_weight), gather(up_weight), gather(down_weight)]
    qkv_bias, first_gain, first_bias, proj_bias, second_gain, second_bias, up_bias, down_bias = vectors
    act1 = first_norm(x, first_gain, first_bias)
    if by_permutes:
        act1, qkv_pieces[-1] = lax.optimization_barrier((act1, qkv_pieces[-1]))
        qkv_full = with_partner(qkv_pieces)
    qkv = project_qkv(ids, act1, qkv_bias, qkv_full)
    attended, stats = attention(lens, qkv)
    if by_permutes:
        up_pieces[1:] = lax.optimization_barrier((attended, *up_pieces[1:]))[1:]
        others = with_partner(up_pieces) + [rest]
    held = others[:-1] if by_permutes else [attended]
    c = quad_swap(after(out_grad, *held)).reshape(n, width)
    middle, out, hidden, slope, act2 = mlp(
        ids, x, attended, proj_bias, second_gain, second_bias, up_bias, down_bias, others
    )
    output = quad_swap(after(out, c).reshape(row_count, piece_len, width))
    du, dm, dy, dout, vecs, uvec = mlp_back(ids, c, middle, slope, second_gain, others)
    up_outer_grad = up_outer(after(act2, output), du, attended, dy)
    down_sides = down_outer(ids, after(hidden, up_outer_grad), c)
    if by_permutes:
        down_blocks = merge(ids, down_sides[0], swap(down_sides[1], "row", 1), False, "down_merge")
        dout = after(dout, *down_blocks)
    dqkv = attention_back(lens, qkv, attended, dout, stats)
    if by_permutes:
        up_grad, proj_grad = split(scatter_narrow(up_outer_grad), FF // 2)
        down_got = from_peers(down_blocks, QUAD_STEPS)
        output = lax.reduce_precision(output, 8, 7)
        act1 = after(act1, output, *down_got[1:])
    qkv_sides = qkv_outer(ids, act1, dqkv)
    if by_permutes:
        down_got[0] = after(down_got[0], *qkv_sides)
        down_line = add_quad(ids, down_got, False, "down_add")
        qkv_mine = after(qkv_sides[0], down_line)
        down_line = line_swap(down_line)
        qkv_blocks = merge(ids, qkv_mine, swap(qkv_sides[1], "row", 1), False, "qkv_merge")
        dqkv = after(dqkv, *qkv_blocks)
        qkv_got = from_peers(qkv_blocks, QUAD_STEPS)
        qkv_shards = add_quad(ids, qkv_got, True, "qkv_add")
        qkv_grad = total_of(from_peers(qkv_shards, LINE_STEPS))
        down_grad = total_of([down_line[e] for e in range(groups)])
    else:
        down_grad = scatter_sides(down_sides, row_index)
        up_grad = scatter(up_outer_grad[:, :, : FF // 2])
        proj_grad = scatter(up_outer_grad[:, :, FF // 2 :])
        qkv_grad = scatter_sides(qkv_sides, row_index)
    *dx, vecs1 = input_grad(ids, x, dm, first_gain, dqkv, qkv_full)
    dx = from_peers(dx, QUAD_STEPS)
    if by_permutes:
        dx[0] = after(dx[0], down_line)
    tokens_grad = join(ids, dx)
    packed = jnp.concatenate(
        [
            vecs1[0, :D], vecs1[1, :D], vecs1[2, :D], vecs1[2, 2 * D :], vecs[2], vecs[0], vecs[1],
            vecs[3], uvec[0],
        ]
    ).reshape(-1, 128)
    if by_permutes:
        packed = all_sum(after(packed, *qkv_shards), (0,) + LINE_STEPS[:2])
        total = all_sum(after(packed, *dx), QUAD_STEPS[:2]).reshape(-1)
    else:
        total = lax.psum(packed, ("tok", "row")).reshape(-1)
    v = [total[i * D : (i + 1) * D] for i in range(8)]
    return (
        output, tokens_grad, qkv_grad, proj_grad, up_grad, down_grad,
        v[0], v[1], v[2], v[3], v[4], v[5], v[6], total[8 * D :], v[7],
    )


def solution(mesh):
    rows = P("row", "tok", None)
    weight = P("tok", "row")
    in_specs = (
        rows, rows, P("row", None, None), P(), P(), weight, P(), P(), weight, P(), P(), P(),
        weight, P(), weight, P(),
    )
    out_specs = (rows, rows, weight, weight, weight, weight) + (P(),) * 9
    return jax.shard_map(
        per_device, mesh=mesh, in_specs=in_specs, out_specs=out_specs, check_vma=False
    )
```
